512 devices in a mesh: wide: 128 (over y_hi, x, z), narrow: 4 (over y_lo, core).
Axes of the slice: x: 4, y: 4 (y_hi: 2, y_lo: 2; y = y_hi * 2 + y_lo), z: 16, core: 2. Of those that a mesh axis runs over, the one named last changes fastest.
Arguments:
- treated: bfloat16 [131072, 512], P(('wide', 'narrow')), may hold values from -6 to 6
- control: bfloat16 [131072, 512], P('wide'), may hold values from -6 to 6
- treated_weight: float32 [131072], P(('wide', 'narrow')), may hold values from 0.5 to 2
- control_weight: float32 [131072], replicated, may hold values from 0.5 to 2
- band: int32 [1024, 24], P(('wide', 'narrow')), may hold values from 0 to 1, as said below
Outputs:
- grad_treated: float32 [131072, 512], P(('wide', 'narrow'))
- grad_control: float32 [131072, 512], P(('wide', 'narrow'))
The draws below stay inside these ranges and needn't reach their ends.
Inputs may be any that keep to these rules, and one draw needn't show every extreme that they name: band[t, k] = 1 pairs treated block t with control block (t // 8 - 1) * 8 + k. For each t the ones form one run of k that contains k = 8 + t % 8; every k whose control block lies outside 0 to 1023 is 0.
All inputs are finite; a program needn't handle non-finite values.
Results may differ from the reference program's by a relative error of at most 0.0055.
Values may be sent and summed in bfloat16 or wider, within the bound.
No kernel may reach another device: no remote copies, remote signals or barrier semaphores. Data moves between devices by JAX's collectives and lax.ppermute only.
A program may use at most 64 MiB of HBM per device.

```python
import math
import jax
import jax.numpy as jnp
from jax import lax

REPRESENT_WIDTH = 512
BLOCK = 128
SWEEPS = 2
SB = 8
SLAB = 1024
NT = 131072
NC = 131072
NTB = 1024
N_WIDE = 128


def draw_band(key, part):
    key_low, key_high = jax.random.split(key)
    blocks = jnp.arange(NTB, dtype=jnp.int32)
    position = blocks % SB
    reach_low = jax.random.randint(key_low, (NTB,), 0, SB + 1, dtype=jnp.int32)
    reach_high = jax.random.randint(key_high, (NTB,), 0, SB + 1, dtype=jnp.int32)
    columns = jnp.arange(3 * SB, dtype=jnp.int32)
    offset = columns[None, :] - SB - position[:, None]
    target = blocks[:, None] + offset
    allowed = (offset >= -reach_low[:, None]) & (offset <= reach_high[:, None]) & (target >= 0) & (target < NTB)
    return allowed.astype(jnp.int32)


def steps_of(key, shape, cuts, low, high):
    loudness = 1.0
    for axis_at, shards_of in cuts:
        heights = jax.random.uniform(jax.random.fold_in(jax.random.fold_in(key, 6), axis_at), (shards_of,), jnp.float32, low / len(cuts), high / len(cuts))
        loudness = loudness * jnp.repeat(jnp.exp(heights), shape[axis_at] // shards_of).reshape((-1,) + (1,) * (len(shape) - 1 - axis_at))
    return loudness


def noise(own_key, shape, deviation, most, cuts=(), held_as=jnp.bfloat16):
    array = deviation * jax.random.normal(own_key, shape, jnp.float32)
    if cuts:
        array = array * steps_of(own_key, shape, cuts, -0.22, 0.18)
    return jnp.clip(array, -most, most).astype(held_as)


def setup_inputs(seed: int = 0) -> dict:
    key_of = jax.random.split(jax.random.key(seed), 6)
    treated = noise(key_of[0], (NT, REPRESENT_WIDTH), 1.0, 6.0, ((0, 512),))
    control = noise(key_of[1], (NC, REPRESENT_WIDTH), 1.0, 6.0, ((0, 128),))
    treated_weight = jnp.clip(jnp.exp(math.log(2.0) - 1.3862944 * jax.random.uniform(key_of[2], (NT,), jnp.float32) ** steps_of(key_of[2], (NT,), ((0, 512),), -0.2, 0.2)), 0.5, 2.0)
    control_weight = jnp.clip(jnp.exp(jax.random.uniform(key_of[3], (NC,), jnp.float32, math.log(0.5), math.log(2.0))), 0.5, 2.0)
    band = draw_band(jax.random.fold_in(key_of[5], 71), 0)
    return {"treated": treated, "control": control, "treated_weight": treated_weight, "control_weight": control_weight, "band": band}


SMOOTHING_TEMP = 0.05
EPSILON = 1e-06

def normalize(features):
    values = features.astype(jnp.float32)
    return (values * lax.rsqrt(lax.optimization_barrier(jnp.mean(values * values, axis=1, keepdims=True)) + EPSILON)).astype(jnp.bfloat16)

def expand(pair_blocks, block_rows):
    block_count, column_count = pair_blocks.shape
    full = jnp.broadcast_to(pair_blocks[:, None, :, None], (block_count, block_rows, column_count, block_rows))
    return full.reshape(block_count * block_rows, column_count * block_rows)

def reference(treated, control, treated_weight, control_weight, band):
    wide_count = N_WIDE
    treated_norm = normalize(treated).reshape(wide_count, SLAB, REPRESENT_WIDTH)
    control_norm = normalize(control)
    slabs = control_norm.reshape(wide_count, SLAB, REPRESENT_WIDTH)
    zero_slab = jnp.zeros((1, SLAB, REPRESENT_WIDTH), jnp.bfloat16)
    padded = jnp.concatenate([zero_slab, slabs, zero_slab], axis=0)
    blocks = band.reshape(wide_count, SB, 3 * SB)
    weights_treated = treated_weight.reshape(wide_count, SLAB)
    indices = jnp.arange(wide_count, dtype=jnp.int32)
    zero_row = jnp.zeros((1, SLAB), jnp.float32)

    def kernel_of(slab_index):
        band_span = lax.dynamic_slice_in_dim(padded, slab_index, 3, 0).reshape(3 * SLAB, REPRESENT_WIDTH)
        pairwise_inner = jnp.dot(treated_norm[slab_index], band_span.T, preferred_element_type=jnp.float32)
        paired_mask = expand(blocks[slab_index], BLOCK) > 0
        return (band_span, jnp.where(paired_mask, jnp.exp(pairwise_inner / (REPRESENT_WIDTH * SMOOTHING_TEMP)), 0.0))
    col_pad = jnp.concatenate([zero_row, jnp.ones((wide_count, SLAB), jnp.float32), zero_row], axis=0)
    row_scale = jnp.zeros((wide_count, SLAB), jnp.float32)
    for sweep_index in range(SWEEPS):

        def sweep_part(slab_index, col_pad=col_pad):
            band_span, kernel = kernel_of(slab_index)
            scales = lax.dynamic_slice_in_dim(col_pad, slab_index, 3, 0).reshape(3 * SLAB)
            row_values = weights_treated[slab_index] / lax.optimization_barrier(jnp.sum(kernel * scales[None, :], axis=1))
            return (row_values, lax.optimization_barrier(jnp.sum(kernel * row_values[:, None], axis=0)).reshape(3, SLAB))
        row_scale, column_parts = lax.map(sweep_part, indices)
        column_total = jnp.zeros((wide_count + 2, SLAB), jnp.float32)
        column_total = column_total.at[0:wide_count].add(column_parts[:, 0])
        column_total = column_total.at[1:wide_count + 1].add(column_parts[:, 1])
        column_total = column_total.at[2:wide_count + 2].add(column_parts[:, 2])
        col_scale = control_weight.reshape(wide_count, SLAB) / column_total[1:wide_count + 1]
        col_pad = jnp.concatenate([zero_row, col_scale, zero_row], axis=0)

    def finish(pull_total, slab_index):
        band_span, kernel = kernel_of(slab_index)
        scales = lax.dynamic_slice_in_dim(col_pad, slab_index, 3, 0).reshape(3 * SLAB)
        transport = row_scale[slab_index][:, None] * kernel * scales[None, :]
        plan_bf = transport.astype(jnp.bfloat16)
        pulled = jnp.dot(plan_bf, band_span, preferred_element_type=jnp.float32)
        own_rows = treated_norm[slab_index]
        treated_grad = lax.optimization_barrier(jnp.sum(transport, axis=1))[:, None] * own_rows.astype(jnp.float32) - pulled
        pushed = jnp.dot(plan_bf.T, own_rows, preferred_element_type=jnp.float32).reshape(3, SLAB, REPRESENT_WIDTH)
        current = lax.dynamic_slice_in_dim(pull_total, slab_index, 3, 0)
        pull_total = lax.dynamic_update_slice_in_dim(pull_total, current + pushed, slab_index, 0)
        return (pull_total, treated_grad)
    pull_total, treated_grad = lax.scan(finish, jnp.zeros((wide_count + 2, SLAB, REPRESENT_WIDTH), jnp.float32), indices)
    grad_treated = treated_grad.reshape(NT, REPRESENT_WIDTH)
    grad_control = control_weight[:, None] * control_norm.astype(jnp.float32) - pull_total[1:wide_count + 1].reshape(NC, REPRESENT_WIDTH)
    return (grad_treated, grad_control)
```

```python
import jax
import jax.numpy as jnp
from jax import lax
from jax.sharding import PartitionSpec as P

SWEEPS = 2
SMOOTHING_TEMP = 0.05
EPSILON = 1e-06

SWAP_Y = [(0, 2), (2, 0), (1, 3), (3, 1)]
SWAP_CORE = [(0, 1), (1, 0), (2, 3), (3, 2)]


def from_low(block, hops):
    count = lax.axis_size("wide")
    return lax.ppermute(block, "wide", [(i, i + hops) for i in range(count - hops)])


def from_high(block, hops):
    count = lax.axis_size("wide")
    return lax.ppermute(block, "wide", [(i + hops, i) for i in range(count - hops)])


def normalize(features):
    values = features.astype(jnp.float32)
    return (values * lax.rsqrt(jnp.mean(values * values, axis=1, keepdims=True) + EPSILON)).astype(
        jnp.bfloat16
    )


def expand(pair_blocks, block_rows):
    block_count, column_count = pair_blocks.shape
    full = jnp.broadcast_to(
        pair_blocks[:, None, :, None], (block_count, block_rows, column_count, block_rows)
    )
    return full.reshape(block_count * block_rows, column_count * block_rows)


def shards(treated, control, treated_weight, control_weight, band):
    quarter, features = treated.shape
    slab = control.shape[0]
    block_rows = quarter // band.shape[0]
    per_quarter = band.shape[0]
    wide_index = lax.axis_index("wide")
    n = lax.axis_index("narrow")
    wide_count = lax.axis_size("wide")
    order = [n, n ^ 2, n ^ 1, n ^ 3]
    scale_factor = 1.0 / (features * SMOOTHING_TEMP)

    def pick(array, axis):
        return [lax.dynamic_index_in_dim(array, o, axis, keepdims=True) for o in order]

    control_parts = pick(control.reshape(4, quarter, features), 0)
    near_raw = jnp.concatenate(control_parts[:2], 0).reshape(2 * quarter, features)
    far_raw = jnp.concatenate(control_parts[2:], 0).reshape(2 * quarter, features)
    low_near = from_low(near_raw, 1)
    high_near = from_high(near_raw, 1)

    pairs = jnp.pad(band.astype(jnp.float32).reshape(1, -1), ((0, 0), (0, quarter - band.size)))
    small = jnp.concatenate([treated_weight[None], pairs], 0)
    treated_y = lax.ppermute(treated, "narrow", SWAP_Y)
    small_y = lax.ppermute(small, "narrow", SWAP_Y)
    treated_pair = jnp.concatenate([treated, treated_y], 0)
    small_pair = jnp.stack([small, small_y], 0)
    treated_far = lax.ppermute(treated_pair, "narrow", SWAP_CORE)
    small_far = lax.ppermute(small_pair, "narrow", SWAP_CORE)
    small_all = jnp.concatenate([small_pair, small_far], 0)
    slab_weight = small_all[:, 0].reshape(slab)
    slab_band = small_all[:, 1, : band.size].reshape(4 * per_quarter, 3, 4, per_quarter)
    slab_band = jnp.concatenate(pick(slab_band, 2), 2)

    treated_slab = normalize(jnp.concatenate([treated_pair, treated_far], 0))
    own_norm = normalize(jnp.concatenate([near_raw, far_raw], 0))

    def kernel_of(rows, columns, pair_blocks):
        inner = lax.dot_general(
            rows, columns, (((1,), (1,)), ((), ())), preferred_element_type=jnp.float32
        )
        return jnp.where(
            expand(pair_blocks, block_rows) > 0, jnp.exp(inner * scale_factor), 0.0
        )

    half_blocks = 2 * per_quarter

    def side_blocks(first):
        chosen = slab_band[:, 0::2, first : first + 2]
        return chosen.reshape(4 * per_quarter, 2 * half_blocks)

    kernel_own = kernel_of(treated_slab, own_norm, slab_band[:, 1].reshape(4 * per_quarter, -1))

    near_sides = jnp.stack([low_near, high_near], 0)
    far_sides = lax.ppermute(near_sides, "narrow", SWAP_CORE)
    near_norm = normalize(near_sides.reshape(slab, features))
    kernel_near = kernel_of(treated_slab, near_norm, side_blocks(0))

    gated, _ = lax.optimization_barrier((treated_pair, near_sides))
    low_treated = from_low(gated, 1)
    high_treated = from_high(gated, 1)
    treated_sides = jnp.stack([low_treated, high_treated], 0)
    treated_sides_far = lax.ppermute(treated_sides, "narrow", SWAP_CORE)

    far_norm = normalize(far_sides.reshape(slab, features))
    kernel_far = kernel_of(treated_slab, far_norm, side_blocks(2))

    weight_slabs = [
        jnp.concatenate(
            pick(
                lax.dynamic_slice_in_dim(
                    control_weight, (wide_index + d) * slab, slab
                ).reshape(4, quarter),
                0,
            ),
            0,
        ).reshape(slab)
        for d in (-1, 0, 1)
    ]
    exists = [wide_index > 0, True, wide_index < wide_count - 1]

    half = slab // 2
    scales = [jnp.ones((slab,), jnp.float32)] * 3
    extra_up = jnp.pad(slab_band[:, 2, 0].reshape(-1), (0, slab - 4 * per_quarter * per_quarter))
    extra_down = jnp.pad(slab_band[:, 0, 0].reshape(-1), (0, slab - 4 * per_quarter * per_quarter))
    received = []
    for sweep_index in range(SWEEPS):
        low, own, high = scales
        near_scale = jnp.concatenate([low[:half], high[:half]])
        far_scale = jnp.concatenate([low[half:], high[half:]])
        row_total = (
            jnp.sum(kernel_own * own[None], axis=1)
            + jnp.sum(kernel_near * near_scale[None], axis=1)
            + jnp.sum(kernel_far * far_scale[None], axis=1)
        )
        row_scale = slab_weight / row_total
        column_own = jnp.sum(kernel_own * row_scale[:, None], axis=0)
        column_near = jnp.sum(kernel_near * row_scale[:, None], axis=0)
        column_far = jnp.sum(kernel_far * row_scale[:, None], axis=0)
        column_low = jnp.concatenate([column_near[:half], column_far[:half]])
        column_high = jnp.concatenate([column_near[half:], column_far[half:]])
        if sweep_index == SWEEPS - 1:
            extra_up = extra_down = row_scale
        from_below = from_low(jnp.stack([column_own, column_high, extra_up], 0), 1)
        from_above = from_high(jnp.stack([column_own, column_low, extra_down], 0), 1)
        from_below2 = from_low(column_high[None], 2)
        from_above2 = from_high(column_low[None], 2)
        totals = [
            column_low + from_below[0] + from_below2[0],
            column_own + from_below[1] + from_above[1],
            column_high + from_above[0] + from_above2[0],
        ]
        scales = [
            jnp.where(there, weight / total, 0.0)
            for there, weight, total in zip(exists, weight_slabs, totals)
        ]
        received.append((from_below[2], from_above[2]))

    low, own, high = scales
    near_scale = jnp.concatenate([low[:half], high[:half]])
    far_scale = jnp.concatenate([low[half:], high[half:]])

    own_row_scale = row_scale[:quarter, None]
    row_mass = jnp.zeros((quarter,), jnp.float32)
    pulled = jnp.zeros((quarter, features), jnp.float32)
    for kernel, scale, columns in (
        (kernel_own, own, own_norm),
        (kernel_near, near_scale, near_norm),
        (kernel_far, far_scale, far_norm),
    ):
        transport = own_row_scale * kernel[:quarter] * scale[None]
        row_mass = row_mass + jnp.sum(transport, axis=1)
        pulled = pulled + jnp.dot(
            transport.astype(jnp.bfloat16), columns, preferred_element_type=jnp.float32
        )
    grad_treated = row_mass[:, None] * treated_slab[:quarter].astype(jnp.float32) - pulled

    own_quarter = own_norm[:quarter]
    sides = jnp.concatenate([treated_sides, treated_sides_far], 1)
    sides_norm = normalize(sides.reshape(2 * slab, features))
    blocks_low, blocks_high = (
        r[: 4 * per_quarter * per_quarter].reshape(4 * per_quarter, per_quarter)
        for r in received[0]
    )
    kernel_mid = kernel_of(treated_slab, own_quarter, slab_band[:, 1, 0])
    kernel_sides = kernel_of(
        sides_norm, own_quarter, jnp.concatenate([blocks_low, blocks_high], 0)
    )
    sides_scale = jnp.concatenate(received[-1])
    own_column_scale = own[None, :quarter]
    pushed = jnp.zeros((quarter, features), jnp.float32)
    for kernel, scale, rows in (
        (kernel_mid, row_scale, treated_slab),
        (kernel_sides, sides_scale, sides_norm),
    ):
        transport = (scale[:, None] * kernel * own_column_scale).astype(jnp.bfloat16)
        pushed = pushed + lax.dot_general(
            transport, rows, (((0,), (0,)), ((), ())), preferred_element_type=jnp.float32
        )
    own_weight = weight_slabs[1][:quarter]
    grad_control = own_weight[:, None] * own_quarter.astype(jnp.float32) - pushed
    return (grad_treated, grad_control)


def solution(mesh):
    return jax.shard_map(
        shards,
        mesh=mesh,
        in_specs=(
            P(("wide", "narrow"), None),
            P("wide", None),
            P(("wide", "narrow")),
            P(),
            P(("wide", "narrow"), None),
        ),
        out_specs=(P(("wide", "narrow"), None), P(("wide", "narrow"), None)),
        check_vma=False,
    )
```

```python
import jax
import jax.numpy as jnp
from jax import lax
from jax.experimental import pallas as pl
from jax.experimental.pallas import tpu as pltpu
from jax.sharding import PartitionSpec as P


SMOOTHING_TEMP = 0.05
EPSILON = 1e-06

SWAP_Y = [(0, 2), (2, 0), (1, 3), (3, 1)]
SWAP_CORE = [(0, 1), (1, 0), (2, 3), (3, 2)]

LANES = 128
QUARTER = 256
HALF = 512
SLAB = 1024
WIDTH = 512
SCALE = 1.0 / (WIDTH * SMOOTHING_TEMP)

F32 = jnp.float32
BF16 = jnp.bfloat16

CORE, Y, ODD, A_EVEN, HAS_ODD, WIDE, WIDE_ODD, WIDE_EVEN = range(8)


def both_ways(pairs, count):
    kept = [(a, b) for a, b in pairs if b < count]
    return kept + [(b, a) for a, b in kept]


def narrow_swap(block, pairs):
    return lax.ppermute(block, "narrow", pairs)


def exchange(block, hops, crossing):
    count = lax.axis_size("wide")
    first = hops if crossing else 0
    pairs = [
        (base + i, base + i + hops) for base in range(first, count, 2 * hops) for i in range(hops)
    ]
    return lax.ppermute(block, "wide", both_ways(pairs, count))


def normalize(features):
    values = features.astype(F32)
    total = jnp.sum(values * values, axis=1, keepdims=True)
    return (values * lax.rsqrt(total * (1.0 / WIDTH) + EPSILON)).astype(BF16)


def nt_dot(a, b):
    return lax.dot_general(a, b, (((1,), (1,)), ((), ())), preferred_element_type=F32)


def identity():
    return lax.broadcasted_iota(jnp.int32, (LANES, LANES), 0) == lax.broadcasted_iota(
        jnp.int32, (LANES, LANES), 1
    )


def to_column(row):
    return jnp.sum(jnp.where(identity(), row, 0.0), axis=1, keepdims=True)


def to_row(column):
    return jnp.sum(jnp.where(identity(), column, 0.0), axis=0, keepdims=True)


def lane_tiles(values):
    total = values[:, :LANES]
    for i in range(1, values.shape[1] // LANES):
        total = total + values[:, i * LANES : (i + 1) * LANES]
    return total


def sublane_tiles(values):
    rows, columns = values.shape
    return jnp.sum(values.reshape(rows // 8, 8, columns), axis=0)


def block_kernel(rows_ref, columns, mask_ref, i, lanes):
    inner = nt_dot(rows_ref[pl.ds(pl.multiple_of(i * QUARTER, QUARTER), QUARTER), :], columns)
    values = jnp.exp(inner * SCALE)
    top = values[:LANES] * mask_ref[pl.ds(2 * i, 1), lanes]
    bottom = values[LANES:] * mask_ref[pl.ds(2 * i + 1, 1), lanes]
    return top, bottom


def fill_kernel(rows_ref, columns_ref, mask_ref, lanes, kernel_ref, sums_ref, before_ref):
    def step(i, carry):
        blocks = block_kernel(rows_ref, columns_ref[...], mask_ref, i, lanes)
        for j, block in enumerate(blocks):
            at = pl.ds(pl.multiple_of(i * QUARTER + j * LANES, LANES), LANES)
            kernel_ref[at, :] = block
            sums = lane_tiles(block)
            if before_ref is not None:
                sums = sums + before_ref[at, :]
            sums_ref[at, :] = sums
        return carry

    lax.fori_loop(0, 4, step, 0)


def prepare_kernel(
    flags, own_ref, y_ref, far_ref, small_ref, small_y_ref, small_far_ref, control_ref, weight_any,
    rows_ref, columns_ref, kernel_ref, sums_ref, mask_ref, weight_ref, pair_ref, column_weight_ref,
    band_ref, fetched_ref, sems,
):
    core, y, odd = flags[CORE], flags[Y], flags[ODD]
    copies = [
        pltpu.make_async_copy(
            weight_any.at[pl.ds(pl.multiple_of(flags[which] * 8, 8), 8), :],
            fetched_ref.at[i],
            sems.at[i],
        )
        for i, which in enumerate((WIDE, WIDE_ODD, WIDE_EVEN))
    ]
    for copy in copies:
        copy.start()
    rows_ref[0:QUARTER, :] = normalize(own_ref[...])
    rows_ref[QUARTER:HALF, :] = normalize(y_ref[...])
    rows_ref[HALF:SLAB, :] = normalize(far_ref[...])
    for i in range(4):
        quarter = (2 * i + core) if i < 2 else (2 * (i - 2) + 1 - core)
        at = pl.ds(pl.multiple_of(quarter * QUARTER, QUARTER), QUARTER)
        columns_ref[i * QUARTER : (i + 1) * QUARTER, :] = normalize(control_ref[at, :])

    band_ref[...] = jnp.zeros_like(band_ref)
    for i, source in enumerate(
        (small_ref[...], small_y_ref[...], small_far_ref[0], small_far_ref[1])
    ):
        band_ref[2 * i : 2 * i + 2, :] = source[2:4]
        for j in range(2):
            at = slice((2 * i + j) * LANES, (2 * i + j + 1) * LANES)
            weight_ref[at, :] = jnp.broadcast_to(to_column(source[j : j + 1]), (LANES, LANES))
    band = band_ref[...].astype(BF16)
    odd_base = odd * 16
    even_base = 16 - odd * 16
    lane = lax.broadcasted_iota(jnp.int32, (1, 3 * SLAB), 1)
    segment = lane // SLAB
    within = lane % SLAB
    block = (lane // LANES) % 2
    own_quarter = jnp.where(
        within < HALF, 2 * (within // QUARTER) + core, 2 * (within // QUARTER - 2) + 1 - core
    )
    side_quarter = 2 * ((within // QUARTER) % 2) + jnp.where(segment == 1, core, 1 - core)
    side_base = jnp.where(within < HALF, odd_base, even_base)
    wanted = jnp.where(segment == 0, 8 + 2 * own_quarter, side_base + 2 * side_quarter) + block
    one_hot = lax.broadcasted_iota(jnp.int32, (LANES, 3 * SLAB), 0) == wanted
    mask_ref[...] = jnp.dot(
        band[:16], jnp.where(one_hot, 1.0, 0.0).astype(BF16), preferred_element_type=F32
    )[:8]
    place = lax.broadcasted_iota(jnp.int32, (16, LANES), 0)
    base = jnp.where(place < 2, 8, jnp.where(place < 4, odd_base, even_base))
    chosen = base + 2 * (2 * y + core) + place % 2
    select = jnp.where(
        lax.broadcasted_iota(jnp.int32, (16, LANES), 1) == chosen, 1.0, 0.0
    ).astype(BF16)
    by_block = nt_dot(select, band).astype(BF16)
    spread = (
        lax.broadcasted_iota(jnp.int32, (LANES, SLAB), 0)
        == lax.broadcasted_iota(jnp.int32, (LANES, SLAB), 1) // LANES
    )
    pair_ref[...] = jnp.dot(
        by_block, jnp.where(spread, 1.0, 0.0).astype(BF16), preferred_element_type=F32
    )[:8]

    fill_kernel(rows_ref, columns_ref, mask_ref, slice(0, SLAB), kernel_ref, sums_ref, None)

    for copy in copies:
        copy.wait()
    column_weight_ref[...] = jnp.zeros_like(column_weight_ref)
    for i in range(3):
        for q in range(4):
            quarter = (2 * q + core) if q < 2 else (2 * (q - 2) + 1 - core)
            for j in range(2):
                at = slice((2 * q + j) * LANES, (2 * q + j + 1) * LANES)
                column_weight_ref[i : i + 1, at] = fetched_ref[i, pl.ds(2 * quarter + j, 1), :]


def near_kernel(
    odd_ref, even_ref, rows_ref, mask_ref, before_ref, columns_ref, kernel_ref, sums_ref
):
    columns_ref[0:HALF, :] = normalize(odd_ref[...])
    columns_ref[HALF:SLAB, :] = normalize(even_ref[...])
    fill_kernel(
        rows_ref, columns_ref, mask_ref, slice(SLAB, 2 * SLAB), kernel_ref, sums_ref, before_ref
    )


def finish_messages(
    flags, own, near, far, first, second, partial_ref, odd_ref, even_ref, a_ref, b_ref
):
    own = jnp.sum(own, axis=0, keepdims=True)
    near = jnp.sum(near, axis=0, keepdims=True)
    far = jnp.sum(far, axis=0, keepdims=True)
    partial_ref[...] = jnp.zeros_like(partial_ref)
    partial_ref[0:1, :] = own
    for i in range(2):
        at = slice(i * HALF, (i + 1) * HALF)
        partial_ref[i + 1 : i + 2, 0:HALF] = near[:, at]
        partial_ref[i + 1 : i + 2, HALF:SLAB] = far[:, at]
    odd = partial_ref[1:2, :]
    even = partial_ref[2:3, :]
    odd_ref[0:1, :] = own
    odd_ref[1:2, :] = odd
    odd_ref[2:4, :] = first
    even_ref[0:1, :] = own
    even_ref[1:2, :] = even
    even_ref[2:4, :] = second
    a_even = flags[A_EVEN] > 0
    a_ref[...] = jnp.where(a_even, even, odd)
    b_ref[...] = jnp.where(a_even, odd, even)


def far_kernel(
    flags, odd_far_ref, even_far_ref, rows_ref, mask_ref, own_kernel_ref, near_kernel_ref,
    before_ref, weight_ref, pair_ref, columns_ref, kernel_ref, partial_ref, odd_ref, even_ref, a_ref, b_ref,
):
    columns_ref[0:HALF, :] = normalize(odd_far_ref[...])
    columns_ref[HALF:SLAB, :] = normalize(even_far_ref[...])

    def step(i, carry):
        own, near, far = carry
        blocks = block_kernel(
            rows_ref, columns_ref[...], mask_ref, i, slice(2 * SLAB, 3 * SLAB)
        )
        for j, block in enumerate(blocks):
            at = pl.ds(pl.multiple_of(i * QUARTER + j * LANES, LANES), LANES)
            kernel_ref[at, :] = block
            sums = lane_tiles(block) + before_ref[at, :]
            scale = weight_ref[at, 0:1] / jnp.sum(sums, axis=1, keepdims=True)
            own = own + sublane_tiles(own_kernel_ref[at, :] * scale)
            near = near + sublane_tiles(near_kernel_ref[at, :] * scale)
            far = far + sublane_tiles(block * scale)
        return own, near, far

    zero = jnp.zeros((8, SLAB), F32)
    own, near, far = lax.fori_loop(0, 4, step, (zero, zero, zero))
    finish_messages(
        flags, own, near, far, pair_ref[2:4, :], pair_ref[4:6, :],
        partial_ref, odd_ref, even_ref, a_ref, b_ref,
    )


def column_scales(flags, partial_ref, odd_ref, even_ref, a_ref, b_ref, column_weight_ref):
    a_even = flags[A_EVEN] > 0
    two_odd = jnp.where(a_even, b_ref[...], a_ref[...])
    two_even = jnp.where(a_even, a_ref[...], b_ref[...])
    own = partial_ref[0:1, :] + odd_ref[1:2, :] + even_ref[1:2, :]
    odd = partial_ref[1:2, :] + odd_ref[0:1, :] + two_odd
    even = partial_ref[2:3, :] + even_ref[0:1, :] + two_even
    has_odd = flags[HAS_ODD] > 0
    own = column_weight_ref[0:1, :] / own
    odd = jnp.where(has_odd, column_weight_ref[1:2, :] / jnp.where(has_odd, odd, 1.0), 0.0)
    even = column_weight_ref[2:3, :] / even
    near = jnp.concatenate([odd[:, :HALF], even[:, :HALF]], axis=1)
    far = jnp.concatenate([odd[:, HALF:], even[:, HALF:]], axis=1)
    return own, near, far


def sweep_kernel(
    flags, partial_in, odd_in, even_in, a_in, b_in, column_weight_ref, own_kernel_ref,
    near_kernel_ref, far_kernel_ref, weight_ref, row_ref, lane_ref, partial_ref, odd_ref,
    even_ref, a_ref, b_ref, flat_ref,
):
    scales = column_scales(flags, partial_in, odd_in, even_in, a_in, b_in, column_weight_ref)
    kernels = (own_kernel_ref, near_kernel_ref, far_kernel_ref)

    def step(i, carry):
        at = pl.ds(pl.multiple_of(i * LANES, LANES), LANES)
        total = jnp.zeros((LANES, LANES), F32)
        for kernel_ref, scale in zip(kernels, scales, strict=True):
            total = total + lane_tiles(kernel_ref[at, :] * scale)
        row_scale = weight_ref[at, 0:1] / jnp.sum(total, axis=1, keepdims=True)
        row_ref[at, :] = jnp.broadcast_to(row_scale, (LANES, LANES))
        flat_ref[pl.ds(i, 1), :] = to_row(row_scale)
        return tuple(
            sums + sublane_tiles(kernel_ref[at, :] * row_scale)
            for kernel_ref, sums in zip(kernels, carry, strict=True)
        )

    zero = jnp.zeros((8, SLAB), F32)
    own, near, far = lax.fori_loop(0, 8, step, (zero, zero, zero))
    for i in range(8):
        lane_ref[0:1, i * LANES : (i + 1) * LANES] = flat_ref[i : i + 1, :]
    flat = jnp.broadcast_to(lane_ref[...], (2, SLAB))
    finish_messages(
        flags, own, near, far, flat, flat, partial_ref, odd_ref, even_ref, a_ref, b_ref
    )


def transposed_kernel(
    flags, columns_ref, rows_ref, odd_near_ref, even_near_ref, odd_far_ref, even_far_ref, pair_ref,
    odd_in, even_in, odd_rows_ref, even_rows_ref, kernel_ref,
):
    at = pl.ds(pl.multiple_of(flags[Y] * QUARTER, QUARTER), QUARTER)
    own = columns_ref[at, :]
    odd_rows_ref[0:HALF, :] = normalize(odd_near_ref[...])
    odd_rows_ref[HALF:SLAB, :] = normalize(odd_far_ref[...])
    even_rows_ref[0:HALF, :] = normalize(even_near_ref[...])
    even_rows_ref[HALF:SLAB, :] = normalize(even_far_ref[...])
    for i, (rows, top, bottom) in enumerate(
        (
            (rows_ref, pair_ref[0:1, :], pair_ref[1:2, :]),
            (odd_rows_ref, odd_in[2:3, :], odd_in[3:4, :]),
            (even_rows_ref, even_in[2:3, :], even_in[3:4, :]),
        )
    ):
        values = jnp.exp(nt_dot(own, rows[...]) * SCALE)
        lanes = slice(i * SLAB, (i + 1) * SLAB)
        kernel_ref[0:LANES, lanes] = values[:LANES] * top
        kernel_ref[LANES:QUARTER, lanes] = values[LANES:] * bottom


def gradient_kernel(
    flags, partial_in, odd_in, even_in, a_in, b_in, column_weight_ref, row_ref, lane_ref,
    own_kernel_ref, near_kernel_ref, far_kernel_ref, own_columns_ref, near_columns_ref,
    far_columns_ref, rows_ref, odd_rows_ref, even_rows_ref, transposed_ref, treated_out,
    control_out,
):
    scales = column_scales(flags, partial_in, odd_in, even_in, a_in, b_in, column_weight_ref)
    row_scale = row_ref[:, 0:1]
    mass = jnp.zeros((QUARTER, LANES), F32)
    pulled = jnp.zeros((QUARTER, WIDTH), F32)
    for kernel_ref, scale, columns_ref in zip(
        (own_kernel_ref, near_kernel_ref, far_kernel_ref),
        scales,
        (own_columns_ref, near_columns_ref, far_columns_ref),
        strict=True,
    ):
        transport = row_scale * kernel_ref[...] * scale
        mass = mass + lane_tiles(transport)
        pulled = pulled + jnp.dot(
            transport.astype(BF16), columns_ref[...], preferred_element_type=F32
        )
    mass = jnp.sum(mass, axis=1, keepdims=True)
    treated_out[...] = mass * rows_ref[0:QUARTER, :].astype(F32) - pulled

    second = flags[Y] > 0

    def own_quarter(row):
        return jnp.where(second, row[:, QUARTER:HALF], row[:, :QUARTER])

    def upright(row):
        return jnp.concatenate([to_column(row[:, :LANES]), to_column(row[:, LANES:])], axis=0)

    own_scale = upright(own_quarter(scales[0]))
    own_weight = upright(own_quarter(column_weight_ref[0:1, :]))
    pushed = jnp.zeros((QUARTER, WIDTH), F32)
    for i, (scale, rows) in enumerate(
        ((lane_ref[...], rows_ref), (odd_in[2:3, :], odd_rows_ref), (even_in[2:3, :], even_rows_ref))
    ):
        transport = scale * transposed_ref[:, i * SLAB : (i + 1) * SLAB] * own_scale
        pushed = pushed + jnp.dot(transport.astype(BF16), rows[...], preferred_element_type=F32)
    at = pl.ds(pl.multiple_of(flags[Y] * QUARTER, QUARTER), QUARTER)
    control_out[...] = own_weight * own_columns_ref[at, :].astype(F32) - pushed


VMEM = pl.BlockSpec(memory_space=pltpu.VMEM)
SMEM = pl.BlockSpec(memory_space=pltpu.SMEM)
ANY = pl.BlockSpec(memory_space=pltpu.HBM)


def call(body, specs, outs, operands, scratch=(), limit=30, out_specs=None):
    return pl.pallas_call(
        body,
        out_shape=tuple(jax.ShapeDtypeStruct(shape, dtype) for shape, dtype in outs),
        in_specs=specs,
        out_specs=out_specs or tuple(VMEM for _ in outs),
        scratch_shapes=list(scratch),
        compiler_params=pltpu.CompilerParams(vmem_limit_bytes=limit << 20),
    )(*operands)


MESSAGES = [((4, SLAB), F32), ((4, SLAB), F32), ((1, SLAB), F32), ((1, SLAB), F32)]


def trade(messages):
    odd, even, a, b = messages
    return (
        exchange(odd, 1, True),
        exchange(even, 1, False),
        exchange(a, 2, True),
        exchange(b, 2, False),
    )


def step(treated, control, treated_weight, control_weight, band):
    wide_index = lax.axis_index("wide")
    n = lax.axis_index("narrow")
    wide_count = lax.axis_size("wide")
    core, y, odd = n % 2, n // 2, wide_index % 2
    toward_odd = wide_index + 2 * odd - 1
    values = (
        core,
        y,
        odd,
        jnp.logical_xor(wide_index % 4 >= 2, odd == 1).astype(jnp.int32),
        ((toward_odd >= 0) & (toward_odd < wide_count)).astype(jnp.int32),
        wide_index,
        jnp.clip(toward_odd, 0, wide_count - 1),
        wide_index + 1 - 2 * odd,
    )
    place = lax.iota(jnp.int32, 8)
    flags = jnp.zeros((8,), jnp.int32)
    for i, value in enumerate(values):
        flags = jnp.where(place == i, value, flags)

    near = lax.dynamic_slice(
        control.reshape(2, 2, QUARTER, WIDTH), (0, core, 0, 0), (2, 1, QUARTER, WIDTH)
    ).reshape(HALF, WIDTH)
    odd_near = exchange(near, 1, True)
    even_near = exchange(near, 1, False)

    small = jnp.concatenate(
        [
            treated_weight.reshape(2, LANES),
            jnp.pad(band.astype(F32), ((0, 0), (0, LANES - band.shape[1]))),
        ],
        0,
    )
    treated_y = narrow_swap(treated, SWAP_Y)
    small_y = narrow_swap(small, SWAP_Y)
    treated_pair = jnp.concatenate([treated, treated_y], 0)
    treated_far = narrow_swap(treated_pair, SWAP_CORE)
    small_far = narrow_swap(jnp.stack([small, small_y], 0), SWAP_CORE)

    weights = control_weight.reshape(-1, LANES)
    rows, own_columns, own_kernel, sums, mask, weight, pairs, column_weight = call(
        prepare_kernel,
        [SMEM] + [VMEM] * 7 + [ANY],
        [
            ((SLAB, WIDTH), BF16),
            ((SLAB, WIDTH), BF16),
            ((SLAB, SLAB), F32),
            ((SLAB, LANES), F32),
            ((8, 3 * SLAB), F32),
            ((SLAB, LANES), F32),
            ((8, SLAB), F32),
            ((8, SLAB), F32),
        ],
        [flags, treated, treated_y, treated_far, small, small_y, small_far, control, weights],
        [
            pltpu.VMEM((LANES, LANES), F32),
            pltpu.VMEM((3, 8, LANES), F32),
            pltpu.SemaphoreType.DMA((3,)),
        ],
    )

    odd_near, even_near, _ = lax.optimization_barrier((odd_near, even_near, sums))
    odd_far = narrow_swap(odd_near, SWAP_CORE)
    even_far = narrow_swap(even_near, SWAP_CORE)
    near_columns, near_values, sums = call(
        near_kernel,
        [VMEM] * 5,
        [((SLAB, WIDTH), BF16), ((SLAB, SLAB), F32), ((SLAB, LANES), F32)],
        [odd_near, even_near, rows, mask, sums],
    )

    odd_treated = exchange(treated_pair, 1, True)
    even_treated = exchange(treated_pair, 1, False)

    far_columns, far_values, partial, *messages = call(
        far_kernel,
        [SMEM] + [VMEM] * 9,
        [((SLAB, WIDTH), BF16), ((SLAB, SLAB), F32), ((8, SLAB), F32), *MESSAGES],
        [flags, odd_far, even_far, rows, mask, own_kernel, near_values, sums, weight, pairs],
    )
    first = trade(messages)
    odd_treated_far = narrow_swap(odd_treated, SWAP_CORE)
    even_treated_far = narrow_swap(even_treated, SWAP_CORE)

    row_scale, lane_scale, partial, *messages = call(
        sweep_kernel,
        [SMEM] + [VMEM] * 10,
        [((SLAB, LANES), F32), ((1, SLAB), F32), ((8, SLAB), F32), *MESSAGES],
        [flags, partial, *first, column_weight, own_kernel, near_values, far_values, weight],
        [pltpu.VMEM((8, LANES), F32)],
    )
    second = trade(messages)

    odd_rows, even_rows, transposed = call(
        transposed_kernel,
        [SMEM] + [VMEM] * 9,
        [((SLAB, WIDTH), BF16), ((SLAB, WIDTH), BF16), ((QUARTER, 3 * SLAB), F32)],
        [
            flags, own_columns, rows, odd_treated, even_treated, odd_treated_far,
            even_treated_far, pairs, first[0], first[1],
        ],
    )

    top = pl.BlockSpec((QUARTER, SLAB), lambda i: (0, 0))
    whole = lambda *shape: pl.BlockSpec(shape, lambda i: (0,) * len(shape))
    return pl.pallas_call(
        gradient_kernel,
        grid=(1,),
        out_shape=(jax.ShapeDtypeStruct((QUARTER, WIDTH), F32),) * 2,
        in_specs=[
            SMEM, whole(8, SLAB), whole(4, SLAB), whole(4, SLAB), whole(1, SLAB), whole(1, SLAB),
            whole(8, SLAB), pl.BlockSpec((QUARTER, LANES), lambda i: (0, 0)), whole(1, SLAB),
            top, top, top,
            *[whole(SLAB, WIDTH)] * 6, whole(QUARTER, 3 * SLAB),
        ],
        out_specs=(whole(QUARTER, WIDTH),) * 2,
        compiler_params=pltpu.CompilerParams(vmem_limit_bytes=30 << 20),
        name="gradient_kernel",
    )(
        flags, partial, *second, column_weight, row_scale, lane_scale, own_kernel, near_values,
        far_values, own_columns, near_columns, far_columns, rows, odd_rows, even_rows, transposed,
    )


def solution(mesh):
    return jax.shard_map(
        step,
        mesh=mesh,
        in_specs=(
            P(("wide", "narrow"), None),
            P("wide", None),
            P(("wide", "narrow")),
            P(),
            P(("wide", "narrow"), None),
        ),
        out_specs=(P(("wide", "narrow"), None), P(("wide", "narrow"), None)),
        check_vma=False,
    )
```

```python
import jax
import jax.numpy as jnp
from jax import lax
from jax.experimental import pallas as pl
from jax.experimental.pallas import tpu as pltpu
from jax.sharding import PartitionSpec as P


SMOOTHING_TEMP = 0.05
EPSILON = 1e-06

SWAP_Y = [(0, 2), (2, 0), (1, 3), (3, 1)]
SWAP_CORE = [(0, 1), (1, 0), (2, 3), (3, 2)]

LANES = 128
QUARTER = 256
HALF = 512
SLAB = 1024
WIDTH = 512
SCALE = 1.0 / (WIDTH * SMOOTHING_TEMP)

F32 = jnp.float32
BF16 = jnp.bfloat16

INFO = 16
MESSAGE = QUARTER + INFO
JOINED = 2 * MESSAGE

NARROW, ODD, A_EVEN, HAS_ODD = range(4)


def both_ways(pairs, count):
    kept = [(a, b) for a, b in pairs if b < count]
    return kept + [(b, a) for a, b in kept]


def narrow_swap(block, pairs):
    return lax.ppermute(block, "narrow", pairs)


def exchange(block, hops, crossing):
    count = lax.axis_size("wide")
    first = hops if crossing else 0
    pairs = [
        (base + i, base + i + hops) for base in range(first, count, 2 * hops) for i in range(hops)
    ]
    return lax.ppermute(block, "wide", both_ways(pairs, count))


def normalize(features):
    values = features.astype(F32)
    total = jnp.sum(values * values, axis=1, keepdims=True)
    return (values * lax.rsqrt(total * (1.0 / WIDTH) + EPSILON)).astype(BF16)


def nt_dot(a, b):
    return lax.dot_general(a, b, (((1,), (1,)), ((), ())), preferred_element_type=F32)


def identity():
    return lax.broadcasted_iota(jnp.int32, (LANES, LANES), 0) == lax.broadcasted_iota(
        jnp.int32, (LANES, LANES), 1
    )


def to_column(row):
    return jnp.sum(jnp.where(identity(), row, 0.0), axis=1, keepdims=True)


def to_row(column):
    return jnp.sum(jnp.where(identity(), column, 0.0), axis=0, keepdims=True)


def lane_tiles(values):
    total = values[:, :LANES]
    for i in range(1, values.shape[1] // LANES):
        total = total + values[:, i * LANES : (i + 1) * LANES]
    return total


def sublane_tiles(values):
    rows, columns = values.shape
    return jnp.sum(values.reshape(rows // 8, 8, columns), axis=0)


def block_kernel(rows_ref, columns, mask_ref, i, lanes):
    inner = nt_dot(rows_ref[pl.ds(pl.multiple_of(i * QUARTER, QUARTER), QUARTER), :], columns)
    values = jnp.exp(inner * SCALE)
    top = values[:LANES] * mask_ref[pl.ds(2 * i, 1), lanes]
    bottom = values[LANES:] * mask_ref[pl.ds(2 * i + 1, 1), lanes]
    return top, bottom


def fill_kernel(rows_ref, columns_ref, mask_ref, lanes, kernel_ref, sums_ref, before_ref):
    def step(i, carry):
        blocks = block_kernel(rows_ref, columns_ref[...], mask_ref, i, lanes)
        for j, block in enumerate(blocks):
            at = pl.ds(pl.multiple_of(i * QUARTER + j * LANES, LANES), LANES)
            kernel_ref[at, :] = block
            sums = lane_tiles(block)
            if before_ref is not None:
                sums = sums + before_ref[at, :]
            sums_ref[at, :] = sums
        return carry

    lax.fori_loop(0, 4, step, 0)


def pack_kernel(treated_ref, weight_ref, band_ref, message_ref, info_ref):
    message_ref[0:QUARTER, :] = normalize(treated_ref[...])
    info_ref[...] = jnp.zeros_like(info_ref)
    weight = weight_ref[...]
    for i in range(3):
        part = weight.astype(BF16).astype(F32)
        info_ref[0:2, i * LANES : (i + 1) * LANES] = part
        weight = weight - part
    info_ref[0:2, 3 * LANES : 3 * LANES + 24] = band_ref[...].astype(F32)
    message_ref[QUARTER:MESSAGE, :] = info_ref[...].astype(BF16)


def join_kernel(own_ref, y_ref, joined_ref):
    joined_ref[0:QUARTER, :] = own_ref[0:QUARTER, :]
    joined_ref[QUARTER:HALF, :] = y_ref[0:QUARTER, :]
    joined_ref[HALF : HALF + INFO, :] = own_ref[QUARTER:MESSAGE, :]
    joined_ref[HALF + INFO : JOINED, :] = y_ref[QUARTER:MESSAGE, :]


def columns_kernel(control_ref, columns_ref):
    columns_ref[...] = normalize(control_ref[...])


def prepare_kernel(
    flags, joined_ref, far_ref, columns_ref, rows_ref, kernel_ref, sums_ref, mask_ref, weight_ref,
    pair_ref, band_ref,
):
    n, odd = flags[NARROW], flags[ODD]
    rows_ref[0:HALF, :] = joined_ref[0:HALF, :]
    rows_ref[HALF:SLAB, :] = far_ref[0:HALF, :]

    band_ref[...] = jnp.zeros_like(band_ref)
    for i, (source, first) in enumerate(
        ((joined_ref, HALF), (joined_ref, HALF + INFO), (far_ref, HALF), (far_ref, HALF + INFO))
    ):
        info = source[first : first + INFO, :].astype(F32)
        band_ref[2 * i : 2 * i + 2, :] = info[0:2, 3 * LANES :]
        weights = info[:, :LANES] + info[:, LANES : 2 * LANES] + info[:, 2 * LANES : 3 * LANES]
        for j in range(2):
            at = slice((2 * i + j) * LANES, (2 * i + j + 1) * LANES)
            weight_ref[at, :] = jnp.broadcast_to(to_column(weights[j : j + 1]), (LANES, LANES))
    band = band_ref[...].astype(BF16)
    odd_base = odd * 16
    even_base = 16 - odd * 16
    lane = lax.broadcasted_iota(jnp.int32, (1, 3 * SLAB), 1)
    segment = lane // SLAB
    wanted = (lane % SLAB) // LANES + jnp.where(
        segment == 0, 8, jnp.where(segment == 1, odd_base, even_base)
    )
    one_hot = lax.broadcasted_iota(jnp.int32, (LANES, 3 * SLAB), 0) == wanted
    mask_ref[...] = jnp.dot(
        band[:16], jnp.where(one_hot, 1.0, 0.0).astype(BF16), preferred_element_type=F32
    )[:8]
    place = lax.broadcasted_iota(jnp.int32, (16, LANES), 0)
    base = jnp.where(place < 2, 8, jnp.where(place < 4, odd_base, even_base))
    chosen = base + 2 * n + place % 2
    select = jnp.where(
        lax.broadcasted_iota(jnp.int32, (16, LANES), 1) == chosen, 1.0, 0.0
    ).astype(BF16)
    by_block = nt_dot(select, band).astype(BF16)
    spread = (
        lax.broadcasted_iota(jnp.int32, (LANES, SLAB), 0)
        == lax.broadcasted_iota(jnp.int32, (LANES, SLAB), 1) // LANES
    )
    pair_ref[...] = jnp.dot(
        by_block, jnp.where(spread, 1.0, 0.0).astype(BF16), preferred_element_type=F32
    )[:8]

    fill_kernel(rows_ref, columns_ref, mask_ref, slice(0, SLAB), kernel_ref, sums_ref, None)


def finish_messages(
    flags, sums, first, second, partial_ref, odd_ref, even_ref, a_ref, b_ref
):
    own, odd, even = (jnp.sum(part, axis=0, keepdims=True) for part in sums)
    partial_ref[...] = jnp.zeros_like(partial_ref)
    partial_ref[0:1, :] = own
    partial_ref[1:2, :] = odd
    partial_ref[2:3, :] = even
    odd_ref[0:1, :] = own
    odd_ref[1:2, :] = odd
    odd_ref[2:4, :] = first
    even_ref[0:1, :] = own
    even_ref[1:2, :] = even
    even_ref[2:4, :] = second
    a_even = flags[A_EVEN] > 0
    a_ref[...] = jnp.where(a_even, even, odd)
    b_ref[...] = jnp.where(a_even, odd, even)


def sides_kernel(
    flags, odd_raw, even_raw, rows_ref, mask_ref, own_kernel_ref, own_sums_ref, weight_ref,
    pair_ref, odd_columns_ref, even_columns_ref, odd_kernel_ref, even_kernel_ref, partial_ref,
    odd_ref, even_ref, a_ref, b_ref, sums_ref,
):
    odd_columns_ref[...] = normalize(odd_raw[...])
    even_columns_ref[...] = normalize(even_raw[...])
    fill_kernel(
        rows_ref, odd_columns_ref, mask_ref, slice(SLAB, 2 * SLAB), odd_kernel_ref, sums_ref,
        own_sums_ref,
    )

    def step(i, carry):
        own, odd, even = carry
        blocks = block_kernel(
            rows_ref, even_columns_ref[...], mask_ref, i, slice(2 * SLAB, 3 * SLAB)
        )
        for j, block in enumerate(blocks):
            at = pl.ds(pl.multiple_of(i * QUARTER + j * LANES, LANES), LANES)
            even_kernel_ref[at, :] = block
            sums = lane_tiles(block) + sums_ref[at, :]
            scale = weight_ref[at, 0:1] / jnp.sum(sums, axis=1, keepdims=True)
            own = own + sublane_tiles(own_kernel_ref[at, :] * scale)
            odd = odd + sublane_tiles(odd_kernel_ref[at, :] * scale)
            even = even + sublane_tiles(block * scale)
        return own, odd, even

    zero = jnp.zeros((8, SLAB), F32)
    sums = lax.fori_loop(0, 4, step, (zero, zero, zero))
    finish_messages(
        flags, sums, pair_ref[2:4, :], pair_ref[4:6, :], partial_ref, odd_ref, even_ref, a_ref,
        b_ref,
    )


def column_scales(flags, partial_ref, odd_ref, even_ref, a_ref, b_ref, weights):
    a_even = flags[A_EVEN] > 0
    two_odd = jnp.where(a_even, b_ref[...], a_ref[...])
    two_even = jnp.where(a_even, a_ref[...], b_ref[...])
    own = partial_ref[0:1, :] + odd_ref[1:2, :] + even_ref[1:2, :]
    odd = partial_ref[1:2, :] + odd_ref[0:1, :] + two_odd
    even = partial_ref[2:3, :] + even_ref[0:1, :] + two_even
    has_odd = flags[HAS_ODD] > 0
    own_weight, odd_weight, even_weight = (ref[...] for ref in weights)
    odd = jnp.where(has_odd, odd_weight / jnp.where(has_odd, odd, 1.0), 0.0)
    return own_weight / own, odd, even_weight / even


def sweep_kernel(
    flags, partial_in, odd_in, even_in, a_in, b_in, own_weight, odd_weight, even_weight,
    own_kernel_ref, odd_kernel_ref, even_kernel_ref, weight_ref, odd_joined, even_joined, row_ref,
    lane_ref, pair_ref, partial_ref, odd_ref, even_ref, a_ref, b_ref, flat_ref,
):
    pair_ref[0:HALF, :] = odd_joined[0:HALF, :]
    pair_ref[HALF:SLAB, :] = even_joined[0:HALF, :]
    scales = column_scales(
        flags, partial_in, odd_in, even_in, a_in, b_in, (own_weight, odd_weight, even_weight)
    )
    kernels = (own_kernel_ref, odd_kernel_ref, even_kernel_ref)

    def step(i, carry):
        at = pl.ds(pl.multiple_of(i * LANES, LANES), LANES)
        total = jnp.zeros((LANES, LANES), F32)
        for kernel_ref, scale in zip(kernels, scales, strict=True):
            total = total + lane_tiles(kernel_ref[at, :] * scale)
        row_scale = weight_ref[at, 0:1] / jnp.sum(total, axis=1, keepdims=True)
        row_ref[at, :] = jnp.broadcast_to(row_scale, (LANES, LANES))
        flat_ref[pl.ds(i, 1), :] = to_row(row_scale)
        return tuple(
            sums + sublane_tiles(kernel_ref[at, :] * row_scale)
            for kernel_ref, sums in zip(kernels, carry, strict=True)
        )

    zero = jnp.zeros((8, SLAB), F32)
    sums = lax.fori_loop(0, 8, step, (zero, zero, zero))
    for i in range(8):
        lane_ref[0:1, i * LANES : (i + 1) * LANES] = flat_ref[i : i + 1, :]
    flat = jnp.broadcast_to(lane_ref[...], (2, SLAB))
    finish_messages(flags, sums, flat, flat, partial_ref, odd_ref, even_ref, a_ref, b_ref)


def transposed_kernel(
    flags, columns_ref, rows_ref, near_ref, far_ref, pair_ref, odd_in, even_in, odd_rows_ref,
    even_rows_ref, kernel_ref,
):
    own = columns_ref[pl.ds(pl.multiple_of(flags[NARROW] * QUARTER, QUARTER), QUARTER), :]
    odd_rows_ref[0:HALF, :] = near_ref[0:HALF, :]
    odd_rows_ref[HALF:SLAB, :] = far_ref[0:HALF, :]
    even_rows_ref[0:HALF, :] = near_ref[HALF:SLAB, :]
    even_rows_ref[HALF:SLAB, :] = far_ref[HALF:SLAB, :]
    for i, (rows, top, bottom) in enumerate(
        (
            (rows_ref, pair_ref[0:1, :], pair_ref[1:2, :]),
            (odd_rows_ref, odd_in[2:3, :], odd_in[3:4, :]),
            (even_rows_ref, even_in[2:3, :], even_in[3:4, :]),
        )
    ):
        values = jnp.exp(nt_dot(own, rows[...]) * SCALE)
        lanes = slice(i * SLAB, (i + 1) * SLAB)
        kernel_ref[0:LANES, lanes] = values[:LANES] * top
        kernel_ref[LANES:QUARTER, lanes] = values[LANES:] * bottom


def gradient_kernel(
    flags, partial_in, odd_in, even_in, a_in, b_in, own_weight, odd_weight, even_weight, row_ref,
    lane_ref, own_kernel_ref, odd_kernel_ref, even_kernel_ref, own_columns_ref, odd_columns_ref,
    even_columns_ref, rows_ref, odd_rows_ref, even_rows_ref, transposed_ref, treated_out,
    control_out,
):
    scales = column_scales(
        flags, partial_in, odd_in, even_in, a_in, b_in, (own_weight, odd_weight, even_weight)
    )
    row_scale = row_ref[:, 0:1]
    mass = jnp.zeros((QUARTER, LANES), F32)
    pulled = jnp.zeros((QUARTER, WIDTH), F32)
    for kernel_ref, scale, columns_ref in zip(
        (own_kernel_ref, odd_kernel_ref, even_kernel_ref),
        scales,
        (own_columns_ref, odd_columns_ref, even_columns_ref),
        strict=True,
    ):
        transport = row_scale * kernel_ref[...] * scale
        mass = mass + lane_tiles(transport)
        pulled = pulled + jnp.dot(
            transport.astype(BF16), columns_ref[...], preferred_element_type=F32
        )
    mass = jnp.sum(mass, axis=1, keepdims=True)
    treated_out[...] = mass * rows_ref[0:QUARTER, :].astype(F32) - pulled

    n = flags[NARROW]

    def own_quarter(row):
        found = row[:, :QUARTER]
        for i in range(1, 4):
            found = jnp.where(n == i, row[:, i * QUARTER : (i + 1) * QUARTER], found)
        return found

    def upright(row):
        return jnp.concatenate([to_column(row[:, :LANES]), to_column(row[:, LANES:])], axis=0)

    own_scale = upright(own_quarter(scales[0]))
    own_mass = upright(own_quarter(own_weight[...]))
    pushed = jnp.zeros((QUARTER, WIDTH), F32)
    for i, (scale, rows) in enumerate(
        ((lane_ref[...], rows_ref), (odd_in[2:3, :], odd_rows_ref), (even_in[2:3, :], even_rows_ref))
    ):
        transport = scale * transposed_ref[:, i * SLAB : (i + 1) * SLAB] * own_scale
        pushed = pushed + jnp.dot(transport.astype(BF16), rows[...], preferred_element_type=F32)
    at = pl.ds(pl.multiple_of(n * QUARTER, QUARTER), QUARTER)
    control_out[...] = own_mass * own_columns_ref[at, :].astype(F32) - pushed


VMEM = pl.BlockSpec(memory_space=pltpu.VMEM)
SMEM = pl.BlockSpec(memory_space=pltpu.SMEM)


def call(body, specs, outs, operands, scratch=(), limit=16, out_specs=None):
    return pl.pallas_call(
        body,
        out_shape=tuple(jax.ShapeDtypeStruct(shape, dtype) for shape, dtype in outs),
        in_specs=specs,
        out_specs=out_specs or tuple(VMEM for _ in outs),
        scratch_shapes=list(scratch),
        compiler_params=pltpu.CompilerParams(vmem_limit_bytes=limit << 20),
    )(*operands)


MESSAGES = [((4, SLAB), F32), ((4, SLAB), F32), ((1, SLAB), F32), ((1, SLAB), F32)]


def trade(messages):
    odd, even, a, b = messages
    return (
        exchange(odd, 1, True),
        exchange(even, 1, False),
        exchange(a, 2, True),
        exchange(b, 2, False),
    )


def step(treated, control, treated_weight, control_weight, band):
    wide_index = lax.axis_index("wide")
    n = lax.axis_index("narrow")
    wide_count = lax.axis_size("wide")
    odd = wide_index % 2
    toward_odd = wide_index + 2 * odd - 1
    toward_even = wide_index + 1 - 2 * odd
    values = (
        n,
        odd,
        jnp.logical_xor(wide_index % 4 >= 2, odd == 1).astype(jnp.int32),
        ((toward_odd >= 0) & (toward_odd < wide_count)).astype(jnp.int32),
    )
    place = lax.iota(jnp.int32, 8)
    flags = jnp.zeros((8,), jnp.int32)
    for i, value in enumerate(values):
        flags = jnp.where(place == i, value, flags)
    weights = [
        lax.dynamic_slice_in_dim(control_weight, jnp.maximum(at, 0) * SLAB, SLAB).reshape(1, SLAB)
        for at in (wide_index, toward_odd, toward_even)
    ]

    odd_control = exchange(control, 1, True)
    even_control = exchange(control, 1, False)
    (own_columns,) = call(columns_kernel, [VMEM], [((SLAB, WIDTH), BF16)], [control])

    (message,) = call(
        pack_kernel,
        [VMEM] * 3,
        [((MESSAGE, WIDTH), BF16)],
        [treated, treated_weight.reshape(2, LANES), band],
        [pltpu.VMEM((INFO, WIDTH), F32)],
    )
    message_y = narrow_swap(message, SWAP_Y)
    (joined,) = call(join_kernel, [VMEM] * 2, [((JOINED, WIDTH), BF16)], [message, message_y])
    joined_far = narrow_swap(joined, SWAP_CORE)
    odd_joined = exchange(joined, 1, True)
    even_joined = exchange(joined, 1, False)

    rows, own_kernel, sums, mask, weight, pairs = call(
        prepare_kernel,
        [SMEM] + [VMEM] * 3,
        [
            ((SLAB, WIDTH), BF16),
            ((SLAB, SLAB), F32),
            ((SLAB, LANES), F32),
            ((8, 3 * SLAB), F32),
            ((SLAB, LANES), F32),
            ((8, SLAB), F32),
        ],
        [flags, joined, joined_far, own_columns],
        [pltpu.VMEM((LANES, LANES), F32)],
    )
    odd_columns, even_columns, odd_kernel, even_kernel, partial, *messages = call(
        sides_kernel,
        [SMEM] + [VMEM] * 8,
        [
            ((SLAB, WIDTH), BF16),
            ((SLAB, WIDTH), BF16),
            ((SLAB, SLAB), F32),
            ((SLAB, SLAB), F32),
            ((8, SLAB), F32),
            *MESSAGES,
        ],
        [flags, odd_control, even_control, rows, mask, own_kernel, sums, weight, pairs],
        [pltpu.VMEM((SLAB, LANES), F32)],
    )
    first = trade(messages)

    row_scale, lane_scale, near_rows, partial, *messages = call(
        sweep_kernel,
        [SMEM] + [VMEM] * 14,
        [((SLAB, LANES), F32), ((1, SLAB), F32), ((SLAB, WIDTH), BF16), ((8, SLAB), F32), *MESSAGES],
        [
            flags, partial, *first, *weights, own_kernel, odd_kernel, even_kernel, weight,
            odd_joined, even_joined,
        ],
        [pltpu.VMEM((8, LANES), F32)],
    )
    second = trade(messages)
    far_rows = narrow_swap(near_rows, SWAP_CORE)

    odd_rows, even_rows, transposed = call(
        transposed_kernel,
        [SMEM] + [VMEM] * 7,
        [((SLAB, WIDTH), BF16), ((SLAB, WIDTH), BF16), ((QUARTER, 3 * SLAB), F32)],
        [flags, own_columns, rows, near_rows, far_rows, pairs, first[0], first[1]],
    )

    top = pl.BlockSpec((QUARTER, SLAB), lambda i: (0, 0))
    whole = lambda *shape: pl.BlockSpec(shape, lambda i: (0,) * len(shape))
    return pl.pallas_call(
        gradient_kernel,
        grid=(1,),
        out_shape=(jax.ShapeDtypeStruct((QUARTER, WIDTH), F32),) * 2,
        in_specs=[
            SMEM, whole(8, SLAB), whole(4, SLAB), whole(4, SLAB), whole(1, SLAB), whole(1, SLAB),
            whole(1, SLAB), whole(1, SLAB), whole(1, SLAB),
            pl.BlockSpec((QUARTER, LANES), lambda i: (0, 0)), whole(1, SLAB), top, top, top,
            *[whole(SLAB, WIDTH)] * 6, whole(QUARTER, 3 * SLAB),
        ],
        out_specs=(whole(QUARTER, WIDTH),) * 2,
        compiler_params=pltpu.CompilerParams(vmem_limit_bytes=16 << 20),
        name="gradient_kernel",
    )(
        flags, partial, *second, *weights, row_scale, lane_scale, own_kernel, odd_kernel,
        even_kernel, own_columns, odd_columns, even_columns, rows, odd_rows, even_rows, transposed,
    )


def solution(mesh):
    return jax.shard_map(
        step,
        mesh=mesh,
        in_specs=(
            P(("wide", "narrow"), None),
            P("wide", None),
            P(("wide", "narrow")),
            P(),
            P(("wide", "narrow"), None),
        ),
        out_specs=(P(("wide", "narrow"), None), P(("wide", "narrow"), None)),
        check_vma=False,
    )
```

```python
import jax
import jax.numpy as jnp
from jax import lax
from jax.experimental import pallas as pl
from jax.experimental.pallas import tpu as pltpu
from jax.sharding import PartitionSpec as P


SMOOTHING_TEMP = 0.05
EPSILON = 1e-06

SWAP_Y = [(0, 2), (2, 0), (1, 3), (3, 1)]
SWAP_CORE = [(0, 1), (1, 0), (2, 3), (3, 2)]

LANES = 128
QUARTER = 256
HALF = 512
SLAB = 1024
WIDTH = 512
SCALE = 1.0 / (WIDTH * SMOOTHING_TEMP)

F32 = jnp.float32
BF16 = jnp.bfloat16

INFO = 16
MESSAGE = QUARTER + INFO
JOINED = 2 * MESSAGE

NARROW, CORE, ODD, A_EVEN, HAS_ODD = range(5)


def both_ways(pairs, count):
    kept = [(a, b) for a, b in pairs if b < count]
    return kept + [(b, a) for a, b in kept]


def narrow_swap(block, pairs):
    return lax.ppermute(block, "narrow", pairs)


def exchange(block, hops, crossing):
    count = lax.axis_size("wide")
    first = hops if crossing else 0
    pairs = [
        (base + i, base + i + hops) for base in range(first, count, 2 * hops) for i in range(hops)
    ]
    return lax.ppermute(block, "wide", both_ways(pairs, count))


def normalize(features):
    values = features.astype(F32)
    total = jnp.sum(values * values, axis=1, keepdims=True)
    return (values * lax.rsqrt(total * (1.0 / WIDTH) + EPSILON)).astype(BF16)


def nt_dot(a, b):
    return lax.dot_general(a, b, (((1,), (1,)), ((), ())), preferred_element_type=F32)


def identity():
    return lax.broadcasted_iota(jnp.int32, (LANES, LANES), 0) == lax.broadcasted_iota(
        jnp.int32, (LANES, LANES), 1
    )


def to_column(row):
    return jnp.sum(jnp.where(identity(), row, 0.0), axis=1, keepdims=True)


def to_row(column):
    return jnp.sum(jnp.where(identity(), column, 0.0), axis=0, keepdims=True)


def lane_tiles(values):
    total = values[:, :LANES]
    for i in range(1, values.shape[1] // LANES):
        total = total + values[:, i * LANES : (i + 1) * LANES]
    return total


def sublane_tiles(values):
    rows, columns = values.shape
    return jnp.sum(values.reshape(rows // 8, 8, columns), axis=0)


def block_kernel(rows_ref, columns, mask_ref, i, lanes):
    inner = nt_dot(rows_ref[pl.ds(pl.multiple_of(i * QUARTER, QUARTER), QUARTER), :], columns)
    values = jnp.exp(inner * SCALE)
    top = values[:LANES] * mask_ref[pl.ds(2 * i, 1), lanes]
    bottom = values[LANES:] * mask_ref[pl.ds(2 * i + 1, 1), lanes]
    return top, bottom


def fill_kernel(rows_ref, columns_ref, mask_ref, lanes, kernel_ref, sums_ref, before_ref):
    def step(i, carry):
        blocks = block_kernel(rows_ref, columns_ref[...], mask_ref, i, lanes)
        for j, block in enumerate(blocks):
            at = pl.ds(pl.multiple_of(i * QUARTER + j * LANES, LANES), LANES)
            kernel_ref[at, :] = block
            sums = lane_tiles(block)
            if before_ref is not None:
                sums = sums + before_ref[at, :]
            sums_ref[at, :] = sums
        return carry

    lax.fori_loop(0, 4, step, 0)


def pack_kernel(treated_ref, weight_ref, band_ref, message_ref, info_ref):
    message_ref[0:QUARTER, :] = normalize(treated_ref[...])
    info_ref[...] = jnp.zeros_like(info_ref)
    weight = weight_ref[...]
    for i in range(3):
        part = weight.astype(BF16).astype(F32)
        info_ref[0:2, i * LANES : (i + 1) * LANES] = part
        weight = weight - part
    info_ref[0:2, 3 * LANES : 3 * LANES + 24] = band_ref[...].astype(F32)
    message_ref[QUARTER:MESSAGE, :] = info_ref[...].astype(BF16)


def join_kernel(own_ref, y_ref, joined_ref):
    joined_ref[0:QUARTER, :] = own_ref[0:QUARTER, :]
    joined_ref[QUARTER:HALF, :] = y_ref[0:QUARTER, :]
    joined_ref[HALF : HALF + INFO, :] = own_ref[QUARTER:MESSAGE, :]
    joined_ref[HALF + INFO : JOINED, :] = y_ref[QUARTER:MESSAGE, :]


def columns_kernel(control_ref, columns_ref):
    columns_ref[...] = normalize(control_ref[...])


def near_columns_kernel(odd_ref, even_ref, columns_ref):
    columns_ref[0:HALF, :] = normalize(odd_ref[...])
    columns_ref[HALF:SLAB, :] = normalize(even_ref[...])


def near_kernel(rows_ref, columns_ref, mask_ref, before_ref, kernel_ref, sums_ref):
    fill_kernel(
        rows_ref, columns_ref, mask_ref, slice(SLAB, 2 * SLAB), kernel_ref, sums_ref, before_ref
    )


def prepare_kernel(
    flags, joined_ref, far_ref, columns_ref, rows_ref, kernel_ref, sums_ref, mask_ref, weight_ref,
    pair_ref, band_ref,
):
    n, odd = flags[NARROW], flags[ODD]
    rows_ref[0:HALF, :] = joined_ref[0:HALF, :]
    rows_ref[HALF:SLAB, :] = far_ref[0:HALF, :]

    band_ref[...] = jnp.zeros_like(band_ref)
    for i, (source, first) in enumerate(
        ((joined_ref, HALF), (joined_ref, HALF + INFO), (far_ref, HALF), (far_ref, HALF + INFO))
    ):
        info = source[first : first + INFO, :].astype(F32)
        band_ref[2 * i : 2 * i + 2, :] = info[0:2, 3 * LANES :]
        weights = info[:, :LANES] + info[:, LANES : 2 * LANES] + info[:, 2 * LANES : 3 * LANES]
        for j in range(2):
            at = slice((2 * i + j) * LANES, (2 * i + j + 1) * LANES)
            weight_ref[at, :] = jnp.broadcast_to(to_column(weights[j : j + 1]), (LANES, LANES))
    band = band_ref[...].astype(BF16)
    odd_base = odd * 16
    even_base = 16 - odd * 16
    lane = lax.broadcasted_iota(jnp.int32, (1, 3 * SLAB), 1)
    segment = lane // SLAB
    core = flags[CORE]
    side = jnp.where(lane % SLAB < HALF, odd_base, even_base)
    side = side + 4 * jnp.where(segment == 1, core, 1 - core) + (lane % HALF) // LANES
    wanted = jnp.where(segment == 0, 8 + lane // LANES, side)
    one_hot = lax.broadcasted_iota(jnp.int32, (LANES, 3 * SLAB), 0) == wanted
    mask_ref[...] = jnp.dot(
        band[:16], jnp.where(one_hot, 1.0, 0.0).astype(BF16), preferred_element_type=F32
    )[:8]
    place = lax.broadcasted_iota(jnp.int32, (16, LANES), 0)
    base = jnp.where(place < 2, 8, jnp.where(place < 4, odd_base, even_base))
    chosen = base + 2 * n + place % 2
    select = jnp.where(
        lax.broadcasted_iota(jnp.int32, (16, LANES), 1) == chosen, 1.0, 0.0
    ).astype(BF16)
    by_block = nt_dot(select, band).astype(BF16)
    spread = (
        lax.broadcasted_iota(jnp.int32, (LANES, SLAB), 0)
        == lax.broadcasted_iota(jnp.int32, (LANES, SLAB), 1) // LANES
    )
    pair_ref[...] = jnp.dot(
        by_block, jnp.where(spread, 1.0, 0.0).astype(BF16), preferred_element_type=F32
    )[:8]

    fill_kernel(rows_ref, columns_ref, mask_ref, slice(0, SLAB), kernel_ref, sums_ref, None)


def regroup(flags, first, second):
    low = jnp.concatenate([first[:, :HALF], second[:, :HALF]], axis=1)
    high = jnp.concatenate([first[:, HALF:], second[:, HALF:]], axis=1)
    swap = flags[CORE] > 0
    return jnp.where(swap, high, low), jnp.where(swap, low, high)


def finish_messages(flags, sums, first, second, partial_ref, odd_ref, even_ref, a_ref, b_ref):
    own, near, far = (jnp.sum(part, axis=0, keepdims=True) for part in sums)
    swap = flags[CORE] > 0
    low = jnp.where(swap, far, near)
    high = jnp.where(swap, near, far)
    odd = jnp.concatenate([low[:, :HALF], high[:, :HALF]], axis=1)
    even = jnp.concatenate([low[:, HALF:], high[:, HALF:]], axis=1)
    partial_ref[...] = jnp.zeros_like(partial_ref)
    partial_ref[0:1, :] = own
    partial_ref[1:2, :] = odd
    partial_ref[2:3, :] = even
    odd_ref[0:1, :] = own
    odd_ref[1:2, :] = odd
    odd_ref[2:4, :] = first
    even_ref[0:1, :] = own
    even_ref[1:2, :] = even
    even_ref[2:4, :] = second
    a_even = flags[A_EVEN] > 0
    a_ref[...] = jnp.where(a_even, even, odd)
    b_ref[...] = jnp.where(a_even, odd, even)


def far_kernel(
    flags, rows_ref, columns_ref, mask_ref, own_kernel_ref, near_kernel_ref, before_ref,
    weight_ref, pair_ref, kernel_ref, partial_ref, odd_ref, even_ref, a_ref, b_ref,
):
    def step(i, carry):
        own, near, far = carry
        blocks = block_kernel(
            rows_ref, columns_ref[...], mask_ref, i, slice(2 * SLAB, 3 * SLAB)
        )
        for j, block in enumerate(blocks):
            at = pl.ds(pl.multiple_of(i * QUARTER + j * LANES, LANES), LANES)
            kernel_ref[at, :] = block
            sums = lane_tiles(block) + before_ref[at, :]
            scale = weight_ref[at, 0:1] / jnp.sum(sums, axis=1, keepdims=True)
            own = own + sublane_tiles(own_kernel_ref[at, :] * scale)
            near = near + sublane_tiles(near_kernel_ref[at, :] * scale)
            far = far + sublane_tiles(block * scale)
        return own, near, far

    zero = jnp.zeros((8, SLAB), F32)
    sums = lax.fori_loop(0, 4, step, (zero, zero, zero))
    finish_messages(
        flags, sums, pair_ref[2:4, :], pair_ref[4:6, :], partial_ref, odd_ref, even_ref, a_ref,
        b_ref,
    )


def column_scales(flags, partial_ref, odd_ref, even_ref, a_ref, b_ref, weights):
    a_even = flags[A_EVEN] > 0
    two_odd = jnp.where(a_even, b_ref[...], a_ref[...])
    two_even = jnp.where(a_even, a_ref[...], b_ref[...])
    own = partial_ref[0:1, :] + odd_ref[1:2, :] + even_ref[1:2, :]
    odd = partial_ref[1:2, :] + odd_ref[0:1, :] + two_odd
    even = partial_ref[2:3, :] + even_ref[0:1, :] + two_even
    has_odd = flags[HAS_ODD] > 0
    own_weight, odd_weight, even_weight = (ref[...] for ref in weights)
    odd = jnp.where(has_odd, odd_weight / jnp.where(has_odd, odd, 1.0), 0.0)
    even = even_weight / even
    return own_weight / own, *regroup(flags, odd, even)


def sweep_kernel(
    flags, partial_in, odd_in, even_in, a_in, b_in, own_weight, odd_weight, even_weight,
    own_kernel_ref, near_kernel_ref, far_kernel_ref, weight_ref, odd_joined, even_joined, row_ref,
    lane_ref, pair_ref, partial_ref, odd_ref, even_ref, a_ref, b_ref, flat_ref,
):
    pair_ref[0:HALF, :] = odd_joined[0:HALF, :]
    pair_ref[HALF:SLAB, :] = even_joined[0:HALF, :]
    scales = column_scales(
        flags, partial_in, odd_in, even_in, a_in, b_in, (own_weight, odd_weight, even_weight)
    )
    kernels = (own_kernel_ref, near_kernel_ref, far_kernel_ref)

    def step(i, carry):
        at = pl.ds(pl.multiple_of(i * LANES, LANES), LANES)
        total = jnp.zeros((LANES, LANES), F32)
        for kernel_ref, scale in zip(kernels, scales, strict=True):
            total = total + lane_tiles(kernel_ref[at, :] * scale)
        row_scale = weight_ref[at, 0:1] / jnp.sum(total, axis=1, keepdims=True)
        row_ref[at, :] = jnp.broadcast_to(row_scale, (LANES, LANES))
        flat_ref[pl.ds(i, 1), :] = to_row(row_scale)
        return tuple(
            sums + sublane_tiles(kernel_ref[at, :] * row_scale)
            for kernel_ref, sums in zip(kernels, carry, strict=True)
        )

    zero = jnp.zeros((8, SLAB), F32)
    sums = lax.fori_loop(0, 8, step, (zero, zero, zero))
    for i in range(8):
        lane_ref[0:1, i * LANES : (i + 1) * LANES] = flat_ref[i : i + 1, :]
    flat = jnp.broadcast_to(lane_ref[...], (2, SLAB))
    finish_messages(flags, sums, flat, flat, partial_ref, odd_ref, even_ref, a_ref, b_ref)


def transposed_kernel(
    flags, columns_ref, rows_ref, near_ref, far_ref, pair_ref, odd_in, even_in, odd_rows_ref,
    even_rows_ref, kernel_ref,
):
    own = columns_ref[pl.ds(pl.multiple_of(flags[NARROW] * QUARTER, QUARTER), QUARTER), :]
    odd_rows_ref[0:HALF, :] = near_ref[0:HALF, :]
    odd_rows_ref[HALF:SLAB, :] = far_ref[0:HALF, :]
    even_rows_ref[0:HALF, :] = near_ref[HALF:SLAB, :]
    even_rows_ref[HALF:SLAB, :] = far_ref[HALF:SLAB, :]
    for i, (rows, top, bottom) in enumerate(
        (
            (rows_ref, pair_ref[0:1, :], pair_ref[1:2, :]),
            (odd_rows_ref, odd_in[2:3, :], odd_in[3:4, :]),
            (even_rows_ref, even_in[2:3, :], even_in[3:4, :]),
        )
    ):
        values = jnp.exp(nt_dot(own, rows[...]) * SCALE)
        lanes = slice(i * SLAB, (i + 1) * SLAB)
        kernel_ref[0:LANES, lanes] = values[:LANES] * top
        kernel_ref[LANES:QUARTER, lanes] = values[LANES:] * bottom


def gradient_kernel(
    flags, partial_in, odd_in, even_in, a_in, b_in, own_weight, odd_weight, even_weight, row_ref,
    lane_ref, own_kernel_ref, near_kernel_ref, far_kernel_ref, own_columns_ref, near_columns_ref,
    far_columns_ref, rows_ref, odd_rows_ref, even_rows_ref, transposed_ref, treated_out,
    control_out,
):
    scales = column_scales(
        flags, partial_in, odd_in, even_in, a_in, b_in, (own_weight, odd_weight, even_weight)
    )
    row_scale = row_ref[:, 0:1]
    mass = jnp.zeros((QUARTER, LANES), F32)
    pulled = jnp.zeros((QUARTER, WIDTH), F32)
    for kernel_ref, scale, columns_ref in zip(
        (own_kernel_ref, near_kernel_ref, far_kernel_ref),
        scales,
        (own_columns_ref, near_columns_ref, far_columns_ref),
        strict=True,
    ):
        transport = row_scale * kernel_ref[...] * scale
        mass = mass + lane_tiles(transport)
        pulled = pulled + jnp.dot(
            transport.astype(BF16), columns_ref[...], preferred_element_type=F32
        )
    mass = jnp.sum(mass, axis=1, keepdims=True)
    treated_out[...] = mass * rows_ref[0:QUARTER, :].astype(F32) - pulled

    n = flags[NARROW]

    def own_quarter(row):
        found = row[:, :QUARTER]
        for i in range(1, 4):
            found = jnp.where(n == i, row[:, i * QUARTER : (i + 1) * QUARTER], found)
        return found

    def upright(row):
        return jnp.concatenate([to_column(row[:, :LANES]), to_column(row[:, LANES:])], axis=0)

    own_scale = upright(own_quarter(scales[0]))
    own_mass = upright(own_quarter(own_weight[...]))
    pushed = jnp.zeros((QUARTER, WIDTH), F32)
    for i, (scale, rows) in enumerate(
        ((lane_ref[...], rows_ref), (odd_in[2:3, :], odd_rows_ref), (even_in[2:3, :], even_rows_ref))
    ):
        transport = scale * transposed_ref[:, i * SLAB : (i + 1) * SLAB] * own_scale
        pushed = pushed + jnp.dot(transport.astype(BF16), rows[...], preferred_element_type=F32)
    at = pl.ds(pl.multiple_of(n * QUARTER, QUARTER), QUARTER)
    control_out[...] = own_mass * own_columns_ref[at, :].astype(F32) - pushed


VMEM = pl.BlockSpec(memory_space=pltpu.VMEM)
SMEM = pl.BlockSpec(memory_space=pltpu.SMEM)


def call(body, specs, outs, operands, scratch=(), limit=16, out_specs=None):
    return pl.pallas_call(
        body,
        out_shape=tuple(jax.ShapeDtypeStruct(shape, dtype) for shape, dtype in outs),
        in_specs=specs,
        out_specs=out_specs or tuple(VMEM for _ in outs),
        scratch_shapes=list(scratch),
        compiler_params=pltpu.CompilerParams(vmem_limit_bytes=limit << 20),
    )(*operands)


MESSAGES = [((4, SLAB), F32), ((4, SLAB), F32), ((1, SLAB), F32), ((1, SLAB), F32)]


def trade(messages):
    odd, even, a, b = messages
    return (
        exchange(odd, 1, True),
        exchange(even, 1, False),
        exchange(a, 2, True),
        exchange(b, 2, False),
    )


def step(treated, control, treated_weight, control_weight, band):
    wide_index = lax.axis_index("wide")
    n = lax.axis_index("narrow")
    wide_count = lax.axis_size("wide")
    odd = wide_index % 2
    toward_odd = wide_index + 2 * odd - 1
    toward_even = wide_index + 1 - 2 * odd
    values = (
        n,
        n % 2,
        odd,
        jnp.logical_xor(wide_index % 4 >= 2, odd == 1).astype(jnp.int32),
        ((toward_odd >= 0) & (toward_odd < wide_count)).astype(jnp.int32),
    )
    place = lax.iota(jnp.int32, 8)
    flags = jnp.zeros((8,), jnp.int32)
    for i, value in enumerate(values):
        flags = jnp.where(place == i, value, flags)
    weights = [
        lax.dynamic_slice_in_dim(control_weight, jnp.maximum(at, 0) * SLAB, SLAB).reshape(1, SLAB)
        for at in (wide_index, toward_odd, toward_even)
    ]

    half = lax.dynamic_slice_in_dim(control, (n % 2) * HALF, HALF)
    odd_control = exchange(half, 1, True)
    even_control = exchange(half, 1, False)
    (own_columns,) = call(columns_kernel, [VMEM], [((SLAB, WIDTH), BF16)], [control])

    treated_weight, flags, *weights = lax.optimization_barrier((treated_weight, flags, *weights))
    (message,) = call(
        pack_kernel,
        [VMEM] * 3,
        [((MESSAGE, WIDTH), BF16)],
        [treated, treated_weight.reshape(2, LANES), band],
        [pltpu.VMEM((INFO, WIDTH), F32)],
    )
    message_y = narrow_swap(message, SWAP_Y)
    (joined,) = call(join_kernel, [VMEM] * 2, [((JOINED, WIDTH), BF16)], [message, message_y])
    joined_far = narrow_swap(joined, SWAP_CORE)
    odd_joined = exchange(joined, 1, True)
    even_joined = exchange(joined, 1, False)

    rows, own_kernel, sums, mask, weight, pairs = call(
        prepare_kernel,
        [SMEM] + [VMEM] * 3,
        [
            ((SLAB, WIDTH), BF16),
            ((SLAB, SLAB), F32),
            ((SLAB, LANES), F32),
            ((8, 3 * SLAB), F32),
            ((SLAB, LANES), F32),
            ((8, SLAB), F32),
        ],
        [flags, joined, joined_far, own_columns],
        [pltpu.VMEM((LANES, LANES), F32)],
    )
    odd_control, even_control, _ = lax.optimization_barrier((odd_control, even_control, sums))
    (near_columns,) = call(
        near_columns_kernel, [VMEM] * 2, [((SLAB, WIDTH), BF16)], [odd_control, even_control]
    )
    far_columns = narrow_swap(near_columns, SWAP_CORE)
    near_values, sums = call(
        near_kernel,
        [VMEM] * 4,
        [((SLAB, SLAB), F32), ((SLAB, LANES), F32)],
        [rows, near_columns, mask, sums],
    )
    far_values, partial, *messages = call(
        far_kernel,
        [SMEM] + [VMEM] * 8,
        [((SLAB, SLAB), F32), ((8, SLAB), F32), *MESSAGES],
        [flags, rows, far_columns, mask, own_kernel, near_values, sums, weight, pairs],
    )
    first = trade(messages)

    row_scale, lane_scale, near_rows, partial, *messages = call(
        sweep_kernel,
        [SMEM] + [VMEM] * 14,
        [((SLAB, LANES), F32), ((1, SLAB), F32), ((SLAB, WIDTH), BF16), ((8, SLAB), F32), *MESSAGES],
        [
            flags, partial, *first, *weights, own_kernel, near_values, far_values, weight,
            odd_joined, even_joined,
        ],
        [pltpu.VMEM((8, LANES), F32)],
    )
    second = trade(messages)
    far_rows = narrow_swap(near_rows, SWAP_CORE)

    odd_rows, even_rows, transposed = call(
        transposed_kernel,
        [SMEM] + [VMEM] * 7,
        [((SLAB, WIDTH), BF16), ((SLAB, WIDTH), BF16), ((QUARTER, 3 * SLAB), F32)],
        [flags, own_columns, rows, near_rows, far_rows, pairs, first[0], first[1]],
    )

    top = pl.BlockSpec((QUARTER, SLAB), lambda i: (0, 0))
    whole = lambda *shape: pl.BlockSpec(shape, lambda i: (0,) * len(shape))
    return pl.pallas_call(
        gradient_kernel,
        grid=(1,),
        out_shape=(jax.ShapeDtypeStruct((QUARTER, WIDTH), F32),) * 2,
        in_specs=[
            SMEM, whole(8, SLAB), whole(4, SLAB), whole(4, SLAB), whole(1, SLAB), whole(1, SLAB),
            whole(1, SLAB), whole(1, SLAB), whole(1, SLAB),
            pl.BlockSpec((QUARTER, LANES), lambda i: (0, 0)), whole(1, SLAB), top, top, top,
            *[whole(SLAB, WIDTH)] * 6, whole(QUARTER, 3 * SLAB),
        ],
        out_specs=(whole(QUARTER, WIDTH),) * 2,
        compiler_params=pltpu.CompilerParams(vmem_limit_bytes=16 << 20),
        name="gradient_kernel",
    )(
        flags, partial, *second, *weights, row_scale, lane_scale, own_kernel, near_values,
        far_values, own_columns, near_columns, far_columns, rows, odd_rows, even_rows, transposed,
    )


def solution(mesh):
    return jax.shard_map(
        step,
        mesh=mesh,
        in_specs=(
            P(("wide", "narrow"), None),
            P("wide", None),
            P(("wide", "narrow")),
            P(),
            P(("wide", "narrow"), None),
        ),
        out_specs=(P(("wide", "narrow"), None), P(("wide", "narrow"), None)),
        check_vma=False,
    )
```

```python
import jax
import jax.numpy as jnp
from jax import lax
from jax.experimental import pallas as pl
from jax.experimental.pallas import tpu as pltpu
from jax.sharding import PartitionSpec as P


SMOOTHING_TEMP = 0.05
EPSILON = 1e-06

SWAP_Y = [(0, 2), (2, 0), (1, 3), (3, 1)]
SWAP_CORE = [(0, 1), (1, 0), (2, 3), (3, 2)]

LANES = 128
QUARTER = 256
HALF = 512
SLAB = 1024
WIDTH = 512
SCALE = 1.0 / (WIDTH * SMOOTHING_TEMP)

F32 = jnp.float32
BF16 = jnp.bfloat16

INFO = 16
MESSAGE = QUARTER + INFO
JOINED = 2 * MESSAGE
LETTER = HALF + MESSAGE

NARROW, CORE, ODD, A_EVEN, HAS_ODD = range(5)


def both_ways(pairs, count):
    kept = [(a, b) for a, b in pairs if b < count]
    return kept + [(b, a) for a, b in kept]


def narrow_swap(block, pairs):
    return lax.ppermute(block, "narrow", pairs)


def exchange(block, hops, crossing):
    count = lax.axis_size("wide")
    first = hops if crossing else 0
    pairs = [
        (base + i, base + i + hops) for base in range(first, count, 2 * hops) for i in range(hops)
    ]
    return lax.ppermute(block, "wide", both_ways(pairs, count))


def normalize(features):
    values = features.astype(F32)
    total = jnp.sum(values * values, axis=1, keepdims=True)
    return (values * lax.rsqrt(total * (1.0 / WIDTH) + EPSILON)).astype(BF16)


def nt_dot(a, b):
    return lax.dot_general(a, b, (((1,), (1,)), ((), ())), preferred_element_type=F32)


def identity():
    return lax.broadcasted_iota(jnp.int32, (LANES, LANES), 0) == lax.broadcasted_iota(
        jnp.int32, (LANES, LANES), 1
    )


def to_column(row):
    return jnp.sum(jnp.where(identity(), row, 0.0), axis=1, keepdims=True)


def to_row(column):
    return jnp.sum(jnp.where(identity(), column, 0.0), axis=0, keepdims=True)


def lane_tiles(values):
    total = values[:, :LANES]
    for i in range(1, values.shape[1] // LANES):
        total = total + values[:, i * LANES : (i + 1) * LANES]
    return total


def sublane_tiles(values):
    rows, columns = values.shape
    return jnp.sum(values.reshape(rows // 8, 8, columns), axis=0)


def block_kernel(rows_ref, columns, mask_ref, i, lanes):
    inner = nt_dot(rows_ref[pl.ds(pl.multiple_of(i * QUARTER, QUARTER), QUARTER), :], columns)
    values = jnp.exp(inner * SCALE)
    top = values[:LANES] * mask_ref[pl.ds(2 * i, 1), lanes]
    bottom = values[LANES:] * mask_ref[pl.ds(2 * i + 1, 1), lanes]
    return top, bottom


def fill_kernel(rows_ref, columns_ref, mask_ref, lanes, kernel_ref, sums_ref, before_ref):
    def step(i, carry):
        blocks = block_kernel(rows_ref, columns_ref[...], mask_ref, i, lanes)
        for j, block in enumerate(blocks):
            at = pl.ds(pl.multiple_of(i * QUARTER + j * LANES, LANES), LANES)
            kernel_ref[at, :] = block
            sums = lane_tiles(block)
            if before_ref is not None:
                sums = sums + before_ref[at, :]
            sums_ref[at, :] = sums
        return carry

    lax.fori_loop(0, 4, step, 0)


def pack_kernel(
    flags, treated_any, control_any, weight_any, band_any, letter_ref, message_ref, treated_ref,
    weight_ref, band_ref, info_ref, sems,
):
    half = pl.ds(pl.multiple_of(flags[CORE] * HALF, HALF), HALF)
    copies = [
        pltpu.make_async_copy(source, target, sems.at[i])
        for i, (source, target) in enumerate(
            (
                (treated_any, treated_ref),
                (weight_any, weight_ref),
                (band_any, band_ref),
                (control_any.at[half, :], letter_ref.at[0:HALF, :]),
            )
        )
    ]
    for copy in copies:
        copy.start()
    info_ref[...] = jnp.zeros_like(info_ref)
    for copy in copies[:3]:
        copy.wait()
    rows = normalize(treated_ref[...])
    weight = weight_ref[...]
    for i in range(3):
        part = weight.astype(BF16).astype(F32)
        info_ref[0:2, i * LANES : (i + 1) * LANES] = part
        weight = weight - part
    info_ref[0:2, 3 * LANES : 3 * LANES + 24] = band_ref[...].astype(F32)
    info = info_ref[...].astype(BF16)
    message_ref[0:QUARTER, :] = rows
    message_ref[QUARTER:MESSAGE, :] = info
    letter_ref[HALF : HALF + QUARTER, :] = rows
    letter_ref[HALF + QUARTER : LETTER, :] = info
    copies[3].wait()


def join_kernel(own_ref, y_ref, joined_ref):
    joined_ref[0:QUARTER, :] = own_ref[0:QUARTER, :]
    joined_ref[QUARTER:HALF, :] = y_ref[0:QUARTER, :]
    joined_ref[HALF : HALF + INFO, :] = own_ref[QUARTER:MESSAGE, :]
    joined_ref[HALF + INFO : JOINED, :] = y_ref[QUARTER:MESSAGE, :]


def columns_kernel(control_any, columns_ref, control_ref, sems):
    copies = [
        pltpu.make_async_copy(
            control_any.at[i * QUARTER : (i + 1) * QUARTER, :],
            control_ref.at[i * QUARTER : (i + 1) * QUARTER, :],
            sems.at[i],
        )
        for i in range(4)
    ]
    for copy in copies:
        copy.start()
    for i, copy in enumerate(copies):
        copy.wait()
        at = slice(i * QUARTER, (i + 1) * QUARTER)
        columns_ref[at, :] = normalize(control_ref[at, :])


def open_kernel(odd_ref, even_ref, columns_ref, quarters_ref):
    columns_ref[0:HALF, :] = normalize(odd_ref[0:HALF, :])
    columns_ref[HALF:SLAB, :] = normalize(even_ref[0:HALF, :])
    quarters_ref[0:QUARTER, :] = odd_ref[HALF : HALF + QUARTER, :]
    quarters_ref[QUARTER:HALF, :] = even_ref[HALF : HALF + QUARTER, :]


def near_kernel(rows_ref, columns_ref, mask_ref, before_ref, kernel_ref, sums_ref):
    fill_kernel(
        rows_ref, columns_ref, mask_ref, slice(SLAB, 2 * SLAB), kernel_ref, sums_ref, before_ref
    )


def prepare_kernel(
    flags, joined_ref, far_ref, columns_ref, rows_ref, kernel_ref, sums_ref, mask_ref, weight_ref,
    pair_ref, band_ref,
):
    n, odd = flags[NARROW], flags[ODD]
    rows_ref[0:HALF, :] = joined_ref[0:HALF, :]
    rows_ref[HALF:SLAB, :] = far_ref[0:HALF, :]

    band_ref[...] = jnp.zeros_like(band_ref)
    for i, (source, first) in enumerate(
        ((joined_ref, HALF), (joined_ref, HALF + INFO), (far_ref, HALF), (far_ref, HALF + INFO))
    ):
        info = source[first : first + INFO, :].astype(F32)
        band_ref[2 * i : 2 * i + 2, :] = info[0:2, 3 * LANES :]
        weights = info[:, :LANES] + info[:, LANES : 2 * LANES] + info[:, 2 * LANES : 3 * LANES]
        for j in range(2):
            at = slice((2 * i + j) * LANES, (2 * i + j + 1) * LANES)
            weight_ref[at, :] = jnp.broadcast_to(to_column(weights[j : j + 1]), (LANES, LANES))
    band = band_ref[...].astype(BF16)
    odd_base = odd * 16
    even_base = 16 - odd * 16
    lane = lax.broadcasted_iota(jnp.int32, (1, 3 * SLAB), 1)
    segment = lane // SLAB
    core = flags[CORE]
    side = jnp.where(lane % SLAB < HALF, odd_base, even_base)
    side = side + 4 * jnp.where(segment == 1, core, 1 - core) + (lane % HALF) // LANES
    wanted = jnp.where(segment == 0, 8 + lane // LANES, side)
    one_hot = lax.broadcasted_iota(jnp.int32, (LANES, 3 * SLAB), 0) == wanted
    mask_ref[...] = jnp.dot(
        band[:16], jnp.where(one_hot, 1.0, 0.0).astype(BF16), preferred_element_type=F32
    )[:8]
    place = lax.broadcasted_iota(jnp.int32, (16, LANES), 0)
    base = jnp.where(place < 2, 8, jnp.where(place < 4, odd_base, even_base))
    chosen = base + 2 * n + place % 2
    select = jnp.where(
        lax.broadcasted_iota(jnp.int32, (16, LANES), 1) == chosen, 1.0, 0.0
    ).astype(BF16)
    by_block = nt_dot(select, band).astype(BF16)
    spread = (
        lax.broadcasted_iota(jnp.int32, (LANES, SLAB), 0)
        == lax.broadcasted_iota(jnp.int32, (LANES, SLAB), 1) // LANES
    )
    pair_ref[...] = jnp.dot(
        by_block, jnp.where(spread, 1.0, 0.0).astype(BF16), preferred_element_type=F32
    )[:8]

    fill_kernel(rows_ref, columns_ref, mask_ref, slice(0, SLAB), kernel_ref, sums_ref, None)


def regroup(flags, first, second):
    low = jnp.concatenate([first[:, :HALF], second[:, :HALF]], axis=1)
    high = jnp.concatenate([first[:, HALF:], second[:, HALF:]], axis=1)
    swap = flags[CORE] > 0
    return jnp.where(swap, high, low), jnp.where(swap, low, high)


def finish_messages(flags, sums, first, second, partial_ref, odd_ref, even_ref, a_ref, b_ref):
    own, near, far = (jnp.sum(part, axis=0, keepdims=True) for part in sums)
    swap = flags[CORE] > 0
    low = jnp.where(swap, far, near)
    high = jnp.where(swap, near, far)
    odd = jnp.concatenate([low[:, :HALF], high[:, :HALF]], axis=1)
    even = jnp.concatenate([low[:, HALF:], high[:, HALF:]], axis=1)
    partial_ref[...] = jnp.zeros_like(partial_ref)
    partial_ref[0:1, :] = own
    partial_ref[1:2, :] = odd
    partial_ref[2:3, :] = even
    odd_ref[0:1, :] = own
    odd_ref[1:2, :] = odd
    odd_ref[2:4, :] = first
    even_ref[0:1, :] = own
    even_ref[1:2, :] = even
    even_ref[2:4, :] = second
    a_even = flags[A_EVEN] > 0
    a_ref[...] = jnp.where(a_even, even, odd)
    b_ref[...] = jnp.where(a_even, odd, even)


def far_kernel(
    flags, rows_ref, columns_ref, mask_ref, own_kernel_ref, near_kernel_ref, before_ref,
    weight_ref, pair_ref, kernel_ref, partial_ref, odd_ref, even_ref, a_ref, b_ref,
):
    def step(i, carry):
        own, near, far = carry
        blocks = block_kernel(
            rows_ref, columns_ref[...], mask_ref, i, slice(2 * SLAB, 3 * SLAB)
        )
        for j, block in enumerate(blocks):
            at = pl.ds(pl.multiple_of(i * QUARTER + j * LANES, LANES), LANES)
            kernel_ref[at, :] = block
            sums = lane_tiles(block) + before_ref[at, :]
            scale = weight_ref[at, 0:1] / jnp.sum(sums, axis=1, keepdims=True)
            own = own + sublane_tiles(own_kernel_ref[at, :] * scale)
            near = near + sublane_tiles(near_kernel_ref[at, :] * scale)
            far = far + sublane_tiles(block * scale)
        return own, near, far

    zero = jnp.zeros((8, SLAB), F32)
    sums = lax.fori_loop(0, 4, step, (zero, zero, zero))
    finish_messages(
        flags, sums, pair_ref[2:4, :], pair_ref[4:6, :], partial_ref, odd_ref, even_ref, a_ref,
        b_ref,
    )


def column_scales(flags, partial_ref, odd_ref, even_ref, a_ref, b_ref, weights):
    a_even = flags[A_EVEN] > 0
    two_odd = jnp.where(a_even, b_ref[...], a_ref[...])
    two_even = jnp.where(a_even, a_ref[...], b_ref[...])
    own = partial_ref[0:1, :] + odd_ref[1:2, :] + even_ref[1:2, :]
    odd = partial_ref[1:2, :] + odd_ref[0:1, :] + two_odd
    even = partial_ref[2:3, :] + even_ref[0:1, :] + two_even
    has_odd = flags[HAS_ODD] > 0
    own_weight, odd_weight, even_weight = (ref[...] for ref in weights)
    odd = jnp.where(has_odd, odd_weight / jnp.where(has_odd, odd, 1.0), 0.0)
    even = even_weight / even
    return own_weight / own, *regroup(flags, odd, even)


def sweep_kernel(
    flags, partial_in, odd_in, even_in, a_in, b_in, own_weight, odd_weight, even_weight,
    own_kernel_ref, near_kernel_ref, far_kernel_ref, weight_ref, quarters_in, quarters_y, row_ref,
    lane_ref, pair_ref, partial_ref, odd_ref, even_ref, a_ref, b_ref, flat_ref,
):
    for i, ref in enumerate((quarters_in, quarters_y)):
        for j in range(2):
            at = j * HALF + i * QUARTER
            pair_ref[at : at + QUARTER, :] = ref[j * QUARTER : (j + 1) * QUARTER, :]
    scales = column_scales(
        flags, partial_in, odd_in, even_in, a_in, b_in, (own_weight, odd_weight, even_weight)
    )
    kernels = (own_kernel_ref, near_kernel_ref, far_kernel_ref)

    def step(i, carry):
        at = pl.ds(pl.multiple_of(i * LANES, LANES), LANES)
        total = jnp.zeros((LANES, LANES), F32)
        for kernel_ref, scale in zip(kernels, scales, strict=True):
            total = total + lane_tiles(kernel_ref[at, :] * scale)
        row_scale = weight_ref[at, 0:1] / jnp.sum(total, axis=1, keepdims=True)
        row_ref[at, :] = jnp.broadcast_to(row_scale, (LANES, LANES))
        flat_ref[pl.ds(i, 1), :] = to_row(row_scale)
        return tuple(
            sums + sublane_tiles(kernel_ref[at, :] * row_scale)
            for kernel_ref, sums in zip(kernels, carry, strict=True)
        )

    zero = jnp.zeros((8, SLAB), F32)
    sums = lax.fori_loop(0, 8, step, (zero, zero, zero))
    for i in range(8):
        lane_ref[0:1, i * LANES : (i + 1) * LANES] = flat_ref[i : i + 1, :]
    flat = jnp.broadcast_to(lane_ref[...], (2, SLAB))
    finish_messages(flags, sums, flat, flat, partial_ref, odd_ref, even_ref, a_ref, b_ref)


def transposed_kernel(
    flags, columns_ref, rows_ref, near_ref, far_ref, pair_ref, odd_in, even_in, odd_rows_ref,
    even_rows_ref, kernel_ref,
):
    own = columns_ref[pl.ds(pl.multiple_of(flags[NARROW] * QUARTER, QUARTER), QUARTER), :]
    odd_rows_ref[0:HALF, :] = near_ref[0:HALF, :]
    odd_rows_ref[HALF:SLAB, :] = far_ref[0:HALF, :]
    even_rows_ref[0:HALF, :] = near_ref[HALF:SLAB, :]
    even_rows_ref[HALF:SLAB, :] = far_ref[HALF:SLAB, :]
    for i, (rows, top, bottom) in enumerate(
        (
            (rows_ref, pair_ref[0:1, :], pair_ref[1:2, :]),
            (odd_rows_ref, odd_in[2:3, :], odd_in[3:4, :]),
            (even_rows_ref, even_in[2:3, :], even_in[3:4, :]),
        )
    ):
        values = jnp.exp(nt_dot(own, rows[...]) * SCALE)
        lanes = slice(i * SLAB, (i + 1) * SLAB)
        kernel_ref[0:LANES, lanes] = values[:LANES] * top
        kernel_ref[LANES:QUARTER, lanes] = values[LANES:] * bottom


def gradient_kernel(
    flags, partial_in, odd_in, even_in, a_in, b_in, own_weight, odd_weight, even_weight, row_ref,
    lane_ref, own_kernel_ref, near_kernel_ref, far_kernel_ref, own_columns_ref, near_columns_ref,
    far_columns_ref, rows_ref, odd_rows_ref, even_rows_ref, transposed_ref, treated_out,
    control_out,
):
    scales = column_scales(
        flags, partial_in, odd_in, even_in, a_in, b_in, (own_weight, odd_weight, even_weight)
    )
    row_scale = row_ref[:, 0:1]
    mass = jnp.zeros((QUARTER, LANES), F32)
    pulled = jnp.zeros((QUARTER, WIDTH), F32)
    for kernel_ref, scale, columns_ref in zip(
        (own_kernel_ref, near_kernel_ref, far_kernel_ref),
        scales,
        (own_columns_ref, near_columns_ref, far_columns_ref),
        strict=True,
    ):
        transport = row_scale * kernel_ref[...] * scale
        mass = mass + lane_tiles(transport)
        pulled = pulled + jnp.dot(
            transport.astype(BF16), columns_ref[...], preferred_element_type=F32
        )
    mass = jnp.sum(mass, axis=1, keepdims=True)
    treated_out[...] = mass * rows_ref[0:QUARTER, :].astype(F32) - pulled

    n = flags[NARROW]

    def own_quarter(row):
        found = row[:, :QUARTER]
        for i in range(1, 4):
            found = jnp.where(n == i, row[:, i * QUARTER : (i + 1) * QUARTER], found)
        return found

    def upright(row):
        return jnp.concatenate([to_column(row[:, :LANES]), to_column(row[:, LANES:])], axis=0)

    own_scale = upright(own_quarter(scales[0]))
    own_mass = upright(own_quarter(own_weight[...]))
    pushed = jnp.zeros((QUARTER, WIDTH), F32)
    for i, (scale, rows) in enumerate(
        ((lane_ref[...], rows_ref), (odd_in[2:3, :], odd_rows_ref), (even_in[2:3, :], even_rows_ref))
    ):
        transport = scale * transposed_ref[:, i * SLAB : (i + 1) * SLAB] * own_scale
        pushed = pushed + jnp.dot(transport.astype(BF16), rows[...], preferred_element_type=F32)
    at = pl.ds(pl.multiple_of(n * QUARTER, QUARTER), QUARTER)
    control_out[...] = own_mass * own_columns_ref[at, :].astype(F32) - pushed


VMEM = pl.BlockSpec(memory_space=pltpu.VMEM)
HBM = pl.BlockSpec(memory_space=pltpu.HBM)
SMEM = pl.BlockSpec(memory_space=pltpu.SMEM)


def call(body, specs, outs, operands, scratch=(), limit=16, out_specs=None):
    return pl.pallas_call(
        body,
        out_shape=tuple(jax.ShapeDtypeStruct(shape, dtype) for shape, dtype in outs),
        in_specs=specs,
        out_specs=out_specs or tuple(VMEM for _ in outs),
        scratch_shapes=list(scratch),
        compiler_params=pltpu.CompilerParams(vmem_limit_bytes=limit << 20),
    )(*operands)


MESSAGES = [((4, SLAB), F32), ((4, SLAB), F32), ((1, SLAB), F32), ((1, SLAB), F32)]


def trade(messages):
    odd, even, a, b = messages
    return (
        exchange(odd, 1, True),
        exchange(even, 1, False),
        exchange(a, 2, True),
        exchange(b, 2, False),
    )


def step(treated, control, treated_weight, control_weight, band):
    wide_index = lax.axis_index("wide")
    n = lax.axis_index("narrow")
    wide_count = lax.axis_size("wide")
    odd = wide_index % 2
    toward_odd = wide_index + 2 * odd - 1
    toward_even = wide_index + 1 - 2 * odd
    values = (
        n,
        n % 2,
        odd,
        jnp.logical_xor(wide_index % 4 >= 2, odd == 1).astype(jnp.int32),
        ((toward_odd >= 0) & (toward_odd < wide_count)).astype(jnp.int32),
    )
    place = lax.iota(jnp.int32, 8)
    flags = jnp.zeros((8,), jnp.int32)
    for i, value in enumerate(values):
        flags = jnp.where(place == i, value, flags)
    weights = [
        lax.dynamic_slice_in_dim(control_weight, jnp.maximum(at, 0) * SLAB, SLAB).reshape(1, SLAB)
        for at in (wide_index, toward_odd, toward_even)
    ]

    treated, control, own_weight, own_band = (
        pltpu.with_memory_space_constraint(x, pltpu.HBM)
        for x in (treated, control, treated_weight.reshape(2, LANES), band)
    )
    letter, message = call(
        pack_kernel,
        [SMEM] + [HBM] * 4,
        [((LETTER, WIDTH), BF16), ((MESSAGE, WIDTH), BF16)],
        [flags, treated, control, own_weight, own_band],
        [
            pltpu.VMEM((QUARTER, WIDTH), BF16),
            pltpu.VMEM((2, LANES), F32),
            pltpu.VMEM((2, 24), jnp.int32),
            pltpu.VMEM((INFO, WIDTH), F32),
            pltpu.SemaphoreType.DMA((4,)),
        ],
    )
    odd_letter = exchange(letter, 1, True)
    even_letter = exchange(letter, 1, False)
    control, *weights = lax.optimization_barrier((control, *weights))
    (own_columns,) = call(
        columns_kernel,
        [HBM],
        [((SLAB, WIDTH), BF16)],
        [pltpu.with_memory_space_constraint(control, pltpu.HBM)],
        [pltpu.VMEM((SLAB, WIDTH), BF16), pltpu.SemaphoreType.DMA((4,))],
    )

    message_y = narrow_swap(message, SWAP_Y)
    (joined,) = call(join_kernel, [VMEM] * 2, [((JOINED, WIDTH), BF16)], [message, message_y])
    joined_far = narrow_swap(joined, SWAP_CORE)

    rows, own_kernel, sums, mask, weight, pairs = call(
        prepare_kernel,
        [SMEM] + [VMEM] * 3,
        [
            ((SLAB, WIDTH), BF16),
            ((SLAB, SLAB), F32),
            ((SLAB, LANES), F32),
            ((8, 3 * SLAB), F32),
            ((SLAB, LANES), F32),
            ((8, SLAB), F32),
        ],
        [flags, joined, joined_far, own_columns],
        [pltpu.VMEM((LANES, LANES), F32)],
    )
    odd_letter, even_letter, _ = lax.optimization_barrier((odd_letter, even_letter, sums))
    near_columns, quarters = call(
        open_kernel,
        [VMEM] * 2,
        [((SLAB, WIDTH), BF16), ((HALF, WIDTH), BF16)],
        [odd_letter, even_letter],
    )
    far_columns = narrow_swap(near_columns, SWAP_CORE)
    quarters_y = narrow_swap(quarters, SWAP_Y)
    near_values, sums = call(
        near_kernel,
        [VMEM] * 4,
        [((SLAB, SLAB), F32), ((SLAB, LANES), F32)],
        [rows, near_columns, mask, sums],
    )
    far_values, partial, *messages = call(
        far_kernel,
        [SMEM] + [VMEM] * 8,
        [((SLAB, SLAB), F32), ((8, SLAB), F32), *MESSAGES],
        [flags, rows, far_columns, mask, own_kernel, near_values, sums, weight, pairs],
    )
    first = trade(messages)

    row_scale, lane_scale, near_rows, partial, *messages = call(
        sweep_kernel,
        [SMEM] + [VMEM] * 14,
        [((SLAB, LANES), F32), ((1, SLAB), F32), ((SLAB, WIDTH), BF16), ((8, SLAB), F32), *MESSAGES],
        [
            flags, partial, *first, *weights, own_kernel, near_values, far_values, weight,
            quarters, quarters_y,
        ],
        [pltpu.VMEM((8, LANES), F32)],
    )
    second = trade(messages)
    far_rows = narrow_swap(near_rows, SWAP_CORE)

    odd_rows, even_rows, transposed = call(
        transposed_kernel,
        [SMEM] + [VMEM] * 7,
        [((SLAB, WIDTH), BF16), ((SLAB, WIDTH), BF16), ((QUARTER, 3 * SLAB), F32)],
        [flags, own_columns, rows, near_rows, far_rows, pairs, first[0], first[1]],
    )

    top = pl.BlockSpec((QUARTER, SLAB), lambda i: (0, 0))
    whole = lambda *shape: pl.BlockSpec(shape, lambda i: (0,) * len(shape))
    return pl.pallas_call(
        gradient_kernel,
        grid=(1,),
        out_shape=(jax.ShapeDtypeStruct((QUARTER, WIDTH), F32),) * 2,
        in_specs=[
            SMEM, whole(8, SLAB), whole(4, SLAB), whole(4, SLAB), whole(1, SLAB), whole(1, SLAB),
            whole(1, SLAB), whole(1, SLAB), whole(1, SLAB),
            pl.BlockSpec((QUARTER, LANES), lambda i: (0, 0)), whole(1, SLAB), top, top, top,
            *[whole(SLAB, WIDTH)] * 6, whole(QUARTER, 3 * SLAB),
        ],
        out_specs=(whole(QUARTER, WIDTH),) * 2,
        compiler_params=pltpu.CompilerParams(vmem_limit_bytes=16 << 20),
        name="gradient_kernel",
    )(
        flags, partial, *second, *weights, row_scale, lane_scale, own_kernel, near_values,
        far_values, own_columns, near_columns, far_columns, rows, odd_rows, even_rows, transposed,
    )


def solution(mesh):
    return jax.shard_map(
        step,
        mesh=mesh,
        in_specs=(
            P(("wide", "narrow"), None),
            P("wide", None),
            P(("wide", "narrow")),
            P(),
            P(("wide", "narrow"), None),
        ),
        out_specs=(P(("wide", "narrow"), None), P(("wide", "narrow"), None)),
        check_vma=False,
    )
```

```python
import jax
import jax.numpy as jnp
from jax import lax
from jax.experimental import pallas as pl
from jax.experimental.pallas import tpu as pltpu
from jax.sharding import PartitionSpec as P


SMOOTHING_TEMP = 0.05
EPSILON = 1e-06

SWAP_Y = [(0, 2), (2, 0), (1, 3), (3, 1)]
SWAP_CORE = [(0, 1), (1, 0), (2, 3), (3, 2)]

LANES = 128
QUARTER = 256
HALF = 512
SLAB = 1024
WIDTH = 512
SCALE = 1.0 / (WIDTH * SMOOTHING_TEMP)

F32 = jnp.float32
BF16 = jnp.bfloat16

INFO = 16
MESSAGE = QUARTER + INFO
JOINED = 2 * MESSAGE
LETTER = HALF + MESSAGE

NARROW, CORE, ODD, A_EVEN, HAS_ODD = range(5)


def both_ways(pairs, count):
    kept = [(a, b) for a, b in pairs if b < count]
    return kept + [(b, a) for a, b in kept]


def narrow_swap(block, pairs):
    return lax.ppermute(block, "narrow", pairs)


def exchange(block, hops, crossing):
    count = lax.axis_size("wide")
    first = hops if crossing else 0
    pairs = [
        (base + i, base + i + hops) for base in range(first, count, 2 * hops) for i in range(hops)
    ]
    return lax.ppermute(block, "wide", both_ways(pairs, count))


def split_exchange(block, crossing):
    count = lax.axis_size("wide")
    narrow = lax.axis_size("narrow")
    pairs = []
    for n in range(narrow):
        hops = 1 + n % 2
        first = hops if crossing else 0
        one = [
            (base + i, base + i + hops)
            for base in range(first, count, 2 * hops)
            for i in range(hops)
        ]
        pairs += [(a * narrow + n, b * narrow + n) for a, b in both_ways(one, count)]
    return lax.ppermute(block, ("wide", "narrow"), pairs)


def normalize(features):
    values = features.astype(F32)
    total = jnp.sum(values * values, axis=1, keepdims=True)
    return (values * lax.rsqrt(total * (1.0 / WIDTH) + EPSILON)).astype(BF16)


def nt_dot(a, b):
    return lax.dot_general(a, b, (((1,), (1,)), ((), ())), preferred_element_type=F32)


def identity():
    return lax.broadcasted_iota(jnp.int32, (LANES, LANES), 0) == lax.broadcasted_iota(
        jnp.int32, (LANES, LANES), 1
    )


def to_column(row):
    return jnp.sum(jnp.where(identity(), row, 0.0), axis=1, keepdims=True)


def to_row(column):
    return jnp.sum(jnp.where(identity(), column, 0.0), axis=0, keepdims=True)


def lane_tiles(values):
    total = values[:, :LANES]
    for i in range(1, values.shape[1] // LANES):
        total = total + values[:, i * LANES : (i + 1) * LANES]
    return total


def sublane_tiles(values):
    rows, columns = values.shape
    return jnp.sum(values.reshape(rows // 8, 8, columns), axis=0)


def block_kernel(rows_ref, columns, mask_ref, i, lanes):
    inner = nt_dot(rows_ref[pl.ds(pl.multiple_of(i * QUARTER, QUARTER), QUARTER), :], columns)
    values = jnp.exp(inner * SCALE)
    top = values[:LANES] * mask_ref[pl.ds(2 * i, 1), lanes]
    bottom = values[LANES:] * mask_ref[pl.ds(2 * i + 1, 1), lanes]
    return top, bottom


def fill_kernel(rows_ref, columns_ref, mask_ref, lanes, kernel_ref, sums_ref, before_ref):
    def step(i, carry):
        blocks = block_kernel(rows_ref, columns_ref[...], mask_ref, i, lanes)
        for j, block in enumerate(blocks):
            at = pl.ds(pl.multiple_of(i * QUARTER + j * LANES, LANES), LANES)
            kernel_ref[at, :] = block
            sums = lane_tiles(block)
            if before_ref is not None:
                sums = sums + before_ref[at, :]
            sums_ref[at, :] = sums
        return carry

    lax.fori_loop(0, 4, step, 0)


def pack_kernel(
    flags, treated_any, control_any, weight_any, band_any, letter_ref, message_ref, treated_ref,
    weight_ref, band_ref, info_ref, sems,
):
    half = pl.ds(pl.multiple_of(flags[CORE] * HALF, HALF), HALF)
    copies = [
        pltpu.make_async_copy(source, target, sems.at[i])
        for i, (source, target) in enumerate(
            (
                (treated_any, treated_ref),
                (weight_any, weight_ref),
                (band_any, band_ref),
                (control_any.at[half, :], letter_ref.at[0:HALF, :]),
            )
        )
    ]
    for copy in copies:
        copy.start()
    info_ref[...] = jnp.zeros_like(info_ref)
    for copy in copies[:3]:
        copy.wait()
    rows = normalize(treated_ref[...])
    weight = weight_ref[...]
    for i in range(3):
        part = weight.astype(BF16).astype(F32)
        info_ref[0:2, i * LANES : (i + 1) * LANES] = part
        weight = weight - part
    info_ref[0:2, 3 * LANES : 3 * LANES + 24] = band_ref[...].astype(F32)
    info = info_ref[...].astype(BF16)
    message_ref[0:QUARTER, :] = rows
    message_ref[QUARTER:MESSAGE, :] = info
    letter_ref[HALF : HALF + QUARTER, :] = rows
    letter_ref[HALF + QUARTER : LETTER, :] = info
    copies[3].wait()


def join_kernel(own_ref, y_ref, joined_ref):
    joined_ref[0:QUARTER, :] = own_ref[0:QUARTER, :]
    joined_ref[QUARTER:HALF, :] = y_ref[0:QUARTER, :]
    joined_ref[HALF : HALF + INFO, :] = own_ref[QUARTER:MESSAGE, :]
    joined_ref[HALF + INFO : JOINED, :] = y_ref[QUARTER:MESSAGE, :]


def columns_kernel(control_any, columns_ref, control_ref, sems):
    copies = [
        pltpu.make_async_copy(
            control_any.at[i * QUARTER : (i + 1) * QUARTER, :],
            control_ref.at[i * QUARTER : (i + 1) * QUARTER, :],
            sems.at[i],
        )
        for i in range(4)
    ]
    for copy in copies:
        copy.start()
    for i, copy in enumerate(copies):
        copy.wait()
        at = slice(i * QUARTER, (i + 1) * QUARTER)
        columns_ref[at, :] = normalize(control_ref[at, :])


def open_kernel(odd_ref, even_ref, columns_ref, quarters_ref):
    columns_ref[0:HALF, :] = normalize(odd_ref[0:HALF, :])
    columns_ref[HALF:SLAB, :] = normalize(even_ref[0:HALF, :])
    quarters_ref[0:QUARTER, :] = odd_ref[HALF : HALF + QUARTER, :]
    quarters_ref[QUARTER:HALF, :] = even_ref[HALF : HALF + QUARTER, :]


def near_kernel(rows_ref, columns_ref, mask_ref, before_ref, kernel_ref, sums_ref):
    fill_kernel(
        rows_ref, columns_ref, mask_ref, slice(SLAB, 2 * SLAB), kernel_ref, sums_ref, before_ref
    )


def prepare_kernel(
    flags, joined_ref, far_ref, columns_ref, rows_ref, kernel_ref, sums_ref, mask_ref, weight_ref,
    pair_ref, band_ref,
):
    n, odd, core = flags[NARROW], flags[ODD], flags[CORE]
    rows_ref[0:HALF, :] = joined_ref[0:HALF, :]
    rows_ref[HALF:SLAB, :] = far_ref[0:HALF, :]

    band_ref[...] = jnp.zeros_like(band_ref)
    for i, (source, first) in enumerate(
        ((joined_ref, HALF), (joined_ref, HALF + INFO), (far_ref, HALF), (far_ref, HALF + INFO))
    ):
        info = source[first : first + INFO, :].astype(F32)
        band_ref[2 * i : 2 * i + 2, :] = info[0:2, 3 * LANES :]
        weights = info[:, :LANES] + info[:, LANES : 2 * LANES] + info[:, 2 * LANES : 3 * LANES]
        for j in range(2):
            at = slice((2 * i + j) * LANES, (2 * i + j + 1) * LANES)
            weight_ref[at, :] = jnp.broadcast_to(to_column(weights[j : j + 1]), (LANES, LANES))
    band = band_ref[...].astype(BF16)
    odd_base = odd * 16
    even_base = 16 - odd * 16
    lane = lax.broadcasted_iota(jnp.int32, (1, 3 * SLAB), 1)
    segment = lane // SLAB
    side = jnp.where(lane % SLAB < HALF, odd_base, even_base)
    side = side + 4 * jnp.where(segment == 1, core, 1 - core) + (lane % HALF) // LANES
    wanted = jnp.where(segment == 0, 8 + lane // LANES, side)
    one_hot = lax.broadcasted_iota(jnp.int32, (LANES, 3 * SLAB), 0) == wanted
    mask_ref[...] = jnp.dot(
        band[:16], jnp.where(one_hot, 1.0, 0.0).astype(BF16), preferred_element_type=F32
    )[:8]
    place = lax.broadcasted_iota(jnp.int32, (16, LANES), 0)
    base = jnp.where(place < 2, 8, jnp.where(place < 6, odd_base, even_base))
    other = (place == 4) | (place == 5) | (place == 8) | (place == 9)
    quarter = n + jnp.where(other, 1 - 2 * core, 0)
    chosen = base + 2 * quarter + place % 2
    select = jnp.where(
        lax.broadcasted_iota(jnp.int32, (16, LANES), 1) == chosen, 1.0, 0.0
    ).astype(BF16)
    by_block = nt_dot(select, band).astype(BF16)
    spread = (
        lax.broadcasted_iota(jnp.int32, (LANES, SLAB), 0)
        == lax.broadcasted_iota(jnp.int32, (LANES, SLAB), 1) // LANES
    )
    pair_ref[...] = jnp.dot(
        by_block, jnp.where(spread, 1.0, 0.0).astype(BF16), preferred_element_type=F32
    )

    fill_kernel(rows_ref, columns_ref, mask_ref, slice(0, SLAB), kernel_ref, sums_ref, None)


def regroup(flags, first, second):
    low = jnp.concatenate([first[:, :HALF], second[:, :HALF]], axis=1)
    high = jnp.concatenate([first[:, HALF:], second[:, HALF:]], axis=1)
    swap = flags[CORE] > 0
    return jnp.where(swap, high, low), jnp.where(swap, low, high)


def finish_messages(flags, sums, first, second, partial_ref, cross_ref, inner_ref):
    own, near, far = (jnp.sum(part, axis=0, keepdims=True) for part in sums)
    one = flags[CORE] > 0
    low = jnp.where(one, far, near)
    high = jnp.where(one, near, far)
    odd = jnp.concatenate([low[:, :HALF], high[:, :HALF]], axis=1)
    even = jnp.concatenate([low[:, HALF:], high[:, HALF:]], axis=1)
    partial_ref[...] = jnp.zeros_like(partial_ref)
    partial_ref[0:1, :] = own
    partial_ref[1:2, :] = odd
    partial_ref[2:3, :] = even
    a_even = flags[A_EVEN] > 0
    for ref, side, along, distant in (
        (cross_ref, odd, first, jnp.where(a_even, even, odd)),
        (inner_ref, even, second, jnp.where(a_even, odd, even)),
    ):
        ref[...] = jnp.zeros_like(ref)
        ref[0:1, :] = jnp.where(one, distant, own)
        ref[1:2, :] = side
        ref[2 : 2 + along.shape[0], :] = along


def stack_kernel(cross_ref, inner_ref, both_ref):
    both_ref[0:8, :] = cross_ref[...]
    both_ref[8:16, :] = inner_ref[...]


def received(flags, mine_ref, theirs_ref):
    one = flags[CORE] > 0
    mine, theirs = mine_ref[...], theirs_ref[...]
    return jnp.where(one, theirs, mine), jnp.where(one, mine, theirs)


def turned(flags, rows):
    swapped = jnp.concatenate([rows[:, HALF:], rows[:, :HALF]], axis=1)
    return jnp.where(flags[CORE] > 0, swapped, rows)


def far_kernel(
    flags, rows_ref, columns_ref, mask_ref, own_kernel_ref, near_kernel_ref, before_ref,
    weight_ref, pair_ref, kernel_ref, partial_ref, cross_ref, inner_ref,
):
    def step(i, carry):
        own, near, far = carry
        blocks = block_kernel(
            rows_ref, columns_ref[...], mask_ref, i, slice(2 * SLAB, 3 * SLAB)
        )
        for j, block in enumerate(blocks):
            at = pl.ds(pl.multiple_of(i * QUARTER + j * LANES, LANES), LANES)
            kernel_ref[at, :] = block
            sums = lane_tiles(block) + before_ref[at, :]
            scale = weight_ref[at, 0:1] / jnp.sum(sums, axis=1, keepdims=True)
            own = own + sublane_tiles(own_kernel_ref[at, :] * scale)
            near = near + sublane_tiles(near_kernel_ref[at, :] * scale)
            far = far + sublane_tiles(block * scale)
        return own, near, far

    zero = jnp.zeros((8, SLAB), F32)
    sums = lax.fori_loop(0, 4, step, (zero, zero, zero))
    finish_messages(
        flags, sums, pair_ref[2:6, :], pair_ref[6:10, :], partial_ref, cross_ref, inner_ref
    )


def column_scales(flags, partial_ref, mine_ref, theirs_ref, weights):
    a_even = flags[A_EVEN] > 0
    close, distant = received(flags, mine_ref, theirs_ref)
    a, b = distant[0:1], distant[8:9]
    own = partial_ref[0:1, :] + close[1:2] + close[9:10]
    odd = partial_ref[1:2, :] + close[0:1] + jnp.where(a_even, b, a)
    even = partial_ref[2:3, :] + close[8:9] + jnp.where(a_even, a, b)
    has_odd = flags[HAS_ODD] > 0
    own_weight, odd_weight, even_weight = (ref[...] for ref in weights)
    odd = jnp.where(has_odd, odd_weight / jnp.where(has_odd, odd, 1.0), 0.0)
    even = even_weight / even
    return own_weight / own, *regroup(flags, odd, even)


def sweep_kernel(
    flags, partial_in, mine_in, theirs_in, own_weight, odd_weight, even_weight, own_kernel_ref,
    near_kernel_ref, far_kernel_ref, weight_ref, row_ref, lane_ref, partial_ref, cross_ref,
    inner_ref, flat_ref,
):
    scales = column_scales(
        flags, partial_in, mine_in, theirs_in, (own_weight, odd_weight, even_weight)
    )
    kernels = (own_kernel_ref, near_kernel_ref, far_kernel_ref)

    def step(i, carry):
        at = pl.ds(pl.multiple_of(i * LANES, LANES), LANES)
        total = jnp.zeros((LANES, LANES), F32)
        for kernel_ref, scale in zip(kernels, scales, strict=True):
            total = total + lane_tiles(kernel_ref[at, :] * scale)
        row_scale = weight_ref[at, 0:1] / jnp.sum(total, axis=1, keepdims=True)
        row_ref[at, :] = jnp.broadcast_to(row_scale, (LANES, LANES))
        flat_ref[pl.ds(i, 1), :] = to_row(row_scale)
        return tuple(
            sums + sublane_tiles(kernel_ref[at, :] * row_scale)
            for kernel_ref, sums in zip(kernels, carry, strict=True)
        )

    zero = jnp.zeros((8, SLAB), F32)
    sums = lax.fori_loop(0, 8, step, (zero, zero, zero))
    for i in range(8):
        lane_ref[0:1, i * LANES : (i + 1) * LANES] = flat_ref[i : i + 1, :]
    flat = lane_ref[...]
    finish_messages(flags, sums, flat, flat, partial_ref, cross_ref, inner_ref)


def quarters_kernel(own_ref, y_ref, pair_ref):
    for i, ref in enumerate((own_ref, y_ref)):
        for j in range(2):
            at = j * HALF + i * QUARTER
            pair_ref[at : at + QUARTER, :] = ref[j * QUARTER : (j + 1) * QUARTER, :]


def transposed_kernel(
    flags, columns_ref, rows_ref, near_ref, far_ref, pair_ref, mine_in, theirs_in, odd_rows_ref,
    even_rows_ref, kernel_ref,
):
    own = columns_ref[pl.ds(pl.multiple_of(flags[NARROW] * QUARTER, QUARTER), QUARTER), :]
    odd_rows_ref[0:HALF, :] = near_ref[0:HALF, :]
    odd_rows_ref[HALF:SLAB, :] = far_ref[0:HALF, :]
    even_rows_ref[0:HALF, :] = near_ref[HALF:SLAB, :]
    even_rows_ref[HALF:SLAB, :] = far_ref[HALF:SLAB, :]
    one = flags[CORE] > 0
    close, _ = received(flags, mine_in, theirs_in)
    odd_pairs = turned(flags, jnp.where(one, close[4:6], close[2:4]))
    even_pairs = turned(flags, jnp.where(one, close[12:14], close[10:12]))
    for i, (rows, top, bottom) in enumerate(
        (
            (rows_ref, pair_ref[0:1, :], pair_ref[1:2, :]),
            (odd_rows_ref, odd_pairs[0:1], odd_pairs[1:2]),
            (even_rows_ref, even_pairs[0:1], even_pairs[1:2]),
        )
    ):
        values = jnp.exp(nt_dot(own, rows[...]) * SCALE)
        lanes = slice(i * SLAB, (i + 1) * SLAB)
        kernel_ref[0:LANES, lanes] = values[:LANES] * top
        kernel_ref[LANES:QUARTER, lanes] = values[LANES:] * bottom


def gradient_kernel(
    flags, partial_in, mine_in, theirs_in, own_weight, odd_weight, even_weight, row_ref, lane_ref,
    own_kernel_ref, near_kernel_ref, far_kernel_ref, own_columns_ref, near_columns_ref,
    far_columns_ref, rows_ref, odd_rows_ref, even_rows_ref, transposed_ref, treated_out,
    control_out,
):
    scales = column_scales(
        flags, partial_in, mine_in, theirs_in, (own_weight, odd_weight, even_weight)
    )
    close, _ = received(flags, mine_in, theirs_in)
    row_scale = row_ref[:, 0:1]
    mass = jnp.zeros((QUARTER, LANES), F32)
    pulled = jnp.zeros((QUARTER, WIDTH), F32)
    for kernel_ref, scale, columns_ref in zip(
        (own_kernel_ref, near_kernel_ref, far_kernel_ref),
        scales,
        (own_columns_ref, near_columns_ref, far_columns_ref),
        strict=True,
    ):
        transport = row_scale * kernel_ref[...] * scale
        mass = mass + lane_tiles(transport)
        pulled = pulled + jnp.dot(
            transport.astype(BF16), columns_ref[...], preferred_element_type=F32
        )
    mass = jnp.sum(mass, axis=1, keepdims=True)
    treated_out[...] = mass * rows_ref[0:QUARTER, :].astype(F32) - pulled

    n = flags[NARROW]

    def own_quarter(row):
        found = row[:, :QUARTER]
        for i in range(1, 4):
            found = jnp.where(n == i, row[:, i * QUARTER : (i + 1) * QUARTER], found)
        return found

    def upright(row):
        return jnp.concatenate([to_column(row[:, :LANES]), to_column(row[:, LANES:])], axis=0)

    own_scale = upright(own_quarter(scales[0]))
    own_mass = upright(own_quarter(own_weight[...]))
    pushed = jnp.zeros((QUARTER, WIDTH), F32)
    for i, (scale, rows) in enumerate(
        (
            (lane_ref[...], rows_ref),
            (turned(flags, close[2:3]), odd_rows_ref),
            (turned(flags, close[10:11]), even_rows_ref),
        )
    ):
        transport = scale * transposed_ref[:, i * SLAB : (i + 1) * SLAB] * own_scale
        pushed = pushed + jnp.dot(transport.astype(BF16), rows[...], preferred_element_type=F32)
    at = pl.ds(pl.multiple_of(n * QUARTER, QUARTER), QUARTER)
    control_out[...] = own_mass * own_columns_ref[at, :].astype(F32) - pushed


VMEM = pl.BlockSpec(memory_space=pltpu.VMEM)
HBM = pl.BlockSpec(memory_space=pltpu.HBM)
SMEM = pl.BlockSpec(memory_space=pltpu.SMEM)


def call(body, specs, outs, operands, scratch=(), limit=16, out_specs=None):
    return pl.pallas_call(
        body,
        out_shape=tuple(jax.ShapeDtypeStruct(shape, dtype) for shape, dtype in outs),
        in_specs=specs,
        out_specs=out_specs or tuple(VMEM for _ in outs),
        scratch_shapes=list(scratch),
        compiler_params=pltpu.CompilerParams(vmem_limit_bytes=limit << 20),
    )(*operands)


MESSAGES = [((8, SLAB), F32), ((8, SLAB), F32)]


def trade(messages):
    cross = split_exchange(messages[0], True)
    inner = split_exchange(messages[1], False)
    (mine,) = call(stack_kernel, [VMEM] * 2, [((16, SLAB), F32)], [cross, inner])
    return mine, narrow_swap(mine, SWAP_CORE)


def step(treated, control, treated_weight, control_weight, band):
    wide_index = lax.axis_index("wide")
    n = lax.axis_index("narrow")
    wide_count = lax.axis_size("wide")
    odd = wide_index % 2
    toward_odd = wide_index + 2 * odd - 1
    toward_even = wide_index + 1 - 2 * odd
    values = (
        n,
        n % 2,
        odd,
        jnp.logical_xor(wide_index % 4 >= 2, odd == 1).astype(jnp.int32),
        ((toward_odd >= 0) & (toward_odd < wide_count)).astype(jnp.int32),
    )
    place = lax.iota(jnp.int32, 8)
    flags = jnp.zeros((8,), jnp.int32)
    for i, value in enumerate(values):
        flags = jnp.where(place == i, value, flags)
    weights = [
        lax.dynamic_slice_in_dim(control_weight, jnp.maximum(at, 0) * SLAB, SLAB).reshape(1, SLAB)
        for at in (wide_index, toward_odd, toward_even)
    ]

    treated, control, own_weight, own_band = (
        pltpu.with_memory_space_constraint(x, pltpu.HBM)
        for x in (treated, control, treated_weight.reshape(2, LANES), band)
    )
    letter, message = call(
        pack_kernel,
        [SMEM] + [HBM] * 4,
        [((LETTER, WIDTH), BF16), ((MESSAGE, WIDTH), BF16)],
        [flags, treated, control, own_weight, own_band],
        [
            pltpu.VMEM((QUARTER, WIDTH), BF16),
            pltpu.VMEM((2, LANES), F32),
            pltpu.VMEM((2, 24), jnp.int32),
            pltpu.VMEM((INFO, WIDTH), F32),
            pltpu.SemaphoreType.DMA((4,)),
        ],
    )
    odd_letter = exchange(letter, 1, True)
    even_letter = exchange(letter, 1, False)
    control, *weights = lax.optimization_barrier((control, *weights))
    (own_columns,) = call(
        columns_kernel,
        [HBM],
        [((SLAB, WIDTH), BF16)],
        [pltpu.with_memory_space_constraint(control, pltpu.HBM)],
        [pltpu.VMEM((SLAB, WIDTH), BF16), pltpu.SemaphoreType.DMA((4,))],
    )

    message_y = narrow_swap(message, SWAP_Y)
    (joined,) = call(join_kernel, [VMEM] * 2, [((JOINED, WIDTH), BF16)], [message, message_y])
    joined_far = narrow_swap(joined, SWAP_CORE)

    rows, own_kernel, sums, mask, weight, pairs = call(
        prepare_kernel,
        [SMEM] + [VMEM] * 3,
        [
            ((SLAB, WIDTH), BF16),
            ((SLAB, SLAB), F32),
            ((SLAB, LANES), F32),
            ((8, 3 * SLAB), F32),
            ((SLAB, LANES), F32),
            ((16, SLAB), F32),
        ],
        [flags, joined, joined_far, own_columns],
        [pltpu.VMEM((LANES, LANES), F32)],
    )
    odd_letter, even_letter, _ = lax.optimization_barrier((odd_letter, even_letter, sums))
    near_columns, quarters = call(
        open_kernel,
        [VMEM] * 2,
        [((SLAB, WIDTH), BF16), ((HALF, WIDTH), BF16)],
        [odd_letter, even_letter],
    )
    far_columns = narrow_swap(near_columns, SWAP_CORE)
    quarters_y = narrow_swap(quarters, SWAP_Y)
    near_values, sums = call(
        near_kernel,
        [VMEM] * 4,
        [((SLAB, SLAB), F32), ((SLAB, LANES), F32)],
        [rows, near_columns, mask, sums],
    )
    far_values, partial, *messages = call(
        far_kernel,
        [SMEM] + [VMEM] * 8,
        [((SLAB, SLAB), F32), ((8, SLAB), F32), *MESSAGES],
        [flags, rows, far_columns, mask, own_kernel, near_values, sums, weight, pairs],
    )
    first = trade(messages)

    row_scale, lane_scale, partial, *messages = call(
        sweep_kernel,
        [SMEM] + [VMEM] * 10,
        [((SLAB, LANES), F32), ((1, SLAB), F32), ((8, SLAB), F32), *MESSAGES],
        [flags, partial, *first, *weights, own_kernel, near_values, far_values, weight],
        [pltpu.VMEM((8, LANES), F32)],
    )
    (near_rows,) = call(
        quarters_kernel, [VMEM] * 2, [((SLAB, WIDTH), BF16)], [quarters, quarters_y]
    )
    second = trade(messages)
    far_rows = narrow_swap(near_rows, SWAP_CORE)

    odd_rows, even_rows, transposed = call(
        transposed_kernel,
        [SMEM] + [VMEM] * 7,
        [((SLAB, WIDTH), BF16), ((SLAB, WIDTH), BF16), ((QUARTER, 3 * SLAB), F32)],
        [flags, own_columns, rows, near_rows, far_rows, pairs, *first],
    )

    top = pl.BlockSpec((QUARTER, SLAB), lambda i: (0, 0))
    whole = lambda *shape: pl.BlockSpec(shape, lambda i: (0,) * len(shape))
    return pl.pallas_call(
        gradient_kernel,
        grid=(1,),
        out_shape=(jax.ShapeDtypeStruct((QUARTER, WIDTH), F32),) * 2,
        in_specs=[
            SMEM, whole(8, SLAB), whole(16, SLAB), whole(16, SLAB),
            whole(1, SLAB), whole(1, SLAB), whole(1, SLAB),
            pl.BlockSpec((QUARTER, LANES), lambda i: (0, 0)), whole(1, SLAB), top, top, top,
            *[whole(SLAB, WIDTH)] * 6, whole(QUARTER, 3 * SLAB),
        ],
        out_specs=(whole(QUARTER, WIDTH),) * 2,
        compiler_params=pltpu.CompilerParams(vmem_limit_bytes=16 << 20),
        name="gradient_kernel",
    )(
        flags, partial, *second, *weights, row_scale, lane_scale, own_kernel, near_values,
        far_values, own_columns, near_columns, far_columns, rows, odd_rows, even_rows, transposed,
    )


def solution(mesh):
    return jax.shard_map(
        step,
        mesh=mesh,
        in_specs=(
            P(("wide", "narrow"), None),
            P("wide", None),
            P(("wide", "narrow")),
            P(),
            P(("wide", "narrow"), None),
        ),
        out_specs=(P(("wide", "narrow"), None), P(("wide", "narrow"), None)),
        check_vma=False,
    )
```

```python
import jax
import jax.numpy as jnp
from jax import lax
from jax.experimental import pallas as pl
from jax.experimental.pallas import tpu as pltpu
from jax.sharding import PartitionSpec as P


SMOOTHING_TEMP = 0.05
EPSILON = 1e-06

SWAP_Y = [(0, 2), (2, 0), (1, 3), (3, 1)]
SWAP_CORE = [(0, 1), (1, 0), (2, 3), (3, 2)]

LANES = 128
QUARTER = 256
HALF = 512
SLAB = 1024
WIDTH = 512
SCALE = 1.0 / (WIDTH * SMOOTHING_TEMP)

F32 = jnp.float32
BF16 = jnp.bfloat16

INFO = 16
MESSAGE = QUARTER + INFO
JOINED = 2 * MESSAGE
LETTER = HALF + QUARTER
NOTE = 16

NARROW, CORE, Y, ODD, A_EVEN, HAS_ODD, FLIPPED = range(7)


def narrow_swap(block, pairs):
    return lax.ppermute(block, "narrow", pairs)


def exchange(block, hops, crossing):
    count = lax.axis_size("wide")
    narrow = lax.axis_size("narrow")
    pairs = []
    for n in range(narrow):
        far = hops[n % 2]
        for base in range(far if crossing else 0, count, 2 * far):
            for low in range(base, base + far):
                high = low + far
                if high < count:
                    other = n ^ 2 if low < count // 2 <= high else n
                    one, two = low * narrow + n, high * narrow + other
                    pairs += [(one, two), (two, one)]
    return lax.ppermute(block, ("wide", "narrow"), pairs)


def normalize(features):
    values = features.astype(F32)
    total = jnp.sum(values * values, axis=1, keepdims=True)
    return (values * lax.rsqrt(total * (1.0 / WIDTH) + EPSILON)).astype(BF16)


def nt_dot(a, b):
    return lax.dot_general(a, b, (((1,), (1,)), ((), ())), preferred_element_type=F32)


def identity():
    return lax.broadcasted_iota(jnp.int32, (LANES, LANES), 0) == lax.broadcasted_iota(
        jnp.int32, (LANES, LANES), 1
    )


def to_column(row):
    return jnp.sum(jnp.where(identity(), row, 0.0), axis=1, keepdims=True)


def to_row(column):
    return jnp.sum(jnp.where(identity(), column, 0.0), axis=0, keepdims=True)


def lane_tiles(values):
    total = values[:, :LANES]
    for i in range(1, values.shape[1] // LANES):
        total = total + values[:, i * LANES : (i + 1) * LANES]
    return total


def sublane_tiles(values):
    rows, columns = values.shape
    return jnp.sum(values.reshape(rows // 8, 8, columns), axis=0)


def block_kernel(rows_ref, columns, mask_ref, i, lanes):
    inner = nt_dot(rows_ref[pl.ds(pl.multiple_of(i * QUARTER, QUARTER), QUARTER), :], columns)
    values = jnp.exp(inner * SCALE)
    top = values[:LANES] * mask_ref[pl.ds(2 * i, 1), lanes]
    bottom = values[LANES:] * mask_ref[pl.ds(2 * i + 1, 1), lanes]
    return top, bottom


def fill_kernel(rows_ref, columns_ref, mask_ref, lanes, kernel_ref, sums_ref, before_ref):
    def step(i, carry):
        blocks = block_kernel(rows_ref, columns_ref[...], mask_ref, i, lanes)
        for j, block in enumerate(blocks):
            at = pl.ds(pl.multiple_of(i * QUARTER + j * LANES, LANES), LANES)
            kernel_ref[at, :] = block
            sums = lane_tiles(block)
            if before_ref is not None:
                sums = sums + before_ref[at, :]
            sums_ref[at, :] = sums
        return carry

    lax.fori_loop(0, 4, step, 0)


def pack_kernel(
    flags, treated_any, control_any, weight_any, band_any, letter_ref, message_ref, treated_ref,
    weight_ref, band_ref, info_ref, sems,
):
    half = pl.ds(pl.multiple_of(flags[CORE] * HALF, HALF), HALF)
    copies = [
        pltpu.make_async_copy(source, target, sems.at[i])
        for i, (source, target) in enumerate(
            (
                (treated_any, treated_ref),
                (weight_any, weight_ref),
                (band_any, band_ref),
                (control_any.at[half, :], letter_ref.at[0:HALF, :]),
            )
        )
    ]
    for copy in copies:
        copy.start()
    info_ref[...] = jnp.zeros_like(info_ref)
    for copy in copies[:3]:
        copy.wait()
    rows = normalize(treated_ref[...])
    weight = weight_ref[...]
    for i in range(3):
        part = weight.astype(BF16).astype(F32)
        info_ref[0:2, i * LANES : (i + 1) * LANES] = part
        weight = weight - part
    info_ref[0:2, 3 * LANES : 3 * LANES + 24] = band_ref[...].astype(F32)
    info = info_ref[...].astype(BF16)
    message_ref[0:QUARTER, :] = rows
    message_ref[QUARTER:MESSAGE, :] = info
    letter_ref[HALF:LETTER, :] = rows
    copies[3].wait()


def join_kernel(flags, own_ref, y_ref, joined_ref):
    for ref, y in ((own_ref, flags[Y]), (y_ref, 1 - flags[Y])):
        joined_ref[pl.ds(pl.multiple_of(y * QUARTER, QUARTER), QUARTER), :] = ref[0:QUARTER, :]
        joined_ref[pl.ds(pl.multiple_of(HALF + y * INFO, INFO), INFO), :] = ref[QUARTER:MESSAGE, :]


def columns_kernel(control_any, columns_ref, control_ref, sems):
    copies = [
        pltpu.make_async_copy(
            control_any.at[i * QUARTER : (i + 1) * QUARTER, :],
            control_ref.at[i * QUARTER : (i + 1) * QUARTER, :],
            sems.at[i],
        )
        for i in range(4)
    ]
    for copy in copies:
        copy.start()
    for i, copy in enumerate(copies):
        copy.wait()
        at = slice(i * QUARTER, (i + 1) * QUARTER)
        columns_ref[at, :] = normalize(control_ref[at, :])


def open_kernel(odd_ref, even_ref, columns_ref, quarters_ref):
    columns_ref[0:HALF, :] = normalize(odd_ref[0:HALF, :])
    columns_ref[HALF:SLAB, :] = normalize(even_ref[0:HALF, :])
    quarters_ref[0:QUARTER, :] = odd_ref[HALF:LETTER, :]
    quarters_ref[QUARTER:HALF, :] = even_ref[HALF:LETTER, :]


def near_kernel(rows_ref, columns_ref, mask_ref, before_ref, kernel_ref, sums_ref):
    fill_kernel(
        rows_ref, columns_ref, mask_ref, slice(SLAB, 2 * SLAB), kernel_ref, sums_ref, before_ref
    )


def prepare_kernel(
    flags, joined_ref, far_ref, columns_ref, rows_ref, kernel_ref, sums_ref, mask_ref, weight_ref,
    pair_ref, band_ref,
):
    n, odd, core = flags[NARROW], flags[ODD], flags[CORE]
    rows_ref[0:HALF, :] = joined_ref[0:HALF, :]
    rows_ref[HALF:SLAB, :] = far_ref[0:HALF, :]

    band_ref[...] = jnp.zeros_like(band_ref)
    for i, (source, first) in enumerate(
        ((joined_ref, HALF), (joined_ref, HALF + INFO), (far_ref, HALF), (far_ref, HALF + INFO))
    ):
        info = source[first : first + INFO, :].astype(F32)
        band_ref[2 * i : 2 * i + 2, :] = info[0:2, 3 * LANES :]
        weights = info[:, :LANES] + info[:, LANES : 2 * LANES] + info[:, 2 * LANES : 3 * LANES]
        for j in range(2):
            at = slice((2 * i + j) * LANES, (2 * i + j + 1) * LANES)
            weight_ref[at, :] = jnp.broadcast_to(to_column(weights[j : j + 1]), (LANES, LANES))
    band = band_ref[...].astype(BF16)
    odd_base = odd * 16
    even_base = 16 - odd * 16
    lane = lax.broadcasted_iota(jnp.int32, (1, 3 * SLAB), 1)
    segment = lane // SLAB
    side = jnp.where(lane % SLAB < HALF, odd_base, even_base)
    side = side + 4 * jnp.where(segment == 1, core, 1 - core) + (lane % HALF) // LANES
    wanted = jnp.where(segment == 0, 8 + lane // LANES, side)
    one_hot = lax.broadcasted_iota(jnp.int32, (LANES, 3 * SLAB), 0) == wanted
    mask_ref[...] = jnp.dot(
        band[:16], jnp.where(one_hot, 1.0, 0.0).astype(BF16), preferred_element_type=F32
    )[:8]
    place = lax.broadcasted_iota(jnp.int32, (32, LANES), 0)
    base = jnp.where(place < 8, odd_base, jnp.where(place < 16, even_base, 8 + 2 * n))
    chosen = base + jnp.where(place < 16, place % 8, place % 2)
    select = jnp.where(
        lax.broadcasted_iota(jnp.int32, (32, LANES), 1) == chosen, 1.0, 0.0
    ).astype(BF16)
    by_block = nt_dot(select, band).astype(BF16)
    spread = (
        lax.broadcasted_iota(jnp.int32, (LANES, SLAB), 0)
        == lax.broadcasted_iota(jnp.int32, (LANES, SLAB), 1) // LANES
    )
    pair_ref[...] = jnp.dot(
        by_block, jnp.where(spread, 1.0, 0.0).astype(BF16), preferred_element_type=F32
    )

    fill_kernel(rows_ref, columns_ref, mask_ref, slice(0, SLAB), kernel_ref, sums_ref, None)


def regroup(flags, first, second):
    low = jnp.concatenate([first[:, :HALF], second[:, :HALF]], axis=1)
    high = jnp.concatenate([first[:, HALF:], second[:, HALF:]], axis=1)
    swap = flags[CORE] > 0
    return jnp.where(swap, high, low), jnp.where(swap, low, high)


def finish_messages(flags, sums, first, second, partial_ref, cross_ref, inner_ref):
    own, near, far = (jnp.sum(part, axis=0, keepdims=True) for part in sums)
    one = flags[CORE] > 0
    low = jnp.where(one, far, near)
    high = jnp.where(one, near, far)
    odd = jnp.concatenate([low[:, :HALF], high[:, :HALF]], axis=1)
    even = jnp.concatenate([low[:, HALF:], high[:, HALF:]], axis=1)
    partial_ref[...] = jnp.zeros_like(partial_ref)
    partial_ref[0:1, :] = own
    partial_ref[1:2, :] = odd
    partial_ref[2:3, :] = even
    a_even = flags[A_EVEN] > 0
    for ref, side, along, distant in (
        (cross_ref, odd, first, jnp.where(a_even, even, odd)),
        (inner_ref, even, second, jnp.where(a_even, odd, even)),
    ):
        ref[...] = jnp.zeros_like(ref)
        ref[0:1, :] = jnp.where(one, distant, own)
        ref[1:2, :] = side
        ref[2 : 2 + along.shape[0], :] = along


def stack_kernel(cross_ref, inner_ref, both_ref):
    both_ref[0:NOTE, :] = cross_ref[...]
    both_ref[NOTE : 2 * NOTE, :] = inner_ref[...]


def received(flags, mine_ref, theirs_ref):
    one = flags[CORE] > 0
    mine, theirs = mine_ref[...], theirs_ref[...]
    return jnp.where(one, theirs, mine), jnp.where(one, mine, theirs)


def turned(flags, rows):
    swapped = jnp.concatenate([rows[:, HALF:], rows[:, :HALF]], axis=1)
    return jnp.where(flags[CORE] > 0, swapped, rows)


def far_kernel(
    flags, rows_ref, columns_ref, mask_ref, own_kernel_ref, near_kernel_ref, before_ref,
    weight_ref, pair_ref, kernel_ref, partial_ref, cross_ref, inner_ref,
):
    def step(i, carry):
        own, near, far = carry
        blocks = block_kernel(
            rows_ref, columns_ref[...], mask_ref, i, slice(2 * SLAB, 3 * SLAB)
        )
        for j, block in enumerate(blocks):
            at = pl.ds(pl.multiple_of(i * QUARTER + j * LANES, LANES), LANES)
            kernel_ref[at, :] = block
            sums = lane_tiles(block) + before_ref[at, :]
            scale = weight_ref[at, 0:1] / jnp.sum(sums, axis=1, keepdims=True)
            own = own + sublane_tiles(own_kernel_ref[at, :] * scale)
            near = near + sublane_tiles(near_kernel_ref[at, :] * scale)
            far = far + sublane_tiles(block * scale)
        return own, near, far

    zero = jnp.zeros((8, SLAB), F32)
    sums = lax.fori_loop(0, 4, step, (zero, zero, zero))
    finish_messages(
        flags, sums, pair_ref[0:8, :], pair_ref[8:16, :], partial_ref, cross_ref, inner_ref
    )


def column_scales(flags, partial_ref, mine_ref, theirs_ref, weights):
    a_even = flags[A_EVEN] > 0
    close, distant = received(flags, mine_ref, theirs_ref)
    a, b = distant[0:1], distant[NOTE : NOTE + 1]
    own = partial_ref[0:1, :] + close[1:2] + close[NOTE + 1 : NOTE + 2]
    odd = partial_ref[1:2, :] + close[0:1] + jnp.where(a_even, b, a)
    even = partial_ref[2:3, :] + close[NOTE : NOTE + 1] + jnp.where(a_even, a, b)
    has_odd = flags[HAS_ODD] > 0
    own_weight, odd_weight, even_weight = (ref[...] for ref in weights)
    odd = jnp.where(has_odd, odd_weight / jnp.where(has_odd, odd, 1.0), 0.0)
    even = even_weight / even
    return own_weight / own, *regroup(flags, odd, even)


def sweep_kernel(
    flags, partial_in, mine_in, theirs_in, own_weight, odd_weight, even_weight, own_kernel_ref,
    near_kernel_ref, far_kernel_ref, weight_ref, row_ref, lane_ref, partial_ref, cross_ref,
    inner_ref, flat_ref,
):
    scales = column_scales(
        flags, partial_in, mine_in, theirs_in, (own_weight, odd_weight, even_weight)
    )
    kernels = (own_kernel_ref, near_kernel_ref, far_kernel_ref)

    def step(i, carry):
        at = pl.ds(pl.multiple_of(i * LANES, LANES), LANES)
        total = jnp.zeros((LANES, LANES), F32)
        for kernel_ref, scale in zip(kernels, scales, strict=True):
            total = total + lane_tiles(kernel_ref[at, :] * scale)
        row_scale = weight_ref[at, 0:1] / jnp.sum(total, axis=1, keepdims=True)
        row_ref[at, :] = jnp.broadcast_to(row_scale, (LANES, LANES))
        flat_ref[pl.ds(i, 1), :] = to_row(row_scale)
        return tuple(
            sums + sublane_tiles(kernel_ref[at, :] * row_scale)
            for kernel_ref, sums in zip(kernels, carry, strict=True)
        )

    zero = jnp.zeros((8, SLAB), F32)
    sums = lax.fori_loop(0, 8, step, (zero, zero, zero))
    for i in range(8):
        lane_ref[0:1, i * LANES : (i + 1) * LANES] = flat_ref[i : i + 1, :]
    flat = lane_ref[...]
    finish_messages(flags, sums, flat, flat, partial_ref, cross_ref, inner_ref)


def quarters_kernel(flags, own_ref, y_ref, pair_ref):
    y = flags[Y]
    odd_y = jnp.where(flags[FLIPPED] > 0, 1 - y, y)
    for ref, odd_at, even_at in ((own_ref, odd_y, y), (y_ref, 1 - odd_y, 1 - y)):
        for at, first in ((odd_at * QUARTER, 0), (HALF + even_at * QUARTER, QUARTER)):
            pair_ref[pl.ds(pl.multiple_of(at, QUARTER), QUARTER), :] = ref[first : first + QUARTER, :]


def transposed_kernel(
    flags, columns_ref, rows_ref, near_ref, far_ref, pair_ref, mine_in, theirs_in, odd_rows_ref,
    even_rows_ref, kernel_ref,
):
    own = columns_ref[pl.ds(pl.multiple_of(flags[NARROW] * QUARTER, QUARTER), QUARTER), :]
    odd_rows_ref[0:HALF, :] = near_ref[0:HALF, :]
    odd_rows_ref[HALF:SLAB, :] = far_ref[0:HALF, :]
    even_rows_ref[0:HALF, :] = near_ref[HALF:SLAB, :]
    even_rows_ref[HALF:SLAB, :] = far_ref[HALF:SLAB, :]
    n = flags[NARROW]
    close, _ = received(flags, mine_in, theirs_in)

    def pairs_of(first):
        found = close[first : first + 2]
        for i in range(1, 4):
            found = jnp.where(n == i, close[first + 2 * i : first + 2 * i + 2], found)
        return turned(flags, found)

    odd_pairs, even_pairs = pairs_of(2), pairs_of(NOTE + 2)
    for i, (rows, top, bottom) in enumerate(
        (
            (rows_ref, pair_ref[16:17, :], pair_ref[17:18, :]),
            (odd_rows_ref, odd_pairs[0:1], odd_pairs[1:2]),
            (even_rows_ref, even_pairs[0:1], even_pairs[1:2]),
        )
    ):
        values = jnp.exp(nt_dot(own, rows[...]) * SCALE)
        lanes = slice(i * SLAB, (i + 1) * SLAB)
        kernel_ref[0:LANES, lanes] = values[:LANES] * top
        kernel_ref[LANES:QUARTER, lanes] = values[LANES:] * bottom


def gradient_kernel(
    flags, partial_in, mine_in, theirs_in, own_weight, odd_weight, even_weight, row_ref, lane_ref,
    own_kernel_ref, near_kernel_ref, far_kernel_ref, own_columns_ref, near_columns_ref,
    far_columns_ref, rows_ref, odd_rows_ref, even_rows_ref, transposed_ref, treated_out,
    control_out,
):
    scales = column_scales(
        flags, partial_in, mine_in, theirs_in, (own_weight, odd_weight, even_weight)
    )
    close, _ = received(flags, mine_in, theirs_in)
    mine = pl.ds(pl.multiple_of(flags[Y] * QUARTER, QUARTER), QUARTER)
    row_scale = row_ref[mine, 0:1]
    mass = jnp.zeros((QUARTER, LANES), F32)
    pulled = jnp.zeros((QUARTER, WIDTH), F32)
    for kernel_ref, scale, columns_ref in zip(
        (own_kernel_ref, near_kernel_ref, far_kernel_ref),
        scales,
        (own_columns_ref, near_columns_ref, far_columns_ref),
        strict=True,
    ):
        transport = row_scale * kernel_ref[mine, :] * scale
        mass = mass + lane_tiles(transport)
        pulled = pulled + jnp.dot(
            transport.astype(BF16), columns_ref[...], preferred_element_type=F32
        )
    mass = jnp.sum(mass, axis=1, keepdims=True)
    treated_out[...] = mass * rows_ref[mine, :].astype(F32) - pulled

    n = flags[NARROW]

    def own_quarter(row):
        found = row[:, :QUARTER]
        for i in range(1, 4):
            found = jnp.where(n == i, row[:, i * QUARTER : (i + 1) * QUARTER], found)
        return found

    def upright(row):
        return jnp.concatenate([to_column(row[:, :LANES]), to_column(row[:, LANES:])], axis=0)

    own_scale = upright(own_quarter(scales[0]))
    own_mass = upright(own_quarter(own_weight[...]))
    pushed = jnp.zeros((QUARTER, WIDTH), F32)
    for i, (scale, rows) in enumerate(
        (
            (lane_ref[...], rows_ref),
            (turned(flags, close[2:3]), odd_rows_ref),
            (turned(flags, close[NOTE + 2 : NOTE + 3]), even_rows_ref),
        )
    ):
        transport = scale * transposed_ref[:, i * SLAB : (i + 1) * SLAB] * own_scale
        pushed = pushed + jnp.dot(transport.astype(BF16), rows[...], preferred_element_type=F32)
    at = pl.ds(pl.multiple_of(n * QUARTER, QUARTER), QUARTER)
    control_out[...] = own_mass * own_columns_ref[at, :].astype(F32) - pushed


VMEM = pl.BlockSpec(memory_space=pltpu.VMEM)
HBM = pl.BlockSpec(memory_space=pltpu.HBM)
SMEM = pl.BlockSpec(memory_space=pltpu.SMEM)


def call(body, specs, outs, operands, scratch=(), limit=16, out_specs=None):
    return pl.pallas_call(
        body,
        out_shape=tuple(jax.ShapeDtypeStruct(shape, dtype) for shape, dtype in outs),
        in_specs=specs,
        out_specs=out_specs or tuple(VMEM for _ in outs),
        scratch_shapes=list(scratch),
        compiler_params=pltpu.CompilerParams(vmem_limit_bytes=limit << 20),
    )(*operands)


MESSAGES = [((NOTE, SLAB), F32), ((NOTE, SLAB), F32)]


def trade(messages):
    cross = exchange(messages[0], (1, 2), True)
    inner = exchange(messages[1], (1, 2), False)
    (mine,) = call(stack_kernel, [VMEM] * 2, [((2 * NOTE, SLAB), F32)], [cross, inner])
    return mine, narrow_swap(mine, SWAP_CORE)


def step(treated, control, treated_weight, control_weight, band):
    wide_index = lax.axis_index("wide")
    n = lax.axis_index("narrow")
    wide_count = lax.axis_size("wide")
    odd = wide_index % 2
    toward_odd = wide_index + 2 * odd - 1
    toward_even = wide_index + 1 - 2 * odd
    values = (
        n,
        n % 2,
        n // 2,
        odd,
        jnp.logical_xor(wide_index % 4 >= 2, odd == 1).astype(jnp.int32),
        ((toward_odd >= 0) & (toward_odd < wide_count)).astype(jnp.int32),
        (jnp.minimum(wide_index, toward_odd) == wide_count // 2 - 1).astype(jnp.int32),
    )
    place = lax.iota(jnp.int32, 8)
    flags = jnp.zeros((8,), jnp.int32)
    for i, value in enumerate(values):
        flags = jnp.where(place == i, value, flags)
    weights = [
        lax.dynamic_slice_in_dim(control_weight, jnp.maximum(at, 0) * SLAB, SLAB).reshape(1, SLAB)
        for at in (wide_index, toward_odd, toward_even)
    ]

    treated, control, own_weight, own_band = (
        pltpu.with_memory_space_constraint(x, pltpu.HBM)
        for x in (treated, control, treated_weight.reshape(2, LANES), band)
    )
    letter, message = call(
        pack_kernel,
        [SMEM] + [HBM] * 4,
        [((LETTER, WIDTH), BF16), ((MESSAGE, WIDTH), BF16)],
        [flags, treated, control, own_weight, own_band],
        [
            pltpu.VMEM((QUARTER, WIDTH), BF16),
            pltpu.VMEM((2, LANES), F32),
            pltpu.VMEM((2, 24), jnp.int32),
            pltpu.VMEM((INFO, WIDTH), F32),
            pltpu.SemaphoreType.DMA((4,)),
        ],
    )
    odd_letter = exchange(letter, (1, 1), True)
    even_letter = exchange(letter, (1, 1), False)
    control, *weights = lax.optimization_barrier((control, *weights))
    (own_columns,) = call(
        columns_kernel,
        [HBM],
        [((SLAB, WIDTH), BF16)],
        [pltpu.with_memory_space_constraint(control, pltpu.HBM)],
        [pltpu.VMEM((SLAB, WIDTH), BF16), pltpu.SemaphoreType.DMA((4,))],
    )

    message_y = narrow_swap(message, SWAP_Y)
    (joined,) = call(
        join_kernel, [SMEM] + [VMEM] * 2, [((JOINED, WIDTH), BF16)], [flags, message, message_y]
    )
    joined_far = narrow_swap(joined, SWAP_CORE)

    rows, own_kernel, sums, mask, weight, pairs = call(
        prepare_kernel,
        [SMEM] + [VMEM] * 3,
        [
            ((SLAB, WIDTH), BF16),
            ((SLAB, SLAB), F32),
            ((SLAB, LANES), F32),
            ((8, 3 * SLAB), F32),
            ((SLAB, LANES), F32),
            ((32, SLAB), F32),
        ],
        [flags, joined, joined_far, own_columns],
        [pltpu.VMEM((LANES, LANES), F32)],
    )
    odd_letter, even_letter, _ = lax.optimization_barrier((odd_letter, even_letter, sums))
    near_columns, quarters = call(
        open_kernel,
        [VMEM] * 2,
        [((SLAB, WIDTH), BF16), ((HALF, WIDTH), BF16)],
        [odd_letter, even_letter],
    )
    far_columns = narrow_swap(near_columns, SWAP_CORE)
    quarters_y = narrow_swap(quarters, SWAP_Y)
    near_values, sums = call(
        near_kernel,
        [VMEM] * 4,
        [((SLAB, SLAB), F32), ((SLAB, LANES), F32)],
        [rows, near_columns, mask, sums],
    )
    far_values, partial, *messages = call(
        far_kernel,
        [SMEM] + [VMEM] * 8,
        [((SLAB, SLAB), F32), ((8, SLAB), F32), *MESSAGES],
        [flags, rows, far_columns, mask, own_kernel, near_values, sums, weight, pairs],
    )
    first = trade(messages)

    row_scale, lane_scale, partial, *messages = call(
        sweep_kernel,
        [SMEM] + [VMEM] * 10,
        [((SLAB, LANES), F32), ((1, SLAB), F32), ((8, SLAB), F32), *MESSAGES],
        [flags, partial, *first, *weights, own_kernel, near_values, far_values, weight],
        [pltpu.VMEM((8, LANES), F32)],
    )
    (near_rows,) = call(
        quarters_kernel,
        [SMEM] + [VMEM] * 2,
        [((SLAB, WIDTH), BF16)],
        [flags, quarters, quarters_y],
    )
    second = trade(messages)
    far_rows = narrow_swap(near_rows, SWAP_CORE)

    odd_rows, even_rows, transposed = call(
        transposed_kernel,
        [SMEM] + [VMEM] * 7,
        [((SLAB, WIDTH), BF16), ((SLAB, WIDTH), BF16), ((QUARTER, 3 * SLAB), F32)],
        [flags, own_columns, rows, near_rows, far_rows, pairs, *first],
    )

    return call(
        gradient_kernel,
        [SMEM] + [VMEM] * 18,
        [((QUARTER, WIDTH), F32)] * 2,
        [
            flags, partial, *second, *weights, row_scale, lane_scale, own_kernel, near_values,
            far_values, own_columns, near_columns, far_columns, rows, odd_rows, even_rows,
            transposed,
        ],
    )


def solution(mesh):
    return jax.shard_map(
        step,
        mesh=mesh,
        in_specs=(
            P(("wide", "narrow"), None),
            P("wide", None),
            P(("wide", "narrow")),
            P(),
            P(("wide", "narrow"), None),
        ),
        out_specs=(P(("wide", "narrow"), None), P(("wide", "narrow"), None)),
        check_vma=False,
    )
```

```python
import jax
import jax.numpy as jnp
from jax import lax
from jax.experimental import pallas as pl
from jax.experimental.pallas import tpu as pltpu
from jax.sharding import PartitionSpec as P


SMOOTHING_TEMP = 0.05
EPSILON = 1e-06

SWAP_Y = [(0, 2), (2, 0), (1, 3), (3, 1)]
SWAP_CORE = [(0, 1), (1, 0), (2, 3), (3, 2)]

LANES = 128
QUARTER = 256
HALF = 512
SLAB = 1024
WIDTH = 512
SCALE = 1.0 / (WIDTH * SMOOTHING_TEMP)

F32 = jnp.float32
BF16 = jnp.bfloat16

INFO = 16
MESSAGE = QUARTER + INFO
JOINED = 2 * MESSAGE
LETTER = HALF + QUARTER
NOTE = 16

NARROW, CORE, Y, ODD, A_EVEN, HAS_ODD, FLIPPED = range(7)


def narrow_swap(block, pairs):
    return lax.ppermute(block, "narrow", pairs)


def exchange(block, hops, crossing):
    count = lax.axis_size("wide")
    narrow = lax.axis_size("narrow")
    pairs = []
    for n in range(narrow):
        far = hops[n % 2]
        for base in range(far if crossing else 0, count, 2 * far):
            for low in range(base, base + far):
                high = low + far
                if high < count:
                    other = n ^ 2 if low < count // 2 <= high else n
                    one, two = low * narrow + n, high * narrow + other
                    pairs += [(one, two), (two, one)]
    return lax.ppermute(block, ("wide", "narrow"), pairs)


def normalize(features):
    values = features.astype(F32)
    total = jnp.sum(values * values, axis=1, keepdims=True)
    return (values * lax.rsqrt(total * (1.0 / WIDTH) + EPSILON)).astype(BF16)


def nt_dot(a, b):
    return lax.dot_general(a, b, (((1,), (1,)), ((), ())), preferred_element_type=F32)


def identity():
    return lax.broadcasted_iota(jnp.int32, (LANES, LANES), 0) == lax.broadcasted_iota(
        jnp.int32, (LANES, LANES), 1
    )


def to_column(row):
    return jnp.sum(jnp.where(identity(), row, 0.0), axis=1, keepdims=True)


def to_row(column):
    return jnp.sum(jnp.where(identity(), column, 0.0), axis=0, keepdims=True)


def lane_tiles(values):
    total = values[:, :LANES]
    for i in range(1, values.shape[1] // LANES):
        total = total + values[:, i * LANES : (i + 1) * LANES]
    return total


def sublane_tiles(values):
    rows, columns = values.shape
    return jnp.sum(values.reshape(rows // 8, 8, columns), axis=0)


def block_kernel(rows_ref, columns, mask_ref, i, lanes):
    inner = nt_dot(rows_ref[pl.ds(pl.multiple_of(i * QUARTER, QUARTER), QUARTER), :], columns)
    values = jnp.exp(inner * SCALE)
    top = values[:LANES] * mask_ref[pl.ds(2 * i, 1), lanes]
    bottom = values[LANES:] * mask_ref[pl.ds(2 * i + 1, 1), lanes]
    return top, bottom


def fill_kernel(rows_ref, columns_ref, mask_ref, lanes, kernel_ref, sums_ref, before_ref):
    def step(i, carry):
        blocks = block_kernel(rows_ref, columns_ref[...], mask_ref, i, lanes)
        for j, block in enumerate(blocks):
            at = pl.ds(pl.multiple_of(i * QUARTER + j * LANES, LANES), LANES)
            kernel_ref[at, :] = block
            sums = lane_tiles(block)
            if before_ref is not None:
                sums = sums + before_ref[at, :]
            sums_ref[at, :] = sums
        return carry

    lax.fori_loop(0, 4, step, 0, unroll=True)


def pack_kernel(
    flags, treated_any, control_any, weight_any, band_any, letter_ref, message_ref, treated_ref,
    weight_ref, band_ref, info_ref, sems,
):
    half = pl.ds(pl.multiple_of(flags[CORE] * HALF, HALF), HALF)
    copies = [
        pltpu.make_async_copy(source, target, sems.at[i])
        for i, (source, target) in enumerate(
            (
                (treated_any, treated_ref),
                (weight_any, weight_ref),
                (band_any, band_ref),
                (control_any.at[half, :], letter_ref.at[0:HALF, :]),
            )
        )
    ]
    for copy in copies:
        copy.start()
    info_ref[...] = jnp.zeros_like(info_ref)
    for copy in copies[:3]:
        copy.wait()
    rows = normalize(treated_ref[...])
    weight = weight_ref[...]
    for i in range(3):
        part = weight.astype(BF16).astype(F32)
        info_ref[0:2, i * LANES : (i + 1) * LANES] = part
        weight = weight - part
    info_ref[0:2, 3 * LANES : 3 * LANES + 24] = band_ref[...].astype(F32)
    info = info_ref[...].astype(BF16)
    message_ref[0:QUARTER, :] = rows
    message_ref[QUARTER:MESSAGE, :] = info
    letter_ref[HALF:LETTER, :] = rows
    copies[3].wait()


def join_kernel(flags, own_ref, y_ref, joined_ref):
    for ref, y in ((own_ref, flags[Y]), (y_ref, 1 - flags[Y])):
        joined_ref[pl.ds(pl.multiple_of(y * QUARTER, QUARTER), QUARTER), :] = ref[0:QUARTER, :]
        joined_ref[pl.ds(pl.multiple_of(HALF + y * INFO, INFO), INFO), :] = ref[QUARTER:MESSAGE, :]


def columns_kernel(control_any, columns_ref, control_ref, sems):
    copies = [
        pltpu.make_async_copy(
            control_any.at[i * QUARTER : (i + 1) * QUARTER, :],
            control_ref.at[i * QUARTER : (i + 1) * QUARTER, :],
            sems.at[i],
        )
        for i in range(4)
    ]
    for copy in copies:
        copy.start()
    for i, copy in enumerate(copies):
        copy.wait()
        at = slice(i * QUARTER, (i + 1) * QUARTER)
        columns_ref[at, :] = normalize(control_ref[at, :])


def open_kernel(odd_ref, even_ref, columns_ref, quarters_ref):
    columns_ref[0:HALF, :] = normalize(odd_ref[0:HALF, :])
    columns_ref[HALF:SLAB, :] = normalize(even_ref[0:HALF, :])
    quarters_ref[0:QUARTER, :] = odd_ref[HALF:LETTER, :]
    quarters_ref[QUARTER:HALF, :] = even_ref[HALF:LETTER, :]


def near_kernel(rows_ref, columns_ref, mask_ref, before_ref, kernel_ref, sums_ref):
    fill_kernel(
        rows_ref, columns_ref, mask_ref, slice(SLAB, 2 * SLAB), kernel_ref, sums_ref, before_ref
    )


def prepare_kernel(
    flags, joined_ref, far_ref, columns_ref, rows_ref, kernel_ref, sums_ref, mask_ref, weight_ref,
    pair_ref, band_ref,
):
    n, odd, core = flags[NARROW], flags[ODD], flags[CORE]
    rows_ref[0:HALF, :] = joined_ref[0:HALF, :]
    rows_ref[HALF:SLAB, :] = far_ref[0:HALF, :]

    band_ref[...] = jnp.zeros_like(band_ref)
    for i, (source, first) in enumerate(
        ((joined_ref, HALF), (joined_ref, HALF + INFO), (far_ref, HALF), (far_ref, HALF + INFO))
    ):
        info = source[first : first + INFO, :].astype(F32)
        band_ref[2 * i : 2 * i + 2, :] = info[0:2, 3 * LANES :]
        weights = info[:, :LANES] + info[:, LANES : 2 * LANES] + info[:, 2 * LANES : 3 * LANES]
        for j in range(2):
            at = slice((2 * i + j) * LANES, (2 * i + j + 1) * LANES)
            weight_ref[at, :] = jnp.broadcast_to(to_column(weights[j : j + 1]), (LANES, LANES))
    band = band_ref[...].astype(BF16)
    odd_base = odd * 16
    even_base = 16 - odd * 16
    lane = lax.broadcasted_iota(jnp.int32, (1, 3 * SLAB), 1)
    segment = lane // SLAB
    side = jnp.where(lane % SLAB < HALF, odd_base, even_base)
    side = side + 4 * jnp.where(segment == 1, core, 1 - core) + (lane % HALF) // LANES
    wanted = jnp.where(segment == 0, 8 + lane // LANES, side)
    one_hot = lax.broadcasted_iota(jnp.int32, (LANES, 3 * SLAB), 0) == wanted
    mask_ref[...] = jnp.dot(
        band[:16], jnp.where(one_hot, 1.0, 0.0).astype(BF16), preferred_element_type=F32
    )[:8]
    place = lax.broadcasted_iota(jnp.int32, (32, LANES), 0)
    base = jnp.where(place < 8, odd_base, jnp.where(place < 16, even_base, 8 + 2 * n))
    chosen = base + jnp.where(place < 16, place % 8, place % 2)
    select = jnp.where(
        lax.broadcasted_iota(jnp.int32, (32, LANES), 1) == chosen, 1.0, 0.0
    ).astype(BF16)
    by_block = nt_dot(select, band).astype(BF16)
    spread = (
        lax.broadcasted_iota(jnp.int32, (LANES, SLAB), 0)
        == lax.broadcasted_iota(jnp.int32, (LANES, SLAB), 1) // LANES
    )
    pair_ref[...] = jnp.dot(
        by_block, jnp.where(spread, 1.0, 0.0).astype(BF16), preferred_element_type=F32
    )

    fill_kernel(rows_ref, columns_ref, mask_ref, slice(0, SLAB), kernel_ref, sums_ref, None)


def regroup(flags, first, second):
    low = jnp.concatenate([first[:, :HALF], second[:, :HALF]], axis=1)
    high = jnp.concatenate([first[:, HALF:], second[:, HALF:]], axis=1)
    swap = flags[CORE] > 0
    return jnp.where(swap, high, low), jnp.where(swap, low, high)


def finish_messages(flags, sums, first, second, partial_ref, cross_ref, inner_ref):
    own, near, far = (jnp.sum(part, axis=0, keepdims=True) for part in sums)
    one = flags[CORE] > 0
    low = jnp.where(one, far, near)
    high = jnp.where(one, near, far)
    odd = jnp.concatenate([low[:, :HALF], high[:, :HALF]], axis=1)
    even = jnp.concatenate([low[:, HALF:], high[:, HALF:]], axis=1)
    partial_ref[...] = jnp.zeros_like(partial_ref)
    partial_ref[0:1, :] = own
    partial_ref[1:2, :] = odd
    partial_ref[2:3, :] = even
    a_even = flags[A_EVEN] > 0
    for ref, side, along, distant in (
        (cross_ref, odd, first, jnp.where(a_even, even, odd)),
        (inner_ref, even, second, jnp.where(a_even, odd, even)),
    ):
        ref[...] = jnp.zeros_like(ref)
        ref[0:1, :] = jnp.where(one, distant, own)
        ref[1:2, :] = side
        ref[2 : 2 + along.shape[0], :] = along


def stack_kernel(cross_ref, inner_ref, both_ref):
    both_ref[0:NOTE, :] = cross_ref[...]
    both_ref[NOTE : 2 * NOTE, :] = inner_ref[...]


def received(flags, mine_ref, theirs_ref):
    one = flags[CORE] > 0
    mine, theirs = mine_ref[...], theirs_ref[...]
    return jnp.where(one, theirs, mine), jnp.where(one, mine, theirs)


def turned(flags, rows):
    swapped = jnp.concatenate([rows[:, HALF:], rows[:, :HALF]], axis=1)
    return jnp.where(flags[CORE] > 0, swapped, rows)


def far_kernel(
    flags, rows_ref, columns_ref, mask_ref, own_kernel_ref, near_kernel_ref, before_ref,
    weight_ref, pair_ref, kernel_ref, partial_ref, cross_ref, inner_ref,
):
    def step(i, carry):
        own, near, far = carry
        blocks = block_kernel(
            rows_ref, columns_ref[...], mask_ref, i, slice(2 * SLAB, 3 * SLAB)
        )
        for j, block in enumerate(blocks):
            at = pl.ds(pl.multiple_of(i * QUARTER + j * LANES, LANES), LANES)
            kernel_ref[at, :] = block
            sums = lane_tiles(block) + before_ref[at, :]
            scale = weight_ref[at, 0:1] / jnp.sum(sums, axis=1, keepdims=True)
            own = own + sublane_tiles(own_kernel_ref[at, :] * scale)
            near = near + sublane_tiles(near_kernel_ref[at, :] * scale)
            far = far + sublane_tiles(block * scale)
        return own, near, far

    zero = jnp.zeros((8, SLAB), F32)
    sums = lax.fori_loop(0, 4, step, (zero, zero, zero), unroll=True)
    finish_messages(
        flags, sums, pair_ref[0:8, :], pair_ref[8:16, :], partial_ref, cross_ref, inner_ref
    )


def column_scales(flags, partial_ref, mine_ref, theirs_ref, weights):
    a_even = flags[A_EVEN] > 0
    close, distant = received(flags, mine_ref, theirs_ref)
    a, b = distant[0:1], distant[NOTE : NOTE + 1]
    own = partial_ref[0:1, :] + close[1:2] + close[NOTE + 1 : NOTE + 2]
    odd = partial_ref[1:2, :] + close[0:1] + jnp.where(a_even, b, a)
    even = partial_ref[2:3, :] + close[NOTE : NOTE + 1] + jnp.where(a_even, a, b)
    has_odd = flags[HAS_ODD] > 0
    own_weight, odd_weight, even_weight = (ref[...] for ref in weights)
    odd = jnp.where(has_odd, odd_weight / jnp.where(has_odd, odd, 1.0), 0.0)
    even = even_weight / even
    return own_weight / own, *regroup(flags, odd, even)


def sweep_kernel(
    flags, partial_in, mine_in, theirs_in, own_weight, odd_weight, even_weight, own_kernel_ref,
    near_kernel_ref, far_kernel_ref, weight_ref, row_ref, lane_ref, partial_ref, cross_ref,
    inner_ref, flat_ref,
):
    scales = column_scales(
        flags, partial_in, mine_in, theirs_in, (own_weight, odd_weight, even_weight)
    )
    kernels = (own_kernel_ref, near_kernel_ref, far_kernel_ref)

    def step(i, carry):
        at = pl.ds(pl.multiple_of(i * LANES, LANES), LANES)
        total = jnp.zeros((LANES, LANES), F32)
        for kernel_ref, scale in zip(kernels, scales, strict=True):
            total = total + lane_tiles(kernel_ref[at, :] * scale)
        row_scale = weight_ref[at, 0:1] / jnp.sum(total, axis=1, keepdims=True)
        row_ref[at, :] = jnp.broadcast_to(row_scale, (LANES, LANES))
        flat_ref[pl.ds(i, 1), :] = to_row(row_scale)
        return tuple(
            sums + sublane_tiles(kernel_ref[at, :] * row_scale)
            for kernel_ref, sums in zip(kernels, carry, strict=True)
        )

    zero = jnp.zeros((8, SLAB), F32)
    sums = lax.fori_loop(0, 8, step, (zero, zero, zero), unroll=True)
    for i in range(8):
        lane_ref[0:1, i * LANES : (i + 1) * LANES] = flat_ref[i : i + 1, :]
    flat = lane_ref[...]
    finish_messages(flags, sums, flat, flat, partial_ref, cross_ref, inner_ref)


def quarters_kernel(flags, own_ref, y_ref, pair_ref):
    y = flags[Y]
    odd_y = jnp.where(flags[FLIPPED] > 0, 1 - y, y)
    for ref, odd_at, even_at in ((own_ref, odd_y, y), (y_ref, 1 - odd_y, 1 - y)):
        for at, first in ((odd_at * QUARTER, 0), (HALF + even_at * QUARTER, QUARTER)):
            pair_ref[pl.ds(pl.multiple_of(at, QUARTER), QUARTER), :] = ref[first : first + QUARTER, :]


def own_control(flags, columns_ref):
    return columns_ref[pl.ds(pl.multiple_of(flags[NARROW] * QUARTER, QUARTER), QUARTER), :]


def own_transposed_kernel(flags, columns_ref, rows_ref, pair_ref, kernel_ref):
    values = jnp.exp(nt_dot(own_control(flags, columns_ref), rows_ref[...]) * SCALE)
    kernel_ref[0:LANES, :] = values[:LANES] * pair_ref[16:17, :]
    kernel_ref[LANES:QUARTER, :] = values[LANES:] * pair_ref[17:18, :]


def push_kernel(lane_ref, kernel_ref, rows_ref, pushed_ref):
    pushed_ref[...] = jnp.dot(
        (lane_ref[...] * kernel_ref[...]).astype(BF16),
        rows_ref[...],
        preferred_element_type=F32,
    )


def transposed_kernel(
    flags, columns_ref, near_ref, far_ref, mine_in, theirs_in, odd_rows_ref, even_rows_ref,
    kernel_ref,
):
    own = own_control(flags, columns_ref)
    odd_rows_ref[0:HALF, :] = near_ref[0:HALF, :]
    odd_rows_ref[HALF:SLAB, :] = far_ref[0:HALF, :]
    even_rows_ref[0:HALF, :] = near_ref[HALF:SLAB, :]
    even_rows_ref[HALF:SLAB, :] = far_ref[HALF:SLAB, :]
    n = flags[NARROW]
    close, _ = received(flags, mine_in, theirs_in)
    for i, (rows_ref, first) in enumerate(((odd_rows_ref, 2), (even_rows_ref, NOTE + 2))):
        found = close[first : first + 2]
        for j in range(1, 4):
            found = jnp.where(n == j, close[first + 2 * j : first + 2 * j + 2], found)
        found = turned(flags, found)
        values = jnp.exp(nt_dot(own, rows_ref[...]) * SCALE)
        lanes = slice(i * SLAB, (i + 1) * SLAB)
        kernel_ref[0:LANES, lanes] = values[:LANES] * found[0:1]
        kernel_ref[LANES:QUARTER, lanes] = values[LANES:] * found[1:2]


def gradient_kernel(
    flags, partial_in, mine_in, theirs_in, own_weight, odd_weight, even_weight, row_ref,
    own_kernel_ref, near_kernel_ref, far_kernel_ref, own_columns_ref, near_columns_ref,
    far_columns_ref, rows_ref, pushed_ref, odd_rows_ref, even_rows_ref, transposed_ref,
    treated_any, control_any, treated_out, control_out, sems,
):
    scales = column_scales(
        flags, partial_in, mine_in, theirs_in, (own_weight, odd_weight, even_weight)
    )
    close, _ = received(flags, mine_in, theirs_in)
    mine = pl.ds(pl.multiple_of(flags[Y] * QUARTER, QUARTER), QUARTER)
    row_scale = row_ref[mine, 0:1]
    mass = jnp.zeros((QUARTER, LANES), F32)
    pulled = jnp.zeros((QUARTER, WIDTH), F32)
    for kernel_ref, scale, columns_ref in zip(
        (own_kernel_ref, near_kernel_ref, far_kernel_ref),
        scales,
        (own_columns_ref, near_columns_ref, far_columns_ref),
        strict=True,
    ):
        transport = row_scale * kernel_ref[mine, :] * scale
        mass = mass + lane_tiles(transport)
        pulled = pulled + jnp.dot(
            transport.astype(BF16), columns_ref[...], preferred_element_type=F32
        )
    mass = jnp.sum(mass, axis=1, keepdims=True)
    treated_out[...] = mass * rows_ref[mine, :].astype(F32) - pulled
    treated_copy = pltpu.make_async_copy(treated_out, treated_any, sems.at[0])
    treated_copy.start()

    n = flags[NARROW]

    def own_quarter(row):
        found = row[:, :QUARTER]
        for i in range(1, 4):
            found = jnp.where(n == i, row[:, i * QUARTER : (i + 1) * QUARTER], found)
        return found

    def upright(row):
        return jnp.concatenate([to_column(row[:, :LANES]), to_column(row[:, LANES:])], axis=0)

    own_scale = upright(own_quarter(scales[0]))
    own_mass = upright(own_quarter(own_weight[...]))
    pushed = pushed_ref[...]
    for i, (row, rows) in enumerate(((2, odd_rows_ref), (NOTE + 2, even_rows_ref))):
        scale = turned(flags, close[row : row + 1])
        transport = (scale * transposed_ref[:, i * SLAB : (i + 1) * SLAB]).astype(BF16)
        pushed = pushed + jnp.dot(transport, rows[...], preferred_element_type=F32)
    at = pl.ds(pl.multiple_of(n * QUARTER, QUARTER), QUARTER)
    control_out[...] = own_mass * own_columns_ref[at, :].astype(F32) - own_scale * pushed
    control_copy = pltpu.make_async_copy(control_out, control_any, sems.at[1])
    control_copy.start()
    treated_copy.wait()
    control_copy.wait()


VMEM = pl.BlockSpec(memory_space=pltpu.VMEM)
HBM = pl.BlockSpec(memory_space=pltpu.HBM)
SMEM = pl.BlockSpec(memory_space=pltpu.SMEM)


def call(body, specs, outs, operands, scratch=(), limit=16, out_specs=None):
    return pl.pallas_call(
        body,
        out_shape=tuple(jax.ShapeDtypeStruct(shape, dtype) for shape, dtype in outs),
        in_specs=specs,
        out_specs=out_specs or tuple(VMEM for _ in outs),
        scratch_shapes=list(scratch),
        compiler_params=pltpu.CompilerParams(vmem_limit_bytes=limit << 20),
    )(*operands)


MESSAGES = [((NOTE, SLAB), F32), ((NOTE, SLAB), F32)]


def trade(messages):
    cross = exchange(messages[0], (1, 2), True)
    inner = exchange(messages[1], (1, 2), False)
    (mine,) = call(stack_kernel, [VMEM] * 2, [((2 * NOTE, SLAB), F32)], [cross, inner])
    return mine, narrow_swap(mine, SWAP_CORE)


def step(treated, control, treated_weight, control_weight, band):
    wide_index = lax.axis_index("wide")
    n = lax.axis_index("narrow")
    wide_count = lax.axis_size("wide")
    odd = wide_index % 2
    toward_odd = wide_index + 2 * odd - 1
    toward_even = wide_index + 1 - 2 * odd
    values = (
        n,
        n % 2,
        n // 2,
        odd,
        jnp.logical_xor(wide_index % 4 >= 2, odd == 1).astype(jnp.int32),
        ((toward_odd >= 0) & (toward_odd < wide_count)).astype(jnp.int32),
        (jnp.minimum(wide_index, toward_odd) == wide_count // 2 - 1).astype(jnp.int32),
    )
    place = lax.iota(jnp.int32, 8)
    flags = jnp.zeros((8,), jnp.int32)
    for i, value in enumerate(values):
        flags = jnp.where(place == i, value, flags)
    weights = [
        lax.dynamic_slice_in_dim(control_weight, jnp.maximum(at, 0) * SLAB, SLAB).reshape(1, SLAB)
        for at in (wide_index, toward_odd, toward_even)
    ]

    treated, control, own_weight, own_band = (
        pltpu.with_memory_space_constraint(x, pltpu.HBM)
        for x in (treated, control, treated_weight.reshape(2, LANES), band)
    )
    letter, message = call(
        pack_kernel,
        [SMEM] + [HBM] * 4,
        [((LETTER, WIDTH), BF16), ((MESSAGE, WIDTH), BF16)],
        [flags, treated, control, own_weight, own_band],
        [
            pltpu.VMEM((QUARTER, WIDTH), BF16),
            pltpu.VMEM((2, LANES), F32),
            pltpu.VMEM((2, 24), jnp.int32),
            pltpu.VMEM((INFO, WIDTH), F32),
            pltpu.SemaphoreType.DMA((4,)),
        ],
    )
    odd_letter = exchange(letter, (1, 1), True)
    even_letter = exchange(letter, (1, 1), False)
    control, *weights = lax.optimization_barrier((control, *weights))
    (own_columns,) = call(
        columns_kernel,
        [HBM],
        [((SLAB, WIDTH), BF16)],
        [pltpu.with_memory_space_constraint(control, pltpu.HBM)],
        [pltpu.VMEM((SLAB, WIDTH), BF16), pltpu.SemaphoreType.DMA((4,))],
    )

    message_y = narrow_swap(message, SWAP_Y)
    (joined,) = call(
        join_kernel, [SMEM] + [VMEM] * 2, [((JOINED, WIDTH), BF16)], [flags, message, message_y]
    )
    joined_far = narrow_swap(joined, SWAP_CORE)

    rows, own_kernel, sums, mask, weight, pairs = call(
        prepare_kernel,
        [SMEM] + [VMEM] * 3,
        [
            ((SLAB, WIDTH), BF16),
            ((SLAB, SLAB), F32),
            ((SLAB, LANES), F32),
            ((8, 3 * SLAB), F32),
            ((SLAB, LANES), F32),
            ((32, SLAB), F32),
        ],
        [flags, joined, joined_far, own_columns],
        [pltpu.VMEM((LANES, LANES), F32)],
    )
    (own_transposed,) = call(
        own_transposed_kernel,
        [SMEM] + [VMEM] * 3,
        [((QUARTER, SLAB), F32)],
        [flags, own_columns, rows, pairs],
    )
    odd_letter, even_letter, _, _ = lax.optimization_barrier(
        (odd_letter, even_letter, sums, own_transposed)
    )
    near_columns, quarters = call(
        open_kernel,
        [VMEM] * 2,
        [((SLAB, WIDTH), BF16), ((HALF, WIDTH), BF16)],
        [odd_letter, even_letter],
    )
    far_columns = narrow_swap(near_columns, SWAP_CORE)
    quarters_y = narrow_swap(quarters, SWAP_Y)
    near_values, sums = call(
        near_kernel,
        [VMEM] * 4,
        [((SLAB, SLAB), F32), ((SLAB, LANES), F32)],
        [rows, near_columns, mask, sums],
    )
    far_values, partial, *messages = call(
        far_kernel,
        [SMEM] + [VMEM] * 8,
        [((SLAB, SLAB), F32), ((8, SLAB), F32), *MESSAGES],
        [flags, rows, far_columns, mask, own_kernel, near_values, sums, weight, pairs],
    )
    first = trade(messages)

    row_scale, lane_scale, partial, *messages = call(
        sweep_kernel,
        [SMEM] + [VMEM] * 10,
        [((SLAB, LANES), F32), ((1, SLAB), F32), ((8, SLAB), F32), *MESSAGES],
        [flags, partial, *first, *weights, own_kernel, near_values, far_values, weight],
        [pltpu.VMEM((8, LANES), F32)],
    )
    (near_rows,) = call(
        quarters_kernel,
        [SMEM] + [VMEM] * 2,
        [((SLAB, WIDTH), BF16)],
        [flags, quarters, quarters_y],
    )
    second = trade(messages)
    far_rows = narrow_swap(near_rows, SWAP_CORE)

    (pushed,) = call(
        push_kernel,
        [VMEM] * 3,
        [((QUARTER, WIDTH), F32)],
        [lane_scale, own_transposed, rows],
    )
    odd_rows, even_rows, transposed = call(
        transposed_kernel,
        [SMEM] + [VMEM] * 5,
        [((SLAB, WIDTH), BF16), ((SLAB, WIDTH), BF16), ((QUARTER, 2 * SLAB), F32)],
        [flags, own_columns, near_rows, far_rows, *first],
    )

    return call(
        gradient_kernel,
        [SMEM] + [VMEM] * 18,
        [((QUARTER, WIDTH), F32)] * 2,
        [
            flags, partial, *second, *weights, row_scale, own_kernel, near_values, far_values,
            own_columns, near_columns, far_columns, rows, pushed, odd_rows, even_rows, transposed,
        ],
        [
            pltpu.VMEM((QUARTER, WIDTH), F32),
            pltpu.VMEM((QUARTER, WIDTH), F32),
            pltpu.SemaphoreType.DMA((2,)),
        ],
        out_specs=(HBM, HBM),
    )


def solution(mesh):
    return jax.shard_map(
        step,
        mesh=mesh,
        in_specs=(
            P(("wide", "narrow"), None),
            P("wide", None),
            P(("wide", "narrow")),
            P(),
            P(("wide", "narrow"), None),
        ),
        out_specs=(P(("wide", "narrow"), None), P(("wide", "narrow"), None)),
        check_vma=False,
    )
```

```python
import jax
import jax.numpy as jnp
from jax import lax
from jax.experimental import pallas as pl
from jax.experimental.pallas import tpu as pltpu
from jax.sharding import PartitionSpec as P


SMOOTHING_TEMP = 0.05
EPSILON = 1e-06

SWAP_Y = [(0, 2), (2, 0), (1, 3), (3, 1)]
SWAP_CORE = [(0, 1), (1, 0), (2, 3), (3, 2)]

LANES = 128
QUARTER = 256
HALF = 512
SLAB = 1024
WIDTH = 512
SCALE = 1.0 / (WIDTH * SMOOTHING_TEMP)

F32 = jnp.float32
BF16 = jnp.bfloat16

INFO = 16
MESSAGE = QUARTER + INFO
JOINED = 2 * MESSAGE
NOTE = 4

NARROW, CORE, Y, ODD, A_EVEN, HAS_ODD, FLIPPED = range(7)


def narrow_swap(block, pairs):
    return lax.ppermute(block, "narrow", pairs)


def exchange(block, hops, crossing):
    count = lax.axis_size("wide")
    narrow = lax.axis_size("narrow")
    pairs = []
    for n in range(narrow):
        far = hops[n % 2]
        for base in range(far if crossing else 0, count, 2 * far):
            for low in range(base, base + far):
                high = low + far
                if high < count:
                    other = n ^ 2 if low < count // 2 <= high else n
                    one, two = low * narrow + n, high * narrow + other
                    pairs += [(one, two), (two, one)]
    return lax.ppermute(block, ("wide", "narrow"), pairs)


def normalize(features):
    values = features.astype(F32)
    total = jnp.sum(values * values, axis=1, keepdims=True)
    return (values * lax.rsqrt(total * (1.0 / WIDTH) + EPSILON)).astype(BF16)


def nt_dot(a, b):
    return lax.dot_general(a, b, (((1,), (1,)), ((), ())), preferred_element_type=F32)


def identity():
    return lax.broadcasted_iota(jnp.int32, (LANES, LANES), 0) == lax.broadcasted_iota(
        jnp.int32, (LANES, LANES), 1
    )


def to_column(row):
    return jnp.sum(jnp.where(identity(), row, 0.0), axis=1, keepdims=True)


def to_row(column):
    return jnp.sum(jnp.where(identity(), column, 0.0), axis=0, keepdims=True)


def lane_tiles(values):
    total = values[:, :LANES]
    for i in range(1, values.shape[1] // LANES):
        total = total + values[:, i * LANES : (i + 1) * LANES]
    return total


def sublane_tiles(values):
    rows, columns = values.shape
    return jnp.sum(values.reshape(rows // 8, 8, columns), axis=0)


def block_kernel(rows_ref, columns, mask_ref, i, lanes):
    inner = nt_dot(rows_ref[pl.ds(pl.multiple_of(i * QUARTER, QUARTER), QUARTER), :], columns)
    values = jnp.exp(inner * SCALE)
    top = values[:LANES] * mask_ref[pl.ds(2 * i, 1), lanes]
    bottom = values[LANES:] * mask_ref[pl.ds(2 * i + 1, 1), lanes]
    return top, bottom


def fill_kernel(rows_ref, columns_ref, mask_ref, lanes, kernel_ref, sums_ref, before_ref):
    def step(i, carry):
        blocks = block_kernel(rows_ref, columns_ref[...], mask_ref, i, lanes)
        for j, block in enumerate(blocks):
            at = pl.ds(pl.multiple_of(i * QUARTER + j * LANES, LANES), LANES)
            kernel_ref[at, :] = block
            sums = lane_tiles(block)
            if before_ref is not None:
                sums = sums + before_ref[at, :]
            sums_ref[at, :] = sums
        return carry

    lax.fori_loop(0, 4, step, 0, unroll=True)


def pack_kernel(
    flags, treated_any, control_any, weight_any, band_any, letter_ref, message_ref, treated_ref,
    weight_ref, band_ref, info_ref, sems,
):
    half = pl.ds(pl.multiple_of(flags[CORE] * HALF, HALF), HALF)
    copies = [
        pltpu.make_async_copy(source, target, sems.at[i])
        for i, (source, target) in enumerate(
            (
                (treated_any, treated_ref),
                (weight_any, weight_ref),
                (band_any, band_ref),
                (control_any.at[half, :], letter_ref),
            )
        )
    ]
    for copy in copies:
        copy.start()
    info_ref[...] = jnp.zeros_like(info_ref)
    for copy in copies[:3]:
        copy.wait()
    rows = normalize(treated_ref[...])
    weight = weight_ref[...]
    for i in range(3):
        part = weight.astype(BF16).astype(F32)
        info_ref[0:2, i * LANES : (i + 1) * LANES] = part
        weight = weight - part
    info_ref[0:2, 3 * LANES : 3 * LANES + 24] = band_ref[...].astype(F32)
    info = info_ref[...].astype(BF16)
    message_ref[0:QUARTER, :] = rows
    message_ref[QUARTER:MESSAGE, :] = info
    copies[3].wait()


def join_kernel(flags, own_ref, y_ref, joined_ref):
    for ref, y in ((own_ref, flags[Y]), (y_ref, 1 - flags[Y])):
        joined_ref[pl.ds(pl.multiple_of(y * QUARTER, QUARTER), QUARTER), :] = ref[0:QUARTER, :]
        joined_ref[pl.ds(pl.multiple_of(HALF + y * INFO, INFO), INFO), :] = ref[QUARTER:MESSAGE, :]


def columns_kernel(control_any, columns_ref, control_ref, sems):
    copies = [
        pltpu.make_async_copy(
            control_any.at[i * QUARTER : (i + 1) * QUARTER, :],
            control_ref.at[i * QUARTER : (i + 1) * QUARTER, :],
            sems.at[i],
        )
        for i in range(4)
    ]
    for copy in copies:
        copy.start()
    for i, copy in enumerate(copies):
        copy.wait()
        at = slice(i * QUARTER, (i + 1) * QUARTER)
        columns_ref[at, :] = normalize(control_ref[at, :])


def open_kernel(odd_ref, even_ref, columns_ref):
    columns_ref[0:HALF, :] = normalize(odd_ref[...])
    columns_ref[HALF:SLAB, :] = normalize(even_ref[...])


def collect_kernel(odd_ref, even_ref, quarters_ref):
    quarters_ref[0:QUARTER, :] = odd_ref[0:QUARTER, :]
    quarters_ref[QUARTER:HALF, :] = even_ref[0:QUARTER, :]


def near_kernel(rows_ref, columns_ref, mask_ref, before_ref, kernel_ref, sums_ref):
    fill_kernel(
        rows_ref, columns_ref, mask_ref, slice(SLAB, 2 * SLAB), kernel_ref, sums_ref, before_ref
    )


def prepare_kernel(
    flags, joined_ref, far_ref, columns_ref, rows_ref, kernel_ref, sums_ref, mask_ref, weight_ref,
    pair_ref, compact_ref, band_ref,
):
    n, odd, core = flags[NARROW], flags[ODD], flags[CORE]
    rows_ref[0:HALF, :] = joined_ref[0:HALF, :]
    rows_ref[HALF:SLAB, :] = far_ref[0:HALF, :]

    band_ref[...] = jnp.zeros_like(band_ref)
    for i, (source, first) in enumerate(
        ((joined_ref, HALF), (joined_ref, HALF + INFO), (far_ref, HALF), (far_ref, HALF + INFO))
    ):
        info = source[first : first + INFO, :].astype(F32)
        band_ref[2 * i : 2 * i + 2, :] = info[0:2, 3 * LANES :]
        weights = info[:, :LANES] + info[:, LANES : 2 * LANES] + info[:, 2 * LANES : 3 * LANES]
        for j in range(2):
            at = slice((2 * i + j) * LANES, (2 * i + j + 1) * LANES)
            weight_ref[at, :] = jnp.broadcast_to(to_column(weights[j : j + 1]), (LANES, LANES))
    band = band_ref[...].astype(BF16)
    odd_base = odd * 16
    even_base = 16 - odd * 16
    lane = lax.broadcasted_iota(jnp.int32, (1, 3 * SLAB), 1)
    segment = lane // SLAB
    side = jnp.where(lane % SLAB < HALF, odd_base, even_base)
    side = side + 4 * jnp.where(segment == 1, core, 1 - core) + (lane % HALF) // LANES
    wanted = jnp.where(segment == 0, 8 + lane // LANES, side)
    one_hot = lax.broadcasted_iota(jnp.int32, (LANES, 3 * SLAB), 0) == wanted
    mask_ref[...] = jnp.dot(
        band[:16], jnp.where(one_hot, 1.0, 0.0).astype(BF16), preferred_element_type=F32
    )[:8]
    place = lax.broadcasted_iota(jnp.int32, (32, LANES), 0)
    base = jnp.where(place < 8, odd_base, jnp.where(place < 16, even_base, 8 + 2 * n))
    chosen = base + jnp.where(place < 16, place % 8, place % 2)
    select = jnp.where(
        lax.broadcasted_iota(jnp.int32, (32, LANES), 1) == chosen, 1.0, 0.0
    ).astype(BF16)
    by_block = nt_dot(select, band).astype(BF16)
    shift = (
        lax.broadcasted_iota(jnp.int32, (LANES, LANES), 0)
        == lax.broadcasted_iota(jnp.int32, (LANES, LANES), 1) % 8
    )
    flat = jnp.dot(
        by_block, jnp.where(shift, 1.0, 0.0).astype(BF16), preferred_element_type=F32
    )
    kept = lax.broadcasted_iota(jnp.int32, (8, LANES), 0) == (
        lax.broadcasted_iota(jnp.int32, (8, LANES), 1) // 8
    )
    compact_ref[...] = jnp.zeros_like(compact_ref)
    for i in range(2):
        row = jnp.where(kept, flat[8 * i : 8 * i + 8], 0.0)
        compact_ref[i : i + 1, 0:LANES] = jnp.sum(row, axis=0, keepdims=True)
    spread = (
        lax.broadcasted_iota(jnp.int32, (LANES, SLAB), 0)
        == lax.broadcasted_iota(jnp.int32, (LANES, SLAB), 1) // LANES
    )
    pair_ref[...] = jnp.dot(
        by_block, jnp.where(spread, 1.0, 0.0).astype(BF16), preferred_element_type=F32
    )[16:24]

    fill_kernel(rows_ref, columns_ref, mask_ref, slice(0, SLAB), kernel_ref, sums_ref, None)


def regroup(flags, first, second):
    low = jnp.concatenate([first[:, :HALF], second[:, :HALF]], axis=1)
    high = jnp.concatenate([first[:, HALF:], second[:, HALF:]], axis=1)
    swap = flags[CORE] > 0
    return jnp.where(swap, high, low), jnp.where(swap, low, high)


def finish_messages(flags, sums, first, second, partial_ref, cross_ref, inner_ref):
    own, near, far = (jnp.sum(part, axis=0, keepdims=True) for part in sums)
    one = flags[CORE] > 0
    low = jnp.where(one, far, near)
    high = jnp.where(one, near, far)
    odd = jnp.concatenate([low[:, :HALF], high[:, :HALF]], axis=1)
    even = jnp.concatenate([low[:, HALF:], high[:, HALF:]], axis=1)
    partial_ref[...] = jnp.zeros_like(partial_ref)
    partial_ref[0:1, :] = own
    partial_ref[1:2, :] = odd
    partial_ref[2:3, :] = even
    a_even = flags[A_EVEN] > 0
    for ref, side, along, distant in (
        (cross_ref, odd, first, jnp.where(a_even, even, odd)),
        (inner_ref, even, second, jnp.where(a_even, odd, even)),
    ):
        ref[...] = jnp.zeros_like(ref)
        ref[0:1, :] = jnp.where(one, distant, own)
        ref[1:2, :] = side
        ref[2 : 2 + along.shape[0], :] = along


def stack_kernel(cross_ref, inner_ref, both_ref):
    both_ref[0:NOTE, :] = cross_ref[...]
    both_ref[NOTE : 2 * NOTE, :] = inner_ref[...]


def received(flags, mine_ref, theirs_ref):
    one = flags[CORE] > 0
    mine, theirs = mine_ref[...], theirs_ref[...]
    return jnp.where(one, theirs, mine), jnp.where(one, mine, theirs)


def turned(flags, rows):
    swapped = jnp.concatenate([rows[:, HALF:], rows[:, :HALF]], axis=1)
    return jnp.where(flags[CORE] > 0, swapped, rows)


def far_kernel(
    flags, rows_ref, columns_ref, mask_ref, own_kernel_ref, near_kernel_ref, before_ref,
    weight_ref, compact_ref, kernel_ref, partial_ref, cross_ref, inner_ref,
):
    def step(i, carry):
        own, near, far = carry
        blocks = block_kernel(
            rows_ref, columns_ref[...], mask_ref, i, slice(2 * SLAB, 3 * SLAB)
        )
        for j, block in enumerate(blocks):
            at = pl.ds(pl.multiple_of(i * QUARTER + j * LANES, LANES), LANES)
            kernel_ref[at, :] = block
            sums = lane_tiles(block) + before_ref[at, :]
            scale = weight_ref[at, 0:1] / jnp.sum(sums, axis=1, keepdims=True)
            own = own + sublane_tiles(own_kernel_ref[at, :] * scale)
            near = near + sublane_tiles(near_kernel_ref[at, :] * scale)
            far = far + sublane_tiles(block * scale)
        return own, near, far

    zero = jnp.zeros((8, SLAB), F32)
    sums = lax.fori_loop(0, 4, step, (zero, zero, zero), unroll=True)
    finish_messages(
        flags, sums, compact_ref[0:1, :], compact_ref[1:2, :], partial_ref, cross_ref, inner_ref
    )


def column_scales(flags, partial_ref, mine_ref, theirs_ref, weights):
    a_even = flags[A_EVEN] > 0
    close, distant = received(flags, mine_ref, theirs_ref)
    a, b = distant[0:1], distant[NOTE : NOTE + 1]
    own = partial_ref[0:1, :] + close[1:2] + close[NOTE + 1 : NOTE + 2]
    odd = partial_ref[1:2, :] + close[0:1] + jnp.where(a_even, b, a)
    even = partial_ref[2:3, :] + close[NOTE : NOTE + 1] + jnp.where(a_even, a, b)
    has_odd = flags[HAS_ODD] > 0
    own_weight, odd_weight, even_weight = (ref[...] for ref in weights)
    odd = jnp.where(has_odd, odd_weight / jnp.where(has_odd, odd, 1.0), 0.0)
    even = even_weight / even
    return own_weight / own, *regroup(flags, odd, even)


def sweep_kernel(
    flags, partial_in, mine_in, theirs_in, own_weight, odd_weight, even_weight, own_kernel_ref,
    near_kernel_ref, far_kernel_ref, weight_ref, row_ref, lane_ref, partial_ref, cross_ref,
    inner_ref, flat_ref,
):
    scales = column_scales(
        flags, partial_in, mine_in, theirs_in, (own_weight, odd_weight, even_weight)
    )
    kernels = (own_kernel_ref, near_kernel_ref, far_kernel_ref)

    def step(i, carry):
        at = pl.ds(pl.multiple_of(i * LANES, LANES), LANES)
        total = jnp.zeros((LANES, LANES), F32)
        for kernel_ref, scale in zip(kernels, scales, strict=True):
            total = total + lane_tiles(kernel_ref[at, :] * scale)
        row_scale = weight_ref[at, 0:1] / jnp.sum(total, axis=1, keepdims=True)
        row_ref[at, :] = jnp.broadcast_to(row_scale, (LANES, LANES))
        flat_ref[pl.ds(i, 1), :] = to_row(row_scale)
        return tuple(
            sums + sublane_tiles(kernel_ref[at, :] * row_scale)
            for kernel_ref, sums in zip(kernels, carry, strict=True)
        )

    zero = jnp.zeros((8, SLAB), F32)
    sums = lax.fori_loop(0, 8, step, (zero, zero, zero), unroll=True)
    for i in range(8):
        lane_ref[0:1, i * LANES : (i + 1) * LANES] = flat_ref[i : i + 1, :]
    flat = lane_ref[...]
    finish_messages(flags, sums, flat, flat, partial_ref, cross_ref, inner_ref)


def quarters_kernel(flags, own_ref, y_ref, pair_ref):
    y = flags[Y]
    odd_y = jnp.where(flags[FLIPPED] > 0, 1 - y, y)
    for ref, odd_at, even_at in ((own_ref, odd_y, y), (y_ref, 1 - odd_y, 1 - y)):
        for at, first in ((odd_at * QUARTER, 0), (HALF + even_at * QUARTER, QUARTER)):
            pair_ref[pl.ds(pl.multiple_of(at, QUARTER), QUARTER), :] = ref[first : first + QUARTER, :]


def own_control(flags, columns_ref):
    return columns_ref[pl.ds(pl.multiple_of(flags[NARROW] * QUARTER, QUARTER), QUARTER), :]


def own_transposed_kernel(flags, columns_ref, rows_ref, pair_ref, kernel_ref):
    values = jnp.exp(nt_dot(own_control(flags, columns_ref), rows_ref[...]) * SCALE)
    kernel_ref[0:LANES, :] = values[:LANES] * pair_ref[0:1, :]
    kernel_ref[LANES:QUARTER, :] = values[LANES:] * pair_ref[1:2, :]


def push_kernel(lane_ref, kernel_ref, rows_ref, pushed_ref):
    pushed_ref[...] = jnp.dot(
        (lane_ref[...] * kernel_ref[...]).astype(BF16),
        rows_ref[...],
        preferred_element_type=F32,
    )


def transposed_kernel(
    flags, columns_ref, near_ref, far_ref, mine_in, theirs_in, odd_rows_ref, even_rows_ref,
    kernel_ref,
):
    own = own_control(flags, columns_ref)
    odd_rows_ref[0:HALF, :] = near_ref[0:HALF, :]
    odd_rows_ref[HALF:SLAB, :] = far_ref[0:HALF, :]
    even_rows_ref[0:HALF, :] = near_ref[HALF:SLAB, :]
    even_rows_ref[HALF:SLAB, :] = far_ref[HALF:SLAB, :]
    n = flags[NARROW]
    close, _ = received(flags, mine_in, theirs_in)
    lane = lax.broadcasted_iota(jnp.int32, (16, LANES), 1)
    wanted = (lane < 64) & (lane // 8 == 2 * n + lax.broadcasted_iota(jnp.int32, (16, LANES), 0))
    spread = (
        lax.broadcasted_iota(jnp.int32, (LANES, SLAB), 0) % 8
        == lax.broadcasted_iota(jnp.int32, (LANES, SLAB), 1) // LANES
    )
    spread = jnp.where(spread, 1.0, 0.0).astype(BF16)
    for i, (rows_ref, first) in enumerate(((odd_rows_ref, 2), (even_rows_ref, NOTE + 2))):
        compact = jnp.where(wanted, close[first : first + 1, :LANES], 0.0).astype(BF16)
        found = turned(flags, jnp.dot(compact, spread, preferred_element_type=F32))
        values = jnp.exp(nt_dot(own, rows_ref[...]) * SCALE)
        lanes = slice(i * SLAB, (i + 1) * SLAB)
        kernel_ref[0:LANES, lanes] = values[:LANES] * found[0:1]
        kernel_ref[LANES:QUARTER, lanes] = values[LANES:] * found[1:2]


def gradient_kernel(
    flags, partial_in, mine_in, theirs_in, own_weight, odd_weight, even_weight, row_ref,
    own_kernel_ref, near_kernel_ref, far_kernel_ref, own_columns_ref, near_columns_ref,
    far_columns_ref, rows_ref, pushed_ref, odd_rows_ref, even_rows_ref, transposed_ref,
    treated_any, control_any, treated_out, control_out, sems,
):
    scales = column_scales(
        flags, partial_in, mine_in, theirs_in, (own_weight, odd_weight, even_weight)
    )
    close, _ = received(flags, mine_in, theirs_in)
    pushed = pushed_ref[...]
    for i, (row, rows) in enumerate(((2, odd_rows_ref), (NOTE + 2, even_rows_ref))):
        scale = turned(flags, close[row : row + 1])
        transport = (scale * transposed_ref[:, i * SLAB : (i + 1) * SLAB]).astype(BF16)
        pushed = pushed + jnp.dot(transport, rows[...], preferred_element_type=F32)
    mine = pl.ds(pl.multiple_of(flags[Y] * QUARTER, QUARTER), QUARTER)
    row_scale = row_ref[mine, 0:1]
    mass = jnp.zeros((QUARTER, LANES), F32)
    pulled = jnp.zeros((QUARTER, WIDTH), F32)
    for kernel_ref, scale, columns_ref in zip(
        (own_kernel_ref, near_kernel_ref, far_kernel_ref),
        scales,
        (own_columns_ref, near_columns_ref, far_columns_ref),
        strict=True,
    ):
        transport = row_scale * kernel_ref[mine, :] * scale
        mass = mass + lane_tiles(transport)
        pulled = pulled + jnp.dot(
            transport.astype(BF16), columns_ref[...], preferred_element_type=F32
        )
    mass = jnp.sum(mass, axis=1, keepdims=True)
    treated_out[...] = mass * rows_ref[mine, :].astype(F32) - pulled
    treated_copy = pltpu.make_async_copy(treated_out, treated_any, sems.at[0])
    treated_copy.start()

    n = flags[NARROW]

    def own_quarter(row):
        found = row[:, :QUARTER]
        for i in range(1, 4):
            found = jnp.where(n == i, row[:, i * QUARTER : (i + 1) * QUARTER], found)
        return found

    def upright(row):
        return jnp.concatenate([to_column(row[:, :LANES]), to_column(row[:, LANES:])], axis=0)

    own_scale = upright(own_quarter(scales[0]))
    own_mass = upright(own_quarter(own_weight[...]))
    at = pl.ds(pl.multiple_of(n * QUARTER, QUARTER), QUARTER)
    control_out[...] = own_mass * own_columns_ref[at, :].astype(F32) - own_scale * pushed
    control_copy = pltpu.make_async_copy(control_out, control_any, sems.at[1])
    control_copy.start()
    treated_copy.wait()
    control_copy.wait()


VMEM = pl.BlockSpec(memory_space=pltpu.VMEM)
HBM = pl.BlockSpec(memory_space=pltpu.HBM)
SMEM = pl.BlockSpec(memory_space=pltpu.SMEM)


def call(body, specs, outs, operands, scratch=(), limit=16, out_specs=None):
    return pl.pallas_call(
        body,
        out_shape=tuple(jax.ShapeDtypeStruct(shape, dtype) for shape, dtype in outs),
        in_specs=specs,
        out_specs=out_specs or tuple(VMEM for _ in outs),
        scratch_shapes=list(scratch),
        compiler_params=pltpu.CompilerParams(vmem_limit_bytes=limit << 20),
    )(*operands)


MESSAGES = [((NOTE, SLAB), F32), ((NOTE, SLAB), F32)]


def trade(messages):
    cross = exchange(messages[0], (1, 2), True)
    inner = exchange(messages[1], (1, 2), False)
    (mine,) = call(stack_kernel, [VMEM] * 2, [((2 * NOTE, SLAB), F32)], [cross, inner])
    return mine, narrow_swap(mine, SWAP_CORE)


def step(treated, control, treated_weight, control_weight, band):
    wide_index = lax.axis_index("wide")
    n = lax.axis_index("narrow")
    wide_count = lax.axis_size("wide")
    odd = wide_index % 2
    toward_odd = wide_index + 2 * odd - 1
    toward_even = wide_index + 1 - 2 * odd
    values = (
        n,
        n % 2,
        n // 2,
        odd,
        jnp.logical_xor(wide_index % 4 >= 2, odd == 1).astype(jnp.int32),
        ((toward_odd >= 0) & (toward_odd < wide_count)).astype(jnp.int32),
        (jnp.minimum(wide_index, toward_odd) == wide_count // 2 - 1).astype(jnp.int32),
    )
    place = lax.iota(jnp.int32, 8)
    flags = jnp.zeros((8,), jnp.int32)
    for i, value in enumerate(values):
        flags = jnp.where(place == i, value, flags)
    weights = [
        lax.dynamic_slice_in_dim(control_weight, jnp.maximum(at, 0) * SLAB, SLAB).reshape(1, SLAB)
        for at in (wide_index, toward_odd, toward_even)
    ]

    treated, control, own_weight, own_band = (
        pltpu.with_memory_space_constraint(x, pltpu.HBM)
        for x in (treated, control, treated_weight.reshape(2, LANES), band)
    )
    letter, message = call(
        pack_kernel,
        [SMEM] + [HBM] * 4,
        [((HALF, WIDTH), BF16), ((MESSAGE, WIDTH), BF16)],
        [flags, treated, control, own_weight, own_band],
        [
            pltpu.VMEM((QUARTER, WIDTH), BF16),
            pltpu.VMEM((2, LANES), F32),
            pltpu.VMEM((2, 24), jnp.int32),
            pltpu.VMEM((INFO, WIDTH), F32),
            pltpu.SemaphoreType.DMA((4,)),
        ],
    )
    odd_letter = exchange(letter, (1, 1), True)
    even_letter = exchange(letter, (1, 1), False)
    control, *weights = lax.optimization_barrier((control, *weights))
    (own_columns,) = call(
        columns_kernel,
        [HBM],
        [((SLAB, WIDTH), BF16)],
        [pltpu.with_memory_space_constraint(control, pltpu.HBM)],
        [pltpu.VMEM((SLAB, WIDTH), BF16), pltpu.SemaphoreType.DMA((4,))],
    )

    odd_message = exchange(message, (1, 1), True)
    even_message = exchange(message, (1, 1), False)
    message_y = narrow_swap(message, SWAP_Y)
    (joined,) = call(
        join_kernel, [SMEM] + [VMEM] * 2, [((JOINED, WIDTH), BF16)], [flags, message, message_y]
    )
    joined_far = narrow_swap(joined, SWAP_CORE)

    rows, own_kernel, sums, mask, weight, pairs, compact = call(
        prepare_kernel,
        [SMEM] + [VMEM] * 3,
        [
            ((SLAB, WIDTH), BF16),
            ((SLAB, SLAB), F32),
            ((SLAB, LANES), F32),
            ((8, 3 * SLAB), F32),
            ((SLAB, LANES), F32),
            ((8, SLAB), F32),
            ((8, SLAB), F32),
        ],
        [flags, joined, joined_far, own_columns],
        [pltpu.VMEM((LANES, LANES), F32)],
    )
    (own_transposed,) = call(
        own_transposed_kernel,
        [SMEM] + [VMEM] * 3,
        [((QUARTER, SLAB), F32)],
        [flags, own_columns, rows, pairs],
    )
    odd_letter, even_letter, _ = lax.optimization_barrier((odd_letter, even_letter, sums))
    (near_columns,) = call(
        open_kernel,
        [VMEM] * 2,
        [((SLAB, WIDTH), BF16)],
        [odd_letter, even_letter],
    )
    far_columns = narrow_swap(near_columns, SWAP_CORE)
    (quarters,) = call(
        collect_kernel, [VMEM] * 2, [((HALF, WIDTH), BF16)], [odd_message, even_message]
    )
    quarters_y = narrow_swap(quarters, SWAP_Y)
    near_values, sums = call(
        near_kernel,
        [VMEM] * 4,
        [((SLAB, SLAB), F32), ((SLAB, LANES), F32)],
        [rows, near_columns, mask, sums],
    )
    far_values, partial, *messages = call(
        far_kernel,
        [SMEM] + [VMEM] * 8,
        [((SLAB, SLAB), F32), ((8, SLAB), F32), *MESSAGES],
        [flags, rows, far_columns, mask, own_kernel, near_values, sums, weight, compact],
    )
    first = trade(messages)

    row_scale, lane_scale, partial, *messages = call(
        sweep_kernel,
        [SMEM] + [VMEM] * 10,
        [((SLAB, LANES), F32), ((1, SLAB), F32), ((8, SLAB), F32), *MESSAGES],
        [flags, partial, *first, *weights, own_kernel, near_values, far_values, weight],
        [pltpu.VMEM((8, LANES), F32)],
    )
    (near_rows,) = call(
        quarters_kernel,
        [SMEM] + [VMEM] * 2,
        [((SLAB, WIDTH), BF16)],
        [flags, quarters, quarters_y],
    )
    second = trade(messages)
    far_rows = narrow_swap(near_rows, SWAP_CORE)

    (pushed,) = call(
        push_kernel,
        [VMEM] * 3,
        [((QUARTER, WIDTH), F32)],
        [lane_scale, own_transposed, rows],
    )
    odd_rows, even_rows, transposed = call(
        transposed_kernel,
        [SMEM] + [VMEM] * 5,
        [((SLAB, WIDTH), BF16), ((SLAB, WIDTH), BF16), ((QUARTER, 2 * SLAB), F32)],
        [flags, own_columns, near_rows, far_rows, *first],
    )

    return call(
        gradient_kernel,
        [SMEM] + [VMEM] * 18,
        [((QUARTER, WIDTH), F32)] * 2,
        [
            flags, partial, *second, *weights, row_scale, own_kernel, near_values, far_values,
            own_columns, near_columns, far_columns, rows, pushed, odd_rows, even_rows, transposed,
        ],
        [
            pltpu.VMEM((QUARTER, WIDTH), F32),
            pltpu.VMEM((QUARTER, WIDTH), F32),
            pltpu.SemaphoreType.DMA((2,)),
        ],
        out_specs=(HBM, HBM),
    )


def solution(mesh):
    return jax.shard_map(
        step,
        mesh=mesh,
        in_specs=(
            P(("wide", "narrow"), None),
            P("wide", None),
            P(("wide", "narrow")),
            P(),
            P(("wide", "narrow"), None),
        ),
        out_specs=(P(("wide", "narrow"), None), P(("wide", "narrow"), None)),
        check_vma=False,
    )
```

```python
import jax
import jax.numpy as jnp
from jax import lax
from jax.experimental import pallas as pl
from jax.experimental.pallas import tpu as pltpu
from jax.sharding import PartitionSpec as P


SMOOTHING_TEMP = 0.05
EPSILON = 1e-06

SWAP_Y = [(0, 2), (2, 0), (1, 3), (3, 1)]
SWAP_CORE = [(0, 1), (1, 0), (2, 3), (3, 2)]

LANES = 128
QUARTER = 256
HALF = 512
SLAB = 1024
WIDTH = 512
SCALE = 1.0 / (WIDTH * SMOOTHING_TEMP)

F32 = jnp.float32
BF16 = jnp.bfloat16

INFO = 16
MESSAGE = QUARTER + INFO
JOINED = 2 * MESSAGE
NOTE = 4

NARROW, CORE, Y, ODD, A_EVEN, HAS_ODD, FLIPPED, WIDE, WIDE_ODD, WIDE_EVEN = range(10)


def narrow_swap(block, pairs):
    return lax.ppermute(block, "narrow", pairs)


def exchange(block, hops, crossing):
    count = lax.axis_size("wide")
    narrow = lax.axis_size("narrow")
    pairs = []
    for n in range(narrow):
        far = hops[n % 2]
        for base in range(far if crossing else 0, count, 2 * far):
            for low in range(base, base + far):
                high = low + far
                if high < count:
                    other = n ^ 2 if low < count // 2 <= high else n
                    one, two = low * narrow + n, high * narrow + other
                    pairs += [(one, two), (two, one)]
    return lax.ppermute(block, ("wide", "narrow"), pairs)


def normalize(features):
    values = features.astype(F32)
    total = jnp.sum(values * values, axis=1, keepdims=True)
    return (values * lax.rsqrt(total * (1.0 / WIDTH) + EPSILON)).astype(BF16)


def nt_dot(a, b):
    return lax.dot_general(a, b, (((1,), (1,)), ((), ())), preferred_element_type=F32)


def identity():
    return lax.broadcasted_iota(jnp.int32, (LANES, LANES), 0) == lax.broadcasted_iota(
        jnp.int32, (LANES, LANES), 1
    )


def to_column(row):
    return jnp.sum(jnp.where(identity(), row, 0.0), axis=1, keepdims=True)


def to_row(column):
    return jnp.sum(jnp.where(identity(), column, 0.0), axis=0, keepdims=True)


def lane_tiles(values):
    total = values[:, :LANES]
    for i in range(1, values.shape[1] // LANES):
        total = total + values[:, i * LANES : (i + 1) * LANES]
    return total


def sublane_tiles(values):
    rows, columns = values.shape
    return jnp.sum(values.reshape(rows // 8, 8, columns), axis=0)


def block_kernel(rows_ref, columns, mask_ref, i, lanes):
    inner = nt_dot(rows_ref[pl.ds(pl.multiple_of(i * QUARTER, QUARTER), QUARTER), :], columns)
    values = jnp.exp(inner * SCALE)
    top = values[:LANES] * mask_ref[pl.ds(2 * i, 1), lanes]
    bottom = values[LANES:] * mask_ref[pl.ds(2 * i + 1, 1), lanes]
    return top, bottom


def fill_kernel(rows_ref, columns_ref, mask_ref, lanes, kernel_ref, sums_ref, before_ref):
    def step(i, carry):
        blocks = block_kernel(rows_ref, columns_ref[...], mask_ref, i, lanes)
        for j, block in enumerate(blocks):
            at = pl.ds(pl.multiple_of(i * QUARTER + j * LANES, LANES), LANES)
            kernel_ref[at, :] = block
            sums = lane_tiles(block)
            if before_ref is not None:
                sums = sums + before_ref[at, :]
            sums_ref[at, :] = sums
        return carry

    lax.fori_loop(0, 4, step, 0, unroll=True)


def pack_kernel(
    flags, treated_any, control_any, weight_any, band_any, letter_ref, other_ref, message_ref,
    treated_ref, weight_ref, band_ref, info_ref, sems,
):
    half = pl.ds(pl.multiple_of(flags[CORE] * HALF, HALF), HALF)
    other = pl.ds(pl.multiple_of((1 - flags[CORE]) * HALF, HALF), HALF)
    copies = [
        pltpu.make_async_copy(source, target, sems.at[i])
        for i, (source, target) in enumerate(
            (
                (treated_any, treated_ref),
                (weight_any, weight_ref),
                (band_any, band_ref),
                (control_any.at[half, :], letter_ref),
                (control_any.at[other, :], other_ref),
            )
        )
    ]
    for copy in copies:
        copy.start()
    info_ref[...] = jnp.zeros_like(info_ref)
    for copy in copies[:3]:
        copy.wait()
    rows = normalize(treated_ref[...])
    weight = weight_ref[...]
    for i in range(3):
        part = weight.astype(BF16).astype(F32)
        info_ref[0:2, i * LANES : (i + 1) * LANES] = part
        weight = weight - part
    info_ref[0:2, 3 * LANES : 3 * LANES + 24] = band_ref[...].astype(F32)
    info = info_ref[...].astype(BF16)
    message_ref[0:QUARTER, :] = rows
    message_ref[QUARTER:MESSAGE, :] = info
    for copy in copies[3:]:
        copy.wait()


def join_kernel(flags, own_ref, y_ref, joined_ref):
    for ref, y in ((own_ref, flags[Y]), (y_ref, 1 - flags[Y])):
        joined_ref[pl.ds(pl.multiple_of(y * QUARTER, QUARTER), QUARTER), :] = ref[0:QUARTER, :]
        joined_ref[pl.ds(pl.multiple_of(HALF + y * INFO, INFO), INFO), :] = ref[QUARTER:MESSAGE, :]


def columns_kernel(
    flags, letter_ref, other_ref, weight_any, columns_ref, own_ref, odd_ref, even_ref, fetched_ref,
    sems,
):
    copies = [
        pltpu.make_async_copy(
            weight_any.at[pl.ds(pl.multiple_of(flags[which] * 8, 8), 8), :],
            fetched_ref.at[i],
            sems.at[i],
        )
        for i, which in enumerate((WIDE, WIDE_ODD, WIDE_EVEN))
    ]
    for copy in copies:
        copy.start()
    for ref, half in ((letter_ref, flags[CORE]), (other_ref, 1 - flags[CORE])):
        columns_ref[pl.ds(pl.multiple_of(half * HALF, HALF), HALF), :] = normalize(ref[...])
    for i, (copy, ref) in enumerate(zip(copies, (own_ref, odd_ref, even_ref), strict=True)):
        copy.wait()
        for j in range(8):
            ref[0:1, j * LANES : (j + 1) * LANES] = fetched_ref[i, j : j + 1, :]


def open_kernel(odd_ref, even_ref, columns_ref):
    columns_ref[0:HALF, :] = normalize(odd_ref[...])
    columns_ref[HALF:SLAB, :] = normalize(even_ref[...])


def collect_kernel(odd_ref, even_ref, quarters_ref):
    quarters_ref[0:QUARTER, :] = odd_ref[0:QUARTER, :]
    quarters_ref[QUARTER:HALF, :] = even_ref[0:QUARTER, :]


def near_kernel(rows_ref, columns_ref, mask_ref, before_ref, kernel_ref, sums_ref):
    fill_kernel(
        rows_ref, columns_ref, mask_ref, slice(SLAB, 2 * SLAB), kernel_ref, sums_ref, before_ref
    )


def prepare_kernel(
    flags, joined_ref, far_ref, columns_ref, rows_ref, kernel_ref, sums_ref, mask_ref, weight_ref,
    pair_ref, compact_ref, band_ref,
):
    n, odd, core = flags[NARROW], flags[ODD], flags[CORE]
    rows_ref[0:HALF, :] = joined_ref[0:HALF, :]
    rows_ref[HALF:SLAB, :] = far_ref[0:HALF, :]

    band_ref[...] = jnp.zeros_like(band_ref)
    for i, (source, first) in enumerate(
        ((joined_ref, HALF), (joined_ref, HALF + INFO), (far_ref, HALF), (far_ref, HALF + INFO))
    ):
        info = source[first : first + INFO, :].astype(F32)
        band_ref[2 * i : 2 * i + 2, :] = info[0:2, 3 * LANES :]
        weights = info[:, :LANES] + info[:, LANES : 2 * LANES] + info[:, 2 * LANES : 3 * LANES]
        for j in range(2):
            at = slice((2 * i + j) * LANES, (2 * i + j + 1) * LANES)
            weight_ref[at, :] = jnp.broadcast_to(to_column(weights[j : j + 1]), (LANES, LANES))
    band = band_ref[...].astype(BF16)
    odd_base = odd * 16
    even_base = 16 - odd * 16
    lane = lax.broadcasted_iota(jnp.int32, (1, 3 * SLAB), 1)
    segment = lane // SLAB
    side = jnp.where(lane % SLAB < HALF, odd_base, even_base)
    side = side + 4 * jnp.where(segment == 1, core, 1 - core) + (lane % HALF) // LANES
    wanted = jnp.where(segment == 0, 8 + lane // LANES, side)
    one_hot = lax.broadcasted_iota(jnp.int32, (LANES, 3 * SLAB), 0) == wanted
    mask_ref[...] = jnp.dot(
        band[:16], jnp.where(one_hot, 1.0, 0.0).astype(BF16), preferred_element_type=F32
    )[:8]
    place = lax.broadcasted_iota(jnp.int32, (32, LANES), 0)
    base = jnp.where(place < 8, odd_base, jnp.where(place < 16, even_base, 8 + 2 * n))
    chosen = base + jnp.where(place < 16, place % 8, place % 2)
    select = jnp.where(
        lax.broadcasted_iota(jnp.int32, (32, LANES), 1) == chosen, 1.0, 0.0
    ).astype(BF16)
    by_block = nt_dot(select, band).astype(BF16)
    shift = (
        lax.broadcasted_iota(jnp.int32, (LANES, LANES), 0)
        == lax.broadcasted_iota(jnp.int32, (LANES, LANES), 1) % 8
    )
    flat = jnp.dot(
        by_block, jnp.where(shift, 1.0, 0.0).astype(BF16), preferred_element_type=F32
    )
    kept = lax.broadcasted_iota(jnp.int32, (8, LANES), 0) == (
        lax.broadcasted_iota(jnp.int32, (8, LANES), 1) // 8
    )
    compact_ref[...] = jnp.zeros_like(compact_ref)
    for i in range(2):
        row = jnp.where(kept, flat[8 * i : 8 * i + 8], 0.0)
        compact_ref[i : i + 1, 0:LANES] = jnp.sum(row, axis=0, keepdims=True)
    spread = (
        lax.broadcasted_iota(jnp.int32, (LANES, SLAB), 0)
        == lax.broadcasted_iota(jnp.int32, (LANES, SLAB), 1) // LANES
    )
    pair_ref[...] = jnp.dot(
        by_block, jnp.where(spread, 1.0, 0.0).astype(BF16), preferred_element_type=F32
    )[16:24]

    fill_kernel(rows_ref, columns_ref, mask_ref, slice(0, SLAB), kernel_ref, sums_ref, None)


def regroup(flags, first, second):
    low = jnp.concatenate([first[:, :HALF], second[:, :HALF]], axis=1)
    high = jnp.concatenate([first[:, HALF:], second[:, HALF:]], axis=1)
    swap = flags[CORE] > 0
    return jnp.where(swap, high, low), jnp.where(swap, low, high)


def finish_messages(flags, sums, first, second, partial_ref, cross_ref, inner_ref):
    own, near, far = (jnp.sum(part, axis=0, keepdims=True) for part in sums)
    one = flags[CORE] > 0
    low = jnp.where(one, far, near)
    high = jnp.where(one, near, far)
    odd = jnp.concatenate([low[:, :HALF], high[:, :HALF]], axis=1)
    even = jnp.concatenate([low[:, HALF:], high[:, HALF:]], axis=1)
    partial_ref[...] = jnp.zeros_like(partial_ref)
    partial_ref[0:1, :] = own
    partial_ref[1:2, :] = odd
    partial_ref[2:3, :] = even
    a_even = flags[A_EVEN] > 0
    for ref, side, along, distant in (
        (cross_ref, odd, first, jnp.where(a_even, even, odd)),
        (inner_ref, even, second, jnp.where(a_even, odd, even)),
    ):
        ref[...] = jnp.zeros_like(ref)
        ref[0:1, :] = jnp.where(one, distant, own)
        ref[1:2, :] = side
        ref[2 : 2 + along.shape[0], :] = along


def stack_kernel(cross_ref, inner_ref, both_ref):
    both_ref[0:NOTE, :] = cross_ref[...]
    both_ref[NOTE : 2 * NOTE, :] = inner_ref[...]


def received(flags, mine_ref, theirs_ref):
    one = flags[CORE] > 0
    mine, theirs = mine_ref[...], theirs_ref[...]
    return jnp.where(one, theirs, mine), jnp.where(one, mine, theirs)


def turned(flags, rows):
    swapped = jnp.concatenate([rows[:, HALF:], rows[:, :HALF]], axis=1)
    return jnp.where(flags[CORE] > 0, swapped, rows)


def far_kernel(
    flags, rows_ref, columns_ref, mask_ref, own_kernel_ref, near_kernel_ref, before_ref,
    weight_ref, compact_ref, kernel_ref, partial_ref, cross_ref, inner_ref,
):
    def step(i, carry):
        own, near, far = carry
        blocks = block_kernel(
            rows_ref, columns_ref[...], mask_ref, i, slice(2 * SLAB, 3 * SLAB)
        )
        for j, block in enumerate(blocks):
            at = pl.ds(pl.multiple_of(i * QUARTER + j * LANES, LANES), LANES)
            kernel_ref[at, :] = block
            sums = lane_tiles(block) + before_ref[at, :]
            scale = weight_ref[at, 0:1] / jnp.sum(sums, axis=1, keepdims=True)
            own = own + sublane_tiles(own_kernel_ref[at, :] * scale)
            near = near + sublane_tiles(near_kernel_ref[at, :] * scale)
            far = far + sublane_tiles(block * scale)
        return own, near, far

    zero = jnp.zeros((8, SLAB), F32)
    sums = lax.fori_loop(0, 4, step, (zero, zero, zero), unroll=True)
    finish_messages(
        flags, sums, compact_ref[0:1, :], compact_ref[1:2, :], partial_ref, cross_ref, inner_ref
    )


def column_scales(flags, partial_ref, mine_ref, theirs_ref, weights):
    a_even = flags[A_EVEN] > 0
    close, distant = received(flags, mine_ref, theirs_ref)
    a, b = distant[0:1], distant[NOTE : NOTE + 1]
    own = partial_ref[0:1, :] + close[1:2] + close[NOTE + 1 : NOTE + 2]
    odd = partial_ref[1:2, :] + close[0:1] + jnp.where(a_even, b, a)
    even = partial_ref[2:3, :] + close[NOTE : NOTE + 1] + jnp.where(a_even, a, b)
    has_odd = flags[HAS_ODD] > 0
    own_weight, odd_weight, even_weight = (ref[...] for ref in weights)
    odd = jnp.where(has_odd, odd_weight / jnp.where(has_odd, odd, 1.0), 0.0)
    even = even_weight / even
    return own_weight / own, *regroup(flags, odd, even)


def sweep_kernel(
    flags, partial_in, mine_in, theirs_in, own_weight, odd_weight, even_weight, own_kernel_ref,
    near_kernel_ref, far_kernel_ref, weight_ref, row_ref, lane_ref, partial_ref, cross_ref,
    inner_ref, flat_ref,
):
    scales = column_scales(
        flags, partial_in, mine_in, theirs_in, (own_weight, odd_weight, even_weight)
    )
    kernels = (own_kernel_ref, near_kernel_ref, far_kernel_ref)

    def step(i, carry):
        at = pl.ds(pl.multiple_of(i * LANES, LANES), LANES)
        total = jnp.zeros((LANES, LANES), F32)
        for kernel_ref, scale in zip(kernels, scales, strict=True):
            total = total + lane_tiles(kernel_ref[at, :] * scale)
        row_scale = weight_ref[at, 0:1] / jnp.sum(total, axis=1, keepdims=True)
        row_ref[at, :] = jnp.broadcast_to(row_scale, (LANES, LANES))
        flat_ref[pl.ds(i, 1), :] = to_row(row_scale)
        return tuple(
            sums + sublane_tiles(kernel_ref[at, :] * row_scale)
            for kernel_ref, sums in zip(kernels, carry, strict=True)
        )

    zero = jnp.zeros((8, SLAB), F32)
    sums = lax.fori_loop(0, 8, step, (zero, zero, zero), unroll=True)
    for i in range(8):
        lane_ref[0:1, i * LANES : (i + 1) * LANES] = flat_ref[i : i + 1, :]
    flat = lane_ref[...]
    finish_messages(flags, sums, flat, flat, partial_ref, cross_ref, inner_ref)


def quarters_kernel(flags, own_ref, y_ref, pair_ref):
    y = flags[Y]
    odd_y = jnp.where(flags[FLIPPED] > 0, 1 - y, y)
    for ref, odd_at, even_at in ((own_ref, odd_y, y), (y_ref, 1 - odd_y, 1 - y)):
        for at, first in ((odd_at * QUARTER, 0), (HALF + even_at * QUARTER, QUARTER)):
            pair_ref[pl.ds(pl.multiple_of(at, QUARTER), QUARTER), :] = ref[first : first + QUARTER, :]


def own_control(flags, columns_ref):
    return columns_ref[pl.ds(pl.multiple_of(flags[NARROW] * QUARTER, QUARTER), QUARTER), :]


def own_transposed_kernel(flags, columns_ref, rows_ref, pair_ref, kernel_ref):
    values = jnp.exp(nt_dot(own_control(flags, columns_ref), rows_ref[...]) * SCALE)
    kernel_ref[0:LANES, :] = values[:LANES] * pair_ref[0:1, :]
    kernel_ref[LANES:QUARTER, :] = values[LANES:] * pair_ref[1:2, :]


def push_kernel(lane_ref, kernel_ref, rows_ref, pushed_ref):
    pushed_ref[...] = jnp.dot(
        (lane_ref[...] * kernel_ref[...]).astype(BF16),
        rows_ref[...],
        preferred_element_type=F32,
    )


def transposed_kernel(
    flags, columns_ref, near_ref, far_ref, mine_in, theirs_in, odd_rows_ref, even_rows_ref,
    kernel_ref,
):
    own = own_control(flags, columns_ref)
    odd_rows_ref[0:HALF, :] = near_ref[0:HALF, :]
    odd_rows_ref[HALF:SLAB, :] = far_ref[0:HALF, :]
    even_rows_ref[0:HALF, :] = near_ref[HALF:SLAB, :]
    even_rows_ref[HALF:SLAB, :] = far_ref[HALF:SLAB, :]
    n = flags[NARROW]
    close, _ = received(flags, mine_in, theirs_in)
    lane = lax.broadcasted_iota(jnp.int32, (16, LANES), 1)
    wanted = (lane < 64) & (lane // 8 == 2 * n + lax.broadcasted_iota(jnp.int32, (16, LANES), 0))
    spread = (
        lax.broadcasted_iota(jnp.int32, (LANES, SLAB), 0) % 8
        == lax.broadcasted_iota(jnp.int32, (LANES, SLAB), 1) // LANES
    )
    spread = jnp.where(spread, 1.0, 0.0).astype(BF16)
    for i, (rows_ref, first) in enumerate(((odd_rows_ref, 2), (even_rows_ref, NOTE + 2))):
        compact = jnp.where(wanted, close[first : first + 1, :LANES], 0.0).astype(BF16)
        found = turned(flags, jnp.dot(compact, spread, preferred_element_type=F32))
        values = jnp.exp(nt_dot(own, rows_ref[...]) * SCALE)
        lanes = slice(i * SLAB, (i + 1) * SLAB)
        kernel_ref[0:LANES, lanes] = values[:LANES] * found[0:1]
        kernel_ref[LANES:QUARTER, lanes] = values[LANES:] * found[1:2]


def gradient_kernel(
    flags, partial_in, mine_in, theirs_in, own_weight, odd_weight, even_weight, row_ref,
    own_kernel_ref, near_kernel_ref, far_kernel_ref, own_columns_ref, near_columns_ref,
    far_columns_ref, rows_ref, pushed_ref, odd_rows_ref, even_rows_ref, transposed_ref,
    treated_any, control_any, treated_out, control_out, sems,
):
    scales = column_scales(
        flags, partial_in, mine_in, theirs_in, (own_weight, odd_weight, even_weight)
    )
    close, _ = received(flags, mine_in, theirs_in)
    pushed = pushed_ref[...]
    for i, (row, rows) in enumerate(((2, odd_rows_ref), (NOTE + 2, even_rows_ref))):
        scale = turned(flags, close[row : row + 1])
        transport = (scale * transposed_ref[:, i * SLAB : (i + 1) * SLAB]).astype(BF16)
        pushed = pushed + jnp.dot(transport, rows[...], preferred_element_type=F32)
    n = flags[NARROW]

    def own_quarter(row):
        found = row[:, :QUARTER]
        for i in range(1, 4):
            found = jnp.where(n == i, row[:, i * QUARTER : (i + 1) * QUARTER], found)
        return found

    def upright(row):
        return jnp.concatenate([to_column(row[:, :LANES]), to_column(row[:, LANES:])], axis=0)

    own_scale = upright(own_quarter(scales[0]))
    own_mass = upright(own_quarter(own_weight[...]))
    at = pl.ds(pl.multiple_of(n * QUARTER, QUARTER), QUARTER)
    control_out[...] = own_mass * own_columns_ref[at, :].astype(F32) - own_scale * pushed
    control_copy = pltpu.make_async_copy(control_out, control_any, sems.at[1])
    control_copy.start()
    mine = pl.ds(pl.multiple_of(flags[Y] * QUARTER, QUARTER), QUARTER)
    row_scale = row_ref[mine, 0:1]
    mass = jnp.zeros((QUARTER, LANES), F32)
    pulled = jnp.zeros((QUARTER, WIDTH), F32)
    for kernel_ref, scale, columns_ref in zip(
        (own_kernel_ref, near_kernel_ref, far_kernel_ref),
        scales,
        (own_columns_ref, near_columns_ref, far_columns_ref),
        strict=True,
    ):
        transport = row_scale * kernel_ref[mine, :] * scale
        mass = mass + lane_tiles(transport)
        pulled = pulled + jnp.dot(
            transport.astype(BF16), columns_ref[...], preferred_element_type=F32
        )
    mass = jnp.sum(mass, axis=1, keepdims=True)
    treated_out[...] = mass * rows_ref[mine, :].astype(F32) - pulled
    treated_copy = pltpu.make_async_copy(treated_out, treated_any, sems.at[0])
    treated_copy.start()

    treated_copy.wait()
    control_copy.wait()


VMEM = pl.BlockSpec(memory_space=pltpu.VMEM)
HBM = pl.BlockSpec(memory_space=pltpu.HBM)
SMEM = pl.BlockSpec(memory_space=pltpu.SMEM)


def call(body, specs, outs, operands, scratch=(), limit=16, out_specs=None):
    return pl.pallas_call(
        body,
        out_shape=tuple(jax.ShapeDtypeStruct(shape, dtype) for shape, dtype in outs),
        in_specs=specs,
        out_specs=out_specs or tuple(VMEM for _ in outs),
        scratch_shapes=list(scratch),
        compiler_params=pltpu.CompilerParams(vmem_limit_bytes=limit << 20),
    )(*operands)


MESSAGES = [((NOTE, SLAB), F32), ((NOTE, SLAB), F32)]


def trade(messages):
    cross = exchange(messages[0], (1, 2), True)
    inner = exchange(messages[1], (1, 2), False)
    (mine,) = call(stack_kernel, [VMEM] * 2, [((2 * NOTE, SLAB), F32)], [cross, inner])
    return mine, narrow_swap(mine, SWAP_CORE)


def step(treated, control, treated_weight, control_weight, band):
    wide_index = lax.axis_index("wide")
    n = lax.axis_index("narrow")
    wide_count = lax.axis_size("wide")
    odd = wide_index % 2
    toward_odd = wide_index + 2 * odd - 1
    toward_even = wide_index + 1 - 2 * odd
    values = (
        n,
        n % 2,
        n // 2,
        odd,
        jnp.logical_xor(wide_index % 4 >= 2, odd == 1).astype(jnp.int32),
        ((toward_odd >= 0) & (toward_odd < wide_count)).astype(jnp.int32),
        (jnp.minimum(wide_index, toward_odd) == wide_count // 2 - 1).astype(jnp.int32),
        wide_index,
        jnp.clip(toward_odd, 0, wide_count - 1),
        toward_even,
    )
    place = lax.iota(jnp.int32, 16)
    flags = jnp.zeros((16,), jnp.int32)
    for i, value in enumerate(values):
        flags = jnp.where(place == i, value, flags)
    treated, control, own_weight, own_band, column_weight = (
        pltpu.with_memory_space_constraint(x, pltpu.HBM)
        for x in (
            treated, control, treated_weight.reshape(2, LANES), band,
            control_weight.reshape(-1, LANES),
        )
    )
    letter, other, message = call(
        pack_kernel,
        [SMEM] + [HBM] * 4,
        [((HALF, WIDTH), BF16), ((HALF, WIDTH), BF16), ((MESSAGE, WIDTH), BF16)],
        [flags, treated, control, own_weight, own_band],
        [
            pltpu.VMEM((QUARTER, WIDTH), BF16),
            pltpu.VMEM((2, LANES), F32),
            pltpu.VMEM((2, 24), jnp.int32),
            pltpu.VMEM((INFO, WIDTH), F32),
            pltpu.SemaphoreType.DMA((5,)),
        ],
    )
    odd_letter = exchange(letter, (1, 1), True)
    even_letter = exchange(letter, (1, 1), False)
    own_columns, *weights = call(
        columns_kernel,
        [SMEM] + [VMEM] * 2 + [HBM],
        [((SLAB, WIDTH), BF16)] + [((1, SLAB), F32)] * 3,
        [flags, letter, other, column_weight],
        [pltpu.VMEM((3, 8, LANES), F32), pltpu.SemaphoreType.DMA((3,))],
    )

    odd_message = exchange(message, (1, 1), True)
    even_message = exchange(message, (1, 1), False)
    message_y = narrow_swap(message, SWAP_Y)
    (joined,) = call(
        join_kernel, [SMEM] + [VMEM] * 2, [((JOINED, WIDTH), BF16)], [flags, message, message_y]
    )
    joined_far = narrow_swap(joined, SWAP_CORE)

    rows, own_kernel, sums, mask, weight, pairs, compact = call(
        prepare_kernel,
        [SMEM] + [VMEM] * 3,
        [
            ((SLAB, WIDTH), BF16),
            ((SLAB, SLAB), F32),
            ((SLAB, LANES), F32),
            ((8, 3 * SLAB), F32),
            ((SLAB, LANES), F32),
            ((8, SLAB), F32),
            ((8, SLAB), F32),
        ],
        [flags, joined, joined_far, own_columns],
        [pltpu.VMEM((LANES, LANES), F32)],
    )
    (own_transposed,) = call(
        own_transposed_kernel,
        [SMEM] + [VMEM] * 3,
        [((QUARTER, SLAB), F32)],
        [flags, own_columns, rows, pairs],
    )
    odd_letter, even_letter, _ = lax.optimization_barrier((odd_letter, even_letter, sums))
    (near_columns,) = call(
        open_kernel,
        [VMEM] * 2,
        [((SLAB, WIDTH), BF16)],
        [odd_letter, even_letter],
    )
    far_columns = narrow_swap(near_columns, SWAP_CORE)
    (quarters,) = call(
        collect_kernel, [VMEM] * 2, [((HALF, WIDTH), BF16)], [odd_message, even_message]
    )
    quarters_y = narrow_swap(quarters, SWAP_Y)
    near_values, sums = call(
        near_kernel,
        [VMEM] * 4,
        [((SLAB, SLAB), F32), ((SLAB, LANES), F32)],
        [rows, near_columns, mask, sums],
    )
    far_values, partial, *messages = call(
        far_kernel,
        [SMEM] + [VMEM] * 8,
        [((SLAB, SLAB), F32), ((8, SLAB), F32), *MESSAGES],
        [flags, rows, far_columns, mask, own_kernel, near_values, sums, weight, compact],
    )
    first = trade(messages)

    row_scale, lane_scale, partial, *messages = call(
        sweep_kernel,
        [SMEM] + [VMEM] * 10,
        [((SLAB, LANES), F32), ((1, SLAB), F32), ((8, SLAB), F32), *MESSAGES],
        [flags, partial, *first, *weights, own_kernel, near_values, far_values, weight],
        [pltpu.VMEM((8, LANES), F32)],
    )
    (near_rows,) = call(
        quarters_kernel,
        [SMEM] + [VMEM] * 2,
        [((SLAB, WIDTH), BF16)],
        [flags, quarters, quarters_y],
    )
    second = trade(messages)
    far_rows = narrow_swap(near_rows, SWAP_CORE)

    (pushed,) = call(
        push_kernel,
        [VMEM] * 3,
        [((QUARTER, WIDTH), F32)],
        [lane_scale, own_transposed, rows],
    )
    odd_rows, even_rows, transposed = call(
        transposed_kernel,
        [SMEM] + [VMEM] * 5,
        [((SLAB, WIDTH), BF16), ((SLAB, WIDTH), BF16), ((QUARTER, 2 * SLAB), F32)],
        [flags, own_columns, near_rows, far_rows, *first],
    )

    return call(
        gradient_kernel,
        [SMEM] + [VMEM] * 18,
        [((QUARTER, WIDTH), F32)] * 2,
        [
            flags, partial, *second, *weights, row_scale, own_kernel, near_values, far_values,
            own_columns, near_columns, far_columns, rows, pushed, odd_rows, even_rows, transposed,
        ],
        [
            pltpu.VMEM((QUARTER, WIDTH), F32),
            pltpu.VMEM((QUARTER, WIDTH), F32),
            pltpu.SemaphoreType.DMA((2,)),
        ],
        out_specs=(HBM, HBM),
    )


def solution(mesh):
    return jax.shard_map(
        step,
        mesh=mesh,
        in_specs=(
            P(("wide", "narrow"), None),
            P("wide", None),
            P(("wide", "narrow")),
            P(),
            P(("wide", "narrow"), None),
        ),
        out_specs=(P(("wide", "narrow"), None), P(("wide", "narrow"), None)),
        check_vma=False,
    )
```

```python
import jax
import jax.numpy as jnp
from jax import lax
from jax.experimental import pallas as pl
from jax.experimental.pallas import tpu as pltpu
from jax.sharding import PartitionSpec as P


SMOOTHING_TEMP = 0.05
EPSILON = 1e-06

SWAP_Y = [(0, 2), (2, 0), (1, 3), (3, 1)]
SWAP_CORE = [(0, 1), (1, 0), (2, 3), (3, 2)]

LANES = 128
QUARTER = 256
HALF = 512
SLAB = 1024
WIDTH = 512
SCALE = 1.0 / (WIDTH * SMOOTHING_TEMP)

F32 = jnp.float32
BF16 = jnp.bfloat16

INFO = 16
MESSAGE = QUARTER + INFO
JOINED = 2 * MESSAGE
NOTE = 4

NARROW, CORE, Y, ODD, A_EVEN, HAS_ODD, FLIPPED, WIDE, WIDE_ODD, WIDE_EVEN = range(10)


def narrow_swap(block, pairs):
    return lax.ppermute(block, "narrow", pairs)


def exchange(block, hops, crossing):
    count = lax.axis_size("wide")
    narrow = lax.axis_size("narrow")
    pairs = []
    for n in range(narrow):
        far = hops[n % 2]
        for base in range(far if crossing else 0, count, 2 * far):
            for low in range(base, base + far):
                high = low + far
                if high < count:
                    other = n ^ 2 if low < count // 2 <= high else n
                    one, two = low * narrow + n, high * narrow + other
                    pairs += [(one, two), (two, one)]
    return lax.ppermute(block, ("wide", "narrow"), pairs)


def normalize(features):
    values = features.astype(F32)
    total = jnp.sum(values * values, axis=1, keepdims=True)
    return (values * lax.rsqrt(total * (1.0 / WIDTH) + EPSILON)).astype(BF16)


def nt_dot(a, b):
    return lax.dot_general(a, b, (((1,), (1,)), ((), ())), preferred_element_type=F32)


def identity():
    return lax.broadcasted_iota(jnp.int32, (LANES, LANES), 0) == lax.broadcasted_iota(
        jnp.int32, (LANES, LANES), 1
    )


def to_column(row):
    return jnp.sum(jnp.where(identity(), row, 0.0), axis=1, keepdims=True)


def to_row(column):
    return jnp.sum(jnp.where(identity(), column, 0.0), axis=0, keepdims=True)


def lane_tiles(values):
    total = values[:, :LANES]
    for i in range(1, values.shape[1] // LANES):
        total = total + values[:, i * LANES : (i + 1) * LANES]
    return total


def sublane_tiles(values):
    rows, columns = values.shape
    return jnp.sum(values.reshape(rows // 8, 8, columns), axis=0)


def block_kernel(rows_ref, columns, mask_ref, i, lanes):
    inner = nt_dot(rows_ref[pl.ds(pl.multiple_of(i * QUARTER, QUARTER), QUARTER), :], columns)
    values = jnp.exp(inner * SCALE)
    top = values[:LANES] * mask_ref[pl.ds(2 * i, 1), lanes]
    bottom = values[LANES:] * mask_ref[pl.ds(2 * i + 1, 1), lanes]
    return top, bottom


def fill_kernel(rows_ref, columns_ref, mask_ref, lanes, kernel_ref, sums_ref, before_ref):
    def step(i, carry):
        blocks = block_kernel(rows_ref, columns_ref[...], mask_ref, i, lanes)
        for j, block in enumerate(blocks):
            at = pl.ds(pl.multiple_of(i * QUARTER + j * LANES, LANES), LANES)
            kernel_ref[at, :] = block
            sums = lane_tiles(block)
            if before_ref is not None:
                sums = sums + before_ref[at, :]
            sums_ref[at, :] = sums
        return carry

    lax.fori_loop(0, 4, step, 0, unroll=True)


def pack_kernel(
    flags, treated_any, control_any, weight_any, band_any, columns_any, letter_ref, other_ref,
    message_ref, own_ref, odd_ref, even_ref, treated_ref, weight_ref, band_ref, info_ref,
    fetched_ref, sems,
):
    half = pl.ds(pl.multiple_of(flags[CORE] * HALF, HALF), HALF)
    other = pl.ds(pl.multiple_of((1 - flags[CORE]) * HALF, HALF), HALF)
    copies = [
        pltpu.make_async_copy(source, target, sems.at[i])
        for i, (source, target) in enumerate(
            (
                (treated_any, treated_ref),
                (weight_any, weight_ref),
                (band_any, band_ref),
                (control_any.at[half, :], letter_ref),
                (control_any.at[other, :], other_ref),
                *(
                    (
                        columns_any.at[pl.ds(pl.multiple_of(flags[which] * 8, 8), 8), :],
                        fetched_ref.at[j],
                    )
                    for j, which in enumerate((WIDE, WIDE_ODD, WIDE_EVEN))
                ),
            )
        )
    ]
    for copy in copies:
        copy.start()
    info_ref[...] = jnp.zeros_like(info_ref)
    for copy in copies[:3]:
        copy.wait()
    rows = normalize(treated_ref[...])
    weight = weight_ref[...]
    for i in range(3):
        part = weight.astype(BF16).astype(F32)
        info_ref[0:2, i * LANES : (i + 1) * LANES] = part
        weight = weight - part
    info_ref[0:2, 3 * LANES : 3 * LANES + 24] = band_ref[...].astype(F32)
    info = info_ref[...].astype(BF16)
    message_ref[0:QUARTER, :] = rows
    message_ref[QUARTER:MESSAGE, :] = info
    for copy in copies[3:]:
        copy.wait()
    for i, ref in enumerate((own_ref, odd_ref, even_ref)):
        for j in range(8):
            ref[0:1, j * LANES : (j + 1) * LANES] = fetched_ref[i, j : j + 1, :]


def join_kernel(flags, own_ref, y_ref, joined_ref):
    for ref, y in ((own_ref, flags[Y]), (y_ref, 1 - flags[Y])):
        joined_ref[pl.ds(pl.multiple_of(y * QUARTER, QUARTER), QUARTER), :] = ref[0:QUARTER, :]
        joined_ref[pl.ds(pl.multiple_of(HALF + y * INFO, INFO), INFO), :] = ref[QUARTER:MESSAGE, :]


def columns_kernel(flags, letter_ref, other_ref, columns_ref):
    for ref, half in ((letter_ref, flags[CORE]), (other_ref, 1 - flags[CORE])):
        columns_ref[pl.ds(pl.multiple_of(half * HALF, HALF), HALF), :] = normalize(ref[...])


def open_kernel(odd_ref, even_ref, columns_ref):
    columns_ref[0:HALF, :] = normalize(odd_ref[...])
    columns_ref[HALF:SLAB, :] = normalize(even_ref[...])


def collect_kernel(odd_ref, even_ref, quarters_ref):
    quarters_ref[0:QUARTER, :] = odd_ref[0:QUARTER, :]
    quarters_ref[QUARTER:HALF, :] = even_ref[0:QUARTER, :]


def near_kernel(rows_ref, columns_ref, mask_ref, before_ref, kernel_ref, sums_ref):
    fill_kernel(
        rows_ref, columns_ref, mask_ref, slice(SLAB, 2 * SLAB), kernel_ref, sums_ref, before_ref
    )


def prepare_kernel(
    flags, joined_ref, far_ref, columns_ref, rows_ref, kernel_ref, sums_ref, mask_ref, weight_ref,
    pair_ref, compact_ref, band_ref,
):
    n, odd, core = flags[NARROW], flags[ODD], flags[CORE]
    rows_ref[0:HALF, :] = joined_ref[0:HALF, :]
    rows_ref[HALF:SLAB, :] = far_ref[0:HALF, :]

    band_ref[...] = jnp.zeros_like(band_ref)
    for i, (source, first) in enumerate(
        ((joined_ref, HALF), (joined_ref, HALF + INFO), (far_ref, HALF), (far_ref, HALF + INFO))
    ):
        info = source[first : first + INFO, :].astype(F32)
        band_ref[2 * i : 2 * i + 2, :] = info[0:2, 3 * LANES :]
        weights = info[:, :LANES] + info[:, LANES : 2 * LANES] + info[:, 2 * LANES : 3 * LANES]
        for j in range(2):
            at = slice((2 * i + j) * LANES, (2 * i + j + 1) * LANES)
            weight_ref[at, :] = jnp.broadcast_to(to_column(weights[j : j + 1]), (LANES, LANES))
    band = band_ref[...].astype(BF16)
    odd_base = odd * 16
    even_base = 16 - odd * 16
    lane = lax.broadcasted_iota(jnp.int32, (1, 3 * SLAB), 1)
    segment = lane // SLAB
    side = jnp.where(lane % SLAB < HALF, odd_base, even_base)
    side = side + 4 * jnp.where(segment == 1, core, 1 - core) + (lane % HALF) // LANES
    wanted = jnp.where(segment == 0, 8 + lane // LANES, side)
    one_hot = lax.broadcasted_iota(jnp.int32, (LANES, 3 * SLAB), 0) == wanted
    mask_ref[...] = jnp.dot(
        band[:16], jnp.where(one_hot, 1.0, 0.0).astype(BF16), preferred_element_type=F32
    )[:8]
    place = lax.broadcasted_iota(jnp.int32, (32, LANES), 0)
    base = jnp.where(place < 8, odd_base, jnp.where(place < 16, even_base, 8 + 2 * n))
    chosen = base + jnp.where(place < 16, place % 8, place % 2)
    select = jnp.where(
        lax.broadcasted_iota(jnp.int32, (32, LANES), 1) == chosen, 1.0, 0.0
    ).astype(BF16)
    by_block = nt_dot(select, band).astype(BF16)
    shift = (
        lax.broadcasted_iota(jnp.int32, (LANES, LANES), 0)
        == lax.broadcasted_iota(jnp.int32, (LANES, LANES), 1) % 8
    )
    flat = jnp.dot(
        by_block, jnp.where(shift, 1.0, 0.0).astype(BF16), preferred_element_type=F32
    )
    kept = lax.broadcasted_iota(jnp.int32, (8, LANES), 0) == (
        lax.broadcasted_iota(jnp.int32, (8, LANES), 1) // 8
    )
    compact_ref[...] = jnp.zeros_like(compact_ref)
    for i in range(2):
        row = jnp.where(kept, flat[8 * i : 8 * i + 8], 0.0)
        compact_ref[i : i + 1, 0:LANES] = jnp.sum(row, axis=0, keepdims=True)
    spread = (
        lax.broadcasted_iota(jnp.int32, (LANES, SLAB), 0)
        == lax.broadcasted_iota(jnp.int32, (LANES, SLAB), 1) // LANES
    )
    pair_ref[...] = jnp.dot(
        by_block, jnp.where(spread, 1.0, 0.0).astype(BF16), preferred_element_type=F32
    )[16:24]

    fill_kernel(rows_ref, columns_ref, mask_ref, slice(0, SLAB), kernel_ref, sums_ref, None)


def regroup(flags, first, second):
    low = jnp.concatenate([first[:, :HALF], second[:, :HALF]], axis=1)
    high = jnp.concatenate([first[:, HALF:], second[:, HALF:]], axis=1)
    swap = flags[CORE] > 0
    return jnp.where(swap, high, low), jnp.where(swap, low, high)


def finish_messages(flags, sums, first, second, partial_ref, cross_ref, inner_ref):
    own, near, far = (jnp.sum(part, axis=0, keepdims=True) for part in sums)
    one = flags[CORE] > 0
    low = jnp.where(one, far, near)
    high = jnp.where(one, near, far)
    odd = jnp.concatenate([low[:, :HALF], high[:, :HALF]], axis=1)
    even = jnp.concatenate([low[:, HALF:], high[:, HALF:]], axis=1)
    partial_ref[...] = jnp.zeros_like(partial_ref)
    partial_ref[0:1, :] = own
    partial_ref[1:2, :] = odd
    partial_ref[2:3, :] = even
    a_even = flags[A_EVEN] > 0
    for ref, side, along, distant in (
        (cross_ref, odd, first, jnp.where(a_even, even, odd)),
        (inner_ref, even, second, jnp.where(a_even, odd, even)),
    ):
        ref[...] = jnp.zeros_like(ref)
        ref[0:1, :] = jnp.where(one, distant, own)
        ref[1:2, :] = side
        ref[2 : 2 + along.shape[0], :] = along


def stack_kernel(cross_ref, inner_ref, both_ref):
    both_ref[0:NOTE, :] = cross_ref[...]
    both_ref[NOTE : 2 * NOTE, :] = inner_ref[...]


def received(flags, mine_ref, theirs_ref):
    one = flags[CORE] > 0
    mine, theirs = mine_ref[...], theirs_ref[...]
    return jnp.where(one, theirs, mine), jnp.where(one, mine, theirs)


def turned(flags, rows):
    swapped = jnp.concatenate([rows[:, HALF:], rows[:, :HALF]], axis=1)
    return jnp.where(flags[CORE] > 0, swapped, rows)


def far_kernel(
    flags, rows_ref, columns_ref, mask_ref, own_kernel_ref, near_kernel_ref, before_ref,
    weight_ref, compact_ref, kernel_ref, partial_ref, cross_ref, inner_ref,
):
    def step(i, carry):
        own, near, far = carry
        blocks = block_kernel(
            rows_ref, columns_ref[...], mask_ref, i, slice(2 * SLAB, 3 * SLAB)
        )
        for j, block in enumerate(blocks):
            at = pl.ds(pl.multiple_of(i * QUARTER + j * LANES, LANES), LANES)
            kernel_ref[at, :] = block
            sums = lane_tiles(block) + before_ref[at, :]
            scale = weight_ref[at, 0:1] / jnp.sum(sums, axis=1, keepdims=True)
            own = own + sublane_tiles(own_kernel_ref[at, :] * scale)
            near = near + sublane_tiles(near_kernel_ref[at, :] * scale)
            far = far + sublane_tiles(block * scale)
        return own, near, far

    zero = jnp.zeros((8, SLAB), F32)
    sums = lax.fori_loop(0, 4, step, (zero, zero, zero), unroll=True)
    finish_messages(
        flags, sums, compact_ref[0:1, :], compact_ref[1:2, :], partial_ref, cross_ref, inner_ref
    )


def column_scales(flags, partial_ref, mine_ref, theirs_ref, weights):
    a_even = flags[A_EVEN] > 0
    close, distant = received(flags, mine_ref, theirs_ref)
    a, b = distant[0:1], distant[NOTE : NOTE + 1]
    own = partial_ref[0:1, :] + close[1:2] + close[NOTE + 1 : NOTE + 2]
    odd = partial_ref[1:2, :] + close[0:1] + jnp.where(a_even, b, a)
    even = partial_ref[2:3, :] + close[NOTE : NOTE + 1] + jnp.where(a_even, a, b)
    has_odd = flags[HAS_ODD] > 0
    own_weight, odd_weight, even_weight = (ref[...] for ref in weights)
    odd = jnp.where(has_odd, odd_weight / jnp.where(has_odd, odd, 1.0), 0.0)
    even = even_weight / even
    return own_weight / own, *regroup(flags, odd, even)


def sweep_kernel(
    flags, partial_in, mine_in, theirs_in, own_weight, odd_weight, even_weight, own_kernel_ref,
    near_kernel_ref, far_kernel_ref, weight_ref, row_ref, lane_ref, partial_ref, cross_ref,
    inner_ref, flat_ref,
):
    scales = column_scales(
        flags, partial_in, mine_in, theirs_in, (own_weight, odd_weight, even_weight)
    )
    kernels = (own_kernel_ref, near_kernel_ref, far_kernel_ref)

    def step(i, carry):
        at = pl.ds(pl.multiple_of(i * LANES, LANES), LANES)
        total = jnp.zeros((LANES, LANES), F32)
        for kernel_ref, scale in zip(kernels, scales, strict=True):
            total = total + lane_tiles(kernel_ref[at, :] * scale)
        row_scale = weight_ref[at, 0:1] / jnp.sum(total, axis=1, keepdims=True)
        row_ref[at, :] = jnp.broadcast_to(row_scale, (LANES, LANES))
        flat_ref[pl.ds(i, 1), :] = to_row(row_scale)
        return tuple(
            sums + sublane_tiles(kernel_ref[at, :] * row_scale)
            for kernel_ref, sums in zip(kernels, carry, strict=True)
        )

    zero = jnp.zeros((8, SLAB), F32)
    sums = lax.fori_loop(0, 8, step, (zero, zero, zero), unroll=True)
    for i in range(8):
        lane_ref[0:1, i * LANES : (i + 1) * LANES] = flat_ref[i : i + 1, :]
    flat = lane_ref[...]
    finish_messages(flags, sums, flat, flat, partial_ref, cross_ref, inner_ref)


def quarters_kernel(flags, own_ref, y_ref, pair_ref):
    y = flags[Y]
    odd_y = jnp.where(flags[FLIPPED] > 0, 1 - y, y)
    for ref, odd_at, even_at in ((own_ref, odd_y, y), (y_ref, 1 - odd_y, 1 - y)):
        for at, first in ((odd_at * QUARTER, 0), (HALF + even_at * QUARTER, QUARTER)):
            pair_ref[pl.ds(pl.multiple_of(at, QUARTER), QUARTER), :] = ref[first : first + QUARTER, :]


def own_control(flags, columns_ref):
    return columns_ref[pl.ds(pl.multiple_of(flags[NARROW] * QUARTER, QUARTER), QUARTER), :]


def own_transposed_kernel(flags, columns_ref, rows_ref, pair_ref, kernel_ref):
    values = jnp.exp(nt_dot(own_control(flags, columns_ref), rows_ref[...]) * SCALE)
    kernel_ref[0:LANES, :] = values[:LANES] * pair_ref[0:1, :]
    kernel_ref[LANES:QUARTER, :] = values[LANES:] * pair_ref[1:2, :]


def push_kernel(lane_ref, kernel_ref, rows_ref, pushed_ref):
    pushed_ref[...] = jnp.dot(
        (lane_ref[...] * kernel_ref[...]).astype(BF16),
        rows_ref[...],
        preferred_element_type=F32,
    )


def transposed_kernel(
    flags, columns_ref, near_ref, far_ref, mine_in, theirs_in, odd_rows_ref, even_rows_ref,
    kernel_ref,
):
    own = own_control(flags, columns_ref)
    odd_rows_ref[0:HALF, :] = near_ref[0:HALF, :]
    odd_rows_ref[HALF:SLAB, :] = far_ref[0:HALF, :]
    even_rows_ref[0:HALF, :] = near_ref[HALF:SLAB, :]
    even_rows_ref[HALF:SLAB, :] = far_ref[HALF:SLAB, :]
    n = flags[NARROW]
    close, _ = received(flags, mine_in, theirs_in)
    lane = lax.broadcasted_iota(jnp.int32, (16, LANES), 1)
    wanted = (lane < 64) & (lane // 8 == 2 * n + lax.broadcasted_iota(jnp.int32, (16, LANES), 0))
    spread = (
        lax.broadcasted_iota(jnp.int32, (LANES, SLAB), 0) % 8
        == lax.broadcasted_iota(jnp.int32, (LANES, SLAB), 1) // LANES
    )
    spread = jnp.where(spread, 1.0, 0.0).astype(BF16)
    for i, (rows_ref, first) in enumerate(((odd_rows_ref, 2), (even_rows_ref, NOTE + 2))):
        compact = jnp.where(wanted, close[first : first + 1, :LANES], 0.0).astype(BF16)
        found = turned(flags, jnp.dot(compact, spread, preferred_element_type=F32))
        values = jnp.exp(nt_dot(own, rows_ref[...]) * SCALE)
        lanes = slice(i * SLAB, (i + 1) * SLAB)
        kernel_ref[0:LANES, lanes] = values[:LANES] * found[0:1]
        kernel_ref[LANES:QUARTER, lanes] = values[LANES:] * found[1:2]


def gradient_kernel(
    flags, partial_in, mine_in, theirs_in, own_weight, odd_weight, even_weight, row_ref,
    own_kernel_ref, near_kernel_ref, far_kernel_ref, own_columns_ref, near_columns_ref,
    far_columns_ref, rows_ref, pushed_ref, odd_rows_ref, even_rows_ref, transposed_ref,
    treated_any, control_any, treated_out, control_out, sems,
):
    scales = column_scales(
        flags, partial_in, mine_in, theirs_in, (own_weight, odd_weight, even_weight)
    )
    close, _ = received(flags, mine_in, theirs_in)
    pushed = pushed_ref[...]
    for i, (row, rows) in enumerate(((2, odd_rows_ref), (NOTE + 2, even_rows_ref))):
        scale = turned(flags, close[row : row + 1])
        transport = (scale * transposed_ref[:, i * SLAB : (i + 1) * SLAB]).astype(BF16)
        pushed = pushed + jnp.dot(transport, rows[...], preferred_element_type=F32)
    n = flags[NARROW]

    def own_quarter(row):
        found = row[:, :QUARTER]
        for i in range(1, 4):
            found = jnp.where(n == i, row[:, i * QUARTER : (i + 1) * QUARTER], found)
        return found

    def upright(row):
        return jnp.concatenate([to_column(row[:, :LANES]), to_column(row[:, LANES:])], axis=0)

    own_scale = upright(own_quarter(scales[0]))
    own_mass = upright(own_quarter(own_weight[...]))
    at = pl.ds(pl.multiple_of(n * QUARTER, QUARTER), QUARTER)
    control_out[...] = own_mass * own_columns_ref[at, :].astype(F32) - own_scale * pushed
    control_copy = pltpu.make_async_copy(control_out, control_any, sems.at[1])
    control_copy.start()
    mine = pl.ds(pl.multiple_of(flags[Y] * QUARTER, QUARTER), QUARTER)
    row_scale = row_ref[mine, 0:1]
    mass = jnp.zeros((QUARTER, LANES), F32)
    pulled = jnp.zeros((QUARTER, WIDTH), F32)
    for kernel_ref, scale, columns_ref in zip(
        (own_kernel_ref, near_kernel_ref, far_kernel_ref),
        scales,
        (own_columns_ref, near_columns_ref, far_columns_ref),
        strict=True,
    ):
        transport = row_scale * kernel_ref[mine, :] * scale
        mass = mass + lane_tiles(transport)
        pulled = pulled + jnp.dot(
            transport.astype(BF16), columns_ref[...], preferred_element_type=F32
        )
    mass = jnp.sum(mass, axis=1, keepdims=True)
    treated_out[...] = mass * rows_ref[mine, :].astype(F32) - pulled
    treated_copy = pltpu.make_async_copy(treated_out, treated_any, sems.at[0])
    treated_copy.start()

    treated_copy.wait()
    control_copy.wait()


VMEM = pl.BlockSpec(memory_space=pltpu.VMEM)
HBM = pl.BlockSpec(memory_space=pltpu.HBM)
SMEM = pl.BlockSpec(memory_space=pltpu.SMEM)


def call(body, specs, outs, operands, scratch=(), limit=16, out_specs=None):
    return pl.pallas_call(
        body,
        out_shape=tuple(jax.ShapeDtypeStruct(shape, dtype) for shape, dtype in outs),
        in_specs=specs,
        out_specs=out_specs or tuple(VMEM for _ in outs),
        scratch_shapes=list(scratch),
        compiler_params=pltpu.CompilerParams(vmem_limit_bytes=limit << 20),
    )(*operands)


MESSAGES = [((NOTE, SLAB), F32), ((NOTE, SLAB), F32)]


def trade(messages):
    cross = exchange(messages[0], (1, 2), True)
    inner = exchange(messages[1], (1, 2), False)
    (mine,) = call(stack_kernel, [VMEM] * 2, [((2 * NOTE, SLAB), F32)], [cross, inner])
    return mine, narrow_swap(mine, SWAP_CORE)


def step(treated, control, treated_weight, control_weight, band):
    wide_index = lax.axis_index("wide")
    n = lax.axis_index("narrow")
    wide_count = lax.axis_size("wide")
    odd = wide_index % 2
    toward_odd = wide_index + 2 * odd - 1
    toward_even = wide_index + 1 - 2 * odd
    values = (
        n,
        n % 2,
        n // 2,
        odd,
        jnp.logical_xor(wide_index % 4 >= 2, odd == 1).astype(jnp.int32),
        ((toward_odd >= 0) & (toward_odd < wide_count)).astype(jnp.int32),
        (jnp.minimum(wide_index, toward_odd) == wide_count // 2 - 1).astype(jnp.int32),
        wide_index,
        jnp.clip(toward_odd, 0, wide_count - 1),
        toward_even,
    )
    place = lax.iota(jnp.int32, 16)
    flags = jnp.zeros((16,), jnp.int32)
    for i, value in enumerate(values):
        flags = jnp.where(place == i, value, flags)
    treated, control, own_weight, own_band, column_weight = (
        pltpu.with_memory_space_constraint(x, pltpu.HBM)
        for x in (
            treated, control, treated_weight.reshape(2, LANES), band,
            control_weight.reshape(-1, LANES),
        )
    )
    letter, other, message, *weights = call(
        pack_kernel,
        [SMEM] + [HBM] * 5,
        [((HALF, WIDTH), BF16), ((HALF, WIDTH), BF16), ((MESSAGE, WIDTH), BF16)]
        + [((1, SLAB), F32)] * 3,
        [flags, treated, control, own_weight, own_band, column_weight],
        [
            pltpu.VMEM((QUARTER, WIDTH), BF16),
            pltpu.VMEM((2, LANES), F32),
            pltpu.VMEM((2, 24), jnp.int32),
            pltpu.VMEM((INFO, WIDTH), F32),
            pltpu.VMEM((3, 8, LANES), F32),
            pltpu.SemaphoreType.DMA((8,)),
        ],
    )
    odd_letter = exchange(letter, (1, 1), True)
    even_letter = exchange(letter, (1, 1), False)
    (own_columns,) = call(
        columns_kernel,
        [SMEM] + [VMEM] * 2,
        [((SLAB, WIDTH), BF16)],
        [flags, letter, other],
    )

    odd_message = exchange(message, (1, 1), True)
    even_message = exchange(message, (1, 1), False)
    message_y = narrow_swap(message, SWAP_Y)
    (joined,) = call(
        join_kernel, [SMEM] + [VMEM] * 2, [((JOINED, WIDTH), BF16)], [flags, message, message_y]
    )
    joined_far = narrow_swap(joined, SWAP_CORE)

    rows, own_kernel, sums, mask, weight, pairs, compact = call(
        prepare_kernel,
        [SMEM] + [VMEM] * 3,
        [
            ((SLAB, WIDTH), BF16),
            ((SLAB, SLAB), F32),
            ((SLAB, LANES), F32),
            ((8, 3 * SLAB), F32),
            ((SLAB, LANES), F32),
            ((8, SLAB), F32),
            ((8, SLAB), F32),
        ],
        [flags, joined, joined_far, own_columns],
        [pltpu.VMEM((LANES, LANES), F32)],
    )
    (own_transposed,) = call(
        own_transposed_kernel,
        [SMEM] + [VMEM] * 3,
        [((QUARTER, SLAB), F32)],
        [flags, own_columns, rows, pairs],
    )
    odd_letter, even_letter, _ = lax.optimization_barrier((odd_letter, even_letter, sums))
    (near_columns,) = call(
        open_kernel,
        [VMEM] * 2,
        [((SLAB, WIDTH), BF16)],
        [odd_letter, even_letter],
    )
    far_columns = narrow_swap(near_columns, SWAP_CORE)
    (quarters,) = call(
        collect_kernel, [VMEM] * 2, [((HALF, WIDTH), BF16)], [odd_message, even_message]
    )
    quarters_y = narrow_swap(quarters, SWAP_Y)
    near_values, sums = call(
        near_kernel,
        [VMEM] * 4,
        [((SLAB, SLAB), F32), ((SLAB, LANES), F32)],
        [rows, near_columns, mask, sums],
    )
    far_values, partial, *messages = call(
        far_kernel,
        [SMEM] + [VMEM] * 8,
        [((SLAB, SLAB), F32), ((8, SLAB), F32), *MESSAGES],
        [flags, rows, far_columns, mask, own_kernel, near_values, sums, weight, compact],
    )
    first = trade(messages)

    row_scale, lane_scale, partial, *messages = call(
        sweep_kernel,
        [SMEM] + [VMEM] * 10,
        [((SLAB, LANES), F32), ((1, SLAB), F32), ((8, SLAB), F32), *MESSAGES],
        [flags, partial, *first, *weights, own_kernel, near_values, far_values, weight],
        [pltpu.VMEM((8, LANES), F32)],
    )
    (near_rows,) = call(
        quarters_kernel,
        [SMEM] + [VMEM] * 2,
        [((SLAB, WIDTH), BF16)],
        [flags, quarters, quarters_y],
    )
    second = trade(messages)
    far_rows = narrow_swap(near_rows, SWAP_CORE)

    (pushed,) = call(
        push_kernel,
        [VMEM] * 3,
        [((QUARTER, WIDTH), F32)],
        [lane_scale, own_transposed, rows],
    )
    odd_rows, even_rows, transposed = call(
        transposed_kernel,
        [SMEM] + [VMEM] * 5,
        [((SLAB, WIDTH), BF16), ((SLAB, WIDTH), BF16), ((QUARTER, 2 * SLAB), F32)],
        [flags, own_columns, near_rows, far_rows, *first],
    )

    return call(
        gradient_kernel,
        [SMEM] + [VMEM] * 18,
        [((QUARTER, WIDTH), F32)] * 2,
        [
            flags, partial, *second, *weights, row_scale, own_kernel, near_values, far_values,
            own_columns, near_columns, far_columns, rows, pushed, odd_rows, even_rows, transposed,
        ],
        [
            pltpu.VMEM((QUARTER, WIDTH), F32),
            pltpu.VMEM((QUARTER, WIDTH), F32),
            pltpu.SemaphoreType.DMA((2,)),
        ],
        out_specs=(HBM, HBM),
    )


def solution(mesh):
    return jax.shard_map(
        step,
        mesh=mesh,
        in_specs=(
            P(("wide", "narrow"), None),
            P("wide", None),
            P(("wide", "narrow")),
            P(),
            P(("wide", "narrow"), None),
        ),
        out_specs=(P(("wide", "narrow"), None), P(("wide", "narrow"), None)),
        check_vma=False,
    )
```
